128 devices in a mesh: lon: 16 (over x, z), lat: 8 (over y, core).
Axes of the slice: x: 4, y: 4, z: 4, core: 2. Of those that a mesh axis runs over, the one named last changes fastest.
Arguments:
- state: float32 [8, 64, 32, 2048], P(None, None, 'lat', 'lon'), may hold values from -6 to 6
- winds: float32 [2, 64, 32, 2048], P(None, None, 'lat', 'lon'), may hold values from -0.3 to 0.3
- diffusivity: float32 [32, 2048], P('lat', 'lon'), may hold values from 0.05 to 0.2
- sounding_cell: int32 [2, 16384], P(None, ('lon', 'lat')), may hold values from 0 to 511
- sounding_owner: int32 [2, 16384, 1], P(None, ('lon', 'lat')), may hold values from 0 to 127; in each aligned block of 128 rows (0 to 127, 128 to 255, ..., all dimensions but the last counted through in order) at most 3 rows name the same one
- step_counts: int32 [2], replicated, may hold values from 1 to 4
- channel_list: int32 [512], replicated, may hold values from 0 to 615
- absorb_table: float32 [512, 616], replicated, may hold values from -0.25 to 0.25
- emit_table: float32 [512, 616], replicated, may hold values from -0.25 to 0.25
- obs_weight: float32 [616], replicated, may hold values from 0.5 to 4
- observed: float32 [2, 128, 128, 3, 512], P(None, ('lon', 'lat')), may hold values from -6 to 6
Outputs:
- gradient: float32 [8, 64, 32, 2048], P(None, None, 'lat', 'lon')
The draws below stay inside these ranges and needn't reach their ends.
Inputs may be any that keep to these rules, and one draw needn't show every extreme that they name: `sounding_owner`: in one slot, at most 3 soundings of one tile's list name the same owner. `sounding_cell`: columns are numbered row by row within the tile. `channel_list`: entries may repeat.
All inputs are finite; a program needn't handle non-finite values.
Results may differ from the reference program's by a relative error of at most 0.00022.
Values sent between devices are 32-bit elements; how exact they have to be, the bound alone decides.
No kernel may reach another device: no remote copies, remote signals or barrier semaphores. Data moves between devices by JAX's collectives and lax.ppermute only.
A program may use at most 128 MiB of HBM per device.

```python
import math
from functools import partial
import jax
import jax.numpy as jnp
import numpy as np
from jax import lax

VARS = 8
LEV = 64
CHAN = 616
USED = 512
CLAT = 4
CLON = 128
SND = 128
MAXSTEP = 4
SLOTS = 2
PROF = 512
NLAT = 32
NLON = 2048
SOUNDINGS = 16384
CAP = 3
N_LAT = 8
DEVICES = 128


def plant(drawn, rng, smallest, top_value):
    longest = drawn.shape.index(max(drawn.shape))
    spots = []
    for shift in (0, 1):
        where = [jax.random.randint(jax.random.fold_in(rng, axis), (), 0, length) for axis, length in enumerate(drawn.shape)]
        where[longest] = (where[longest] + shift) % drawn.shape[longest]
        spots.append(tuple(where))
    return drawn.at[spots[0]].set(smallest).at[spots[1]].set(top_value)


def level_of(rng, dims, cuts, least, largest):
    def one(position, blocks):
        steps = jax.random.uniform(jax.random.fold_in(jax.random.fold_in(rng, 6), position), (blocks,), jnp.float32, least / len(cuts), largest / len(cuts))
        return jnp.repeat(jnp.exp(steps), dims[position] // blocks).reshape((-1,) + (1,) * (len(dims) - position - 1))

    level = one(*cuts[0])
    for cut in cuts[1:]:
        level = level * one(*cut)
    return level


def assign_block(rng, own, number, rows, count, top, most, slope):
    order = jax.random.permutation(rng, count)
    packed, ordinary = load_shares(count, rows * top, most, slope, True), load_shares(count, rows * top, most, slope, False)
    places = jnp.arange(count)

    def named(sizes, offset_by):
        used = int((sizes > 0).sum())
        fixed = max(1, used // 4)
        shifted = fixed + (places - fixed + offset_by * (used - fixed)) % max(1, count - fixed)
        return jnp.zeros((count,), jnp.int32).at[order[jnp.where(places < fixed, places, shifted)]].set(jnp.asarray(sizes, jnp.int32))

    sizes = jnp.where(number % 4 == 0, named(packed, number // 4), named(ordinary, number - number // 4 - 1))
    mixed = jax.random.permutation(jax.random.fold_in(own, 3), count)
    source_of, taker = mixed[0:count // 2 * 2:2], mixed[1:count // 2 * 2:2]
    margin = jnp.minimum(sizes[source_of] - 1, most - sizes[taker]) // 2
    margin = jnp.where((source_of == order[0]) | (taker == order[0]) | (sizes[taker] == 0), 0, jnp.maximum(margin, 0))
    shifted = jax.random.randint(jax.random.fold_in(own, 4), (count // 2,), 0, 1 << 20) % (margin + 1)
    sizes = sizes.at[source_of].add(-shifted).at[taker].add(shifted)
    labels = jnp.searchsorted(jnp.cumsum(sizes), jnp.arange(rows * top), side="right").astype(jnp.int32)
    grid = labels.reshape(top, rows).T
    grid = grid[jax.random.permutation(jax.random.fold_in(own, 1), rows)]
    offset_by = jax.random.randint(jax.random.fold_in(own, 2), (rows, 1), 0, top)
    return jnp.take_along_axis(grid, (jnp.arange(top)[None, :] + offset_by) % top, axis=1)


def load_shares(count, total, most, skew, full):
    loads = [(1 << 20) // math.isqrt(grade ** skew) + 1 for grade in range(1, count + 1)]
    largest = most if full else min(most, max(-(-total // count), total * loads[0] // sum(loads)))
    least = 1 if total - largest >= count - 1 else 0
    counts, surplus = [largest] + [least] * (count - 1), total - largest - least * (count - 1)
    while surplus > 0:
        movable = [i for i in range(1, count) if counts[i] < largest] or [i for i in range(1, count) if counts[i] < most]
        mass, budget = sum([loads[i] for i in movable]), surplus
        for i in movable:
            extra = min(most - counts[i], max(1, budget * loads[i] // mass), surplus)
            counts[i] = counts[i] + extra
            surplus = surplus - extra
    return np.array(counts)


def centred(own_key, extent, deviation, reach, split=(), kind=jnp.bfloat16):
    values = jax.random.normal(own_key, extent, jnp.float32) * deviation
    if len(split) > 0:
        values = level_of(own_key, extent, split, -0.22, 0.18) * values
    return jnp.clip(values, min=-reach, max=reach).astype(kind)


def setup_inputs(seed: int = 0) -> dict:
    key_list = jax.random.split(jax.random.key(seed), 12)
    state = centred(key_list[0], (VARS, LEV, NLAT, NLON), 1.0, 6.0, ((2, 8), (3, 16)), jnp.float32)
    winds = jnp.clip(jax.random.uniform(key_list[1], (2, LEV, NLAT, NLON), jnp.float32, -0.3, 0.3) * level_of(key_list[1], (2, LEV, NLAT, NLON), ((2, 8), (3, 16)), -0.4, 0.0), -0.3, 0.3)
    diffusivity = jnp.clip(0.05 + 0.15 * jax.random.uniform(key_list[2], (NLAT, NLON), jnp.float32) ** level_of(key_list[2], (NLAT, NLON), ((0, 8), (1, 16)), -0.2, 0.2), 0.05, 0.2)
    sounding_cell = plant(jax.random.randint(key_list[3], (SLOTS, SOUNDINGS), 0, CLAT * CLON), jax.random.fold_in(key_list[3], 1), 0, (CLAT * CLON) - 1).astype(jnp.int32)
    sounding_owner_keys = jax.random.split(jax.random.fold_in(key_list[4], 1), SLOTS * SOUNDINGS // SND)
    sounding_owner_turns = jax.random.permutation(jax.random.fold_in(key_list[4], 3), SLOTS * SOUNDINGS // SND)
    sounding_owner = jax.vmap(lambda own, number: assign_block(jax.random.fold_in(key_list[4], 2), own, number, SND, DEVICES, 1, CAP, 2))(sounding_owner_keys, sounding_owner_turns).reshape((SLOTS, SOUNDINGS, 1))
    step_counts = jax.random.randint(key_list[5], (SLOTS,), 1, MAXSTEP + 1).astype(jnp.int32)
    channel_list = plant(jax.random.randint(key_list[6], (USED,), 0, CHAN), jax.random.fold_in(key_list[6], 1), 0, CHAN - 1).astype(jnp.int32)
    absorb_table = centred(key_list[7], (PROF, CHAN), PROF ** -0.5, 0.25, (), jnp.float32)
    emit_table = centred(key_list[8], (PROF, CHAN), PROF ** -0.5, 0.25, (), jnp.float32)
    obs_weight = jnp.clip(jnp.exp(jax.random.uniform(key_list[9], (CHAN,), jnp.float32, math.log(0.5), math.log(4.0))), 0.5, 4.0)
    observed = centred(key_list[10], (SLOTS, DEVICES, DEVICES, CAP, USED), 1.0, 6.0, ((1, 128),), jnp.float32)
    return {"state": state, "winds": winds, "diffusivity": diffusivity, "sounding_cell": sounding_cell, "sounding_owner": sounding_owner, "step_counts": step_counts, "channel_list": channel_list, "absorb_table": absorb_table, "emit_table": emit_table, "obs_weight": obs_weight, "observed": observed}


HIGHEST_MODE = lax.Precision.HIGHEST

def pad_field(values):
    wrapped = jnp.concatenate([values[..., -1:], values, values[..., :1]], axis=-1)
    widths = [(0, 0)] * (values.ndim - 2) + [(1, 1), (0, 0)]
    return jnp.pad(wrapped, widths)

def make_coef(winds, diffusivity):
    return jnp.stack([winds[0] * 0.5 + diffusivity, winds[0] * 0.5 - diffusivity, winds[1] * 0.5 + diffusivity, winds[1] * 0.5 - diffusivity])

def advance(padded, coef_pad):
    centre = padded[:, :, 1:-1, 1:-1]
    lon_band = padded[:, :, 1:-1, :]
    flux_lon = coef_pad[0][:, 1:-1, :-1] * lon_band[..., :-1] + coef_pad[1][:, 1:-1, :-1] * lon_band[..., 1:]
    lat_band = padded[:, :, :, 1:-1]
    flux_lat = coef_pad[2][:, :-1, 1:-1] * lat_band[:, :, :-1, :] + coef_pad[3][:, :-1, 1:-1] * lat_band[:, :, 1:, :]
    return centre - (flux_lon[..., 1:] - flux_lon[..., :-1]) - (flux_lat[:, :, 1:, :] - flux_lat[:, :, :-1, :])

def retreat(padded, coef_pad):
    centre = padded[:, :, 1:-1, 1:-1]
    lon_band = padded[:, :, 1:-1, :]
    step_lon = lon_band[..., 1:] - lon_band[..., :-1]
    result = centre + coef_pad[0][:, 1:-1, 1:-1] * step_lon[..., 1:] + coef_pad[1][:, 1:-1, :-2] * step_lon[..., :-1]
    lat_band = padded[:, :, :, 1:-1]
    step_lat = lat_band[:, :, 1:, :] - lat_band[:, :, :-1, :]
    result = result + coef_pad[2][:, 1:-1, 1:-1] * step_lat[:, :, 1:, :] + coef_pad[3][:, :-2, 1:-1] * step_lat[:, :, :-1, :]
    return result

def select_channels(channel_list, absorb_table, emit_table, obs_weight):
    picker = (jnp.arange(obs_weight.shape[0], dtype=jnp.int32)[:, None] == channel_list[None, :]).astype(jnp.float32)
    absorb = jnp.dot(absorb_table, picker, precision=HIGHEST_MODE, preferred_element_type=jnp.float32)
    emission = jnp.dot(emit_table, picker, precision=HIGHEST_MODE, preferred_element_type=jnp.float32)
    weight = jnp.dot(obs_weight[None, :], picker, precision=HIGHEST_MODE, preferred_element_type=jnp.float32)[0]
    return (absorb, emission, weight)

def radiance(profiles, absorb, emission):
    optical = jnp.dot(profiles, absorb, precision=HIGHEST_MODE, preferred_element_type=jnp.float32)
    bright = jnp.dot(profiles, emission, precision=HIGHEST_MODE, preferred_element_type=jnp.float32)
    return jnp.exp(-jax.nn.softplus(optical)) * bright

def slot_gradient(state_now, slot_index, sounding_cell, sounding_owner, observed, absorb, emission, weight):
    sounding_cells = sounding_cell[slot_index].reshape(DEVICES, SND)
    owners = sounding_owner[slot_index, :, 0].reshape(DEVICES, SND)
    owner_hit = (owners[:, :, None] == jnp.arange(DEVICES, dtype=jnp.int32)[None, None, :]).astype(jnp.int32)
    owner_rank = lax.optimization_barrier(jnp.sum(jnp.cumsum(owner_hit, axis=1) * owner_hit, axis=2)) - 1
    home_index = jnp.broadcast_to(jnp.arange(DEVICES, dtype=jnp.int32)[:, None], (DEVICES, SND))
    wanted = observed[slot_index, owners, home_index, owner_rank].reshape(DEVICES * SND, USED)
    lat_rows = (home_index % N_LAT * CLAT + sounding_cells // CLON).reshape(-1).astype(jnp.int32)
    lon_cols = (home_index // N_LAT * CLON + sounding_cells % CLON).reshape(-1).astype(jnp.int32)
    profiles = state_now[:, :, lat_rows, lon_cols].reshape(PROF, DEVICES * SND).T
    evolved, pullback = jax.vjp(partial(radiance, absorb=absorb, emission=emission), profiles)
    departure = weight[None, :] * (evolved - wanted)
    adjoint_cols = pullback(departure)[0]
    placed = adjoint_cols.T.reshape(VARS, LEV, DEVICES * SND)
    return jnp.zeros_like(state_now).at[:, :, lat_rows, lon_cols].add(placed)

def reference(state, winds, diffusivity, sounding_cell, sounding_owner, step_counts, channel_list, absorb_table, emit_table, obs_weight, observed):
    coef_pad = pad_field(make_coef(winds, diffusivity))
    absorb, emission, weight = select_channels(channel_list, absorb_table, emit_table, obs_weight)
    state_now = state
    slot_fields = []
    for slot_index in range(SLOTS):
        for step_index in range(MAXSTEP):
            state_now = jnp.where(step_index < step_counts[slot_index], advance(pad_field(state_now), coef_pad), state_now)
        slot_fields.append(state_now)
    gradients = [slot_gradient(slot_fields[slot_index], slot_index, sounding_cell, sounding_owner, observed, absorb, emission, weight) for slot_index in range(SLOTS)]
    adjoint = jnp.zeros_like(state)
    for slot_index in reversed(range(SLOTS)):
        adjoint = adjoint + gradients[slot_index]
        for step_index in range(MAXSTEP):
            adjoint = jnp.where(step_index < step_counts[slot_index], retreat(pad_field(adjoint), coef_pad), adjoint)
    return adjoint
```

```python
from functools import partial

import jax
import jax.numpy as jnp
from jax import lax
from jax.experimental import pallas as pl
from jax.experimental.pallas import tpu as pltpu
from jax.sharding import PartitionSpec as P

F32 = jnp.float32
BF16 = jnp.bfloat16
I32 = jnp.int32
VARS = 8
LEV = 64
TILES = 8
MAXSTEP = 4
SND = 128
VMEM_LIMIT = 48 * 1024 * 1024


def struct(*shape, dtype=F32):
    return jax.ShapeDtypeStruct(shape, dtype)


def tiled(*shape):
    zeros = (0,) * (len(shape) - 2)
    return pl.BlockSpec((*shape[:-2], 8, shape[-1]), lambda t: (*zeros, t, 0))


def native(variables):
    return pl.BlockSpec((variables, 32, 128), lambda t: (0, t, 0))


def whole(shape):
    return pl.BlockSpec(shape, lambda *_: (0,) * len(shape))


SMEM_SPEC = pl.BlockSpec(memory_space=pltpu.SMEM)


def lanes():
    return lax.broadcasted_iota(I32, (8, 128), 1)


def roll(x, shift):
    shift = shift % 128
    return x if shift == 0 else pltpu.roll(x, shift, 1)


def own_strip(load, count):
    lane = lanes()
    strip = jnp.zeros((8, 128), F32)
    for g in range(count):
        x = load(g)
        base = 32 * g
        strip = jnp.where((lane >= base + 8) & (lane < base + 16), roll(x, base + 8), strip)
        strip = jnp.where((lane >= base + 16) & (lane < base + 24), roll(x, base + 24), strip)
    return strip


def pack_strips(strips, even, write):
    lane = lanes() % 32
    east = jnp.zeros((8, 128), F32)
    west = jnp.zeros((8, 128), F32)
    for r in range(4):
        here = (lane >= 8 * r) & (lane < 8 * r + 8)
        east = jnp.where(here, roll(strips[r], 8 * r - 16), east)
        west = jnp.where(here, roll(strips[r], 8 * r - 8), west)
    write(jnp.where(even, east, west), jnp.where(even, west, east))


def pack_kernel(meta, state, winds, diff, main, strip, first, second):
    even = meta[1] == 1
    for r in range(4):
        for v in range(VARS):
            main[r, v] = state[v, pl.ds(r, 8, stride=4), :]
        for v in range(2):
            main[r, VARS + v] = winds[v, pl.ds(r, 8, stride=4), :]
        main[r, VARS + 2] = jnp.broadcast_to(diff[r : r + 1, :], (8, 128))
    for b in range(3):
        strips = []
        for r in range(4):
            s = own_strip(lambda g: main[r, 4 * b + g], 4 if b < 2 else 3)
            strip[r, b] = s
            strips.append(s)

        def write(p, q):
            first[b] = p
            second[b] = q

        pack_strips(strips, even, write)


def pack(meta, state, winds, diff):
    return pl.pallas_call(
        pack_kernel,
        grid=(TILES,),
        in_specs=[SMEM_SPEC, native(8), native(2), whole((4, 128))],
        out_specs=[tiled(4, 11, LEV, 128), tiled(4, 3, LEV, 128), tiled(3, LEV, 128), tiled(3, LEV, 128)],
        out_shape=[struct(4, 11, LEV, 128), struct(4, 3, LEV, 128), struct(3, LEV, 128), struct(3, LEV, 128)],
        name="pack",
    )(meta, state, winds, diff)


def complete_kernel(meta, strip, first, second, *outs):
    even = meta[1] == 1
    lane = lanes() % 32
    blocks = strip.shape[1]
    split = blocks // len(outs)
    for b in range(blocks):
        east = jnp.where(even, first[b], second[b])
        west = jnp.where(even, second[b], first[b])
        for r in range(4):
            full = jnp.where(lane < 8, roll(west, -8 * r), strip[r, b])
            outs[b // split][r, b % split] = jnp.where(lane >= 24, roll(east, 24 - 8 * r), full)


def complete(meta, strip, first, second, parts):
    blocks = strip.shape[1]
    split = blocks // parts
    return pl.pallas_call(
        complete_kernel,
        grid=(TILES,),
        in_specs=[SMEM_SPEC, tiled(4, blocks, LEV, 128), tiled(blocks, LEV, 128), tiled(blocks, LEV, 128)],
        out_specs=[tiled(4, split, LEV, 128)] * parts,
        out_shape=[struct(4, split, LEV, 128)] * parts,
        name="complete",
    )(meta, strip, first, second)


def march(field, steps, coef, south, adjoint, edge, record):
    lane = lanes()
    for k in range(steps):
        reach = steps - 1 - k
        new = {}
        before = None
        for i in range(3 - reach, 8 + reach):
            f = field[i]
            a, b, c, d = coef(i)
            if adjoint:
                rise = field[i + 1] - f
                here, passed = c * rise, d * rise
            else:
                here = passed = c * f + d * field[i + 1]
            if before is not None:
                east = roll(f, -1)
                if edge is not None:
                    rim = edge(k, i)
                    east = jnp.where(lane == 127, rim, east)
                if adjoint:
                    slope = east - f
                    flux = b * slope
                else:
                    flux = a * f + b * east
                shifted = roll(flux, 1)
                if edge is not None:
                    shifted = jnp.where(lane == 0, rim, shifted)
                else:
                    record(k, i, jnp.where(lane % 32 == 25, roll(flux, 18), f))
                if adjoint:
                    value = f + a * slope + shifted + here + before
                else:
                    value = f - (flux - shifted) - (here - before)
                if i >= 8:
                    value = value * south
                new[i] = value
            before = passed
        field = new
    return field


def advect_kernel(*refs, adjoint, apart, first, result, addend):
    refs = list(refs)
    meta = refs.pop(0)
    own, r0, r1 = refs[:3]
    refs = refs[3:]
    if apart:
        sown, s0, s1 = refs[:3]
        refs = refs[3:]
        base = 0
    else:
        sown, s0, s1 = own, r0, r1
        base = VARS
    if not first:
        coef_in = refs.pop(0)
    if addend:
        add_main, add_strip = refs[:2]
        refs = refs[2:]
    out = refs.pop(0)
    coef_out = refs.pop(0) if first else None
    rims = refs.pop(0)
    even = meta[2] == 1
    south = meta[3].astype(F32)

    def fetch(tile, pair, other, i, v):
        if i < 4:
            return jnp.where(even, other[i, v], pair[i, v])
        if i < 8:
            return tile[i - 4, v]
        return jnp.where(even, pair[i - 8, v], other[i - 8, v])

    if first:
        lane = lanes()
        for i in range(12):
            w0, w1, dd = (fetch(own, r0, r1, i, VARS + v) for v in range(3))
            coef_out[i, 0] = w0 * 0.5 + dd
            coef_out[i, 1] = w0 * 0.5 - dd
            coef_out[i, 2] = w1 * 0.5 + dd
            coef_out[i, 3] = w1 * 0.5 - dd
            packed = fetch(sown, s0, s1, i, 2)
            spread = []
            for g in range(3):
                one = jnp.where(lane < 32, roll(packed, -32 * g), 0.0)
                one = one + roll(one, 32)
                spread.append(one + roll(one, 64))
            w0, w1, dd = spread
            coef_out[i, 4] = w0 * 0.5 + dd
            coef_out[i, 5] = w0 * 0.5 - dd
            coef_out[i, 6] = w1 * 0.5 + dd
            coef_out[i, 7] = w1 * 0.5 - dd
        coef_in = coef_out

    def coefs(offset):
        return lambda i: tuple(coef_in[i, offset + n] for n in range(4))

    def put(r, v, value):
        if result == "native":
            out[v, pl.ds(r, 8, stride=4), :] = value
        else:
            out[r, v] = value

    def run(steps):
        def block(b, carry):
            strips = {i: fetch(sown, s0, s1, i, base + b) for i in range(4 - steps, 8 + steps)}

            def record(k, i, value):
                rims[k, i] = value

            strips = march(strips, steps, coefs(4), south, adjoint, None, record)
            if result == "both":
                for r in range(4):
                    value = strips[4 + r]
                    out[r, VARS + b] = value + add_strip[r, b] if addend else value
            for g in range(4):
                v = 4 * b + g
                field = {i: fetch(own, r0, r1, i, v) for i in range(4 - steps, 8 + steps)}
                field = march(
                    field, steps, coefs(0), south, adjoint, lambda k, i: roll(rims[k, i], 103 - 32 * g), None
                )
                for r in range(4):
                    put(r, v, field[4 + r] + add_main[r, v] if addend else field[4 + r])
            return carry

        lax.fori_loop(0, 2, block, 0)

    for steps in range(1, MAXSTEP + 1):
        pl.when(meta[0] == steps)(partial(run, steps))


def advect(meta, tile, strips, coef, adjoint, result, addend=None):
    first = coef is None
    args = [meta, *tile]
    specs = [SMEM_SPEC] + [tiled(*t.shape) for t in tile]
    if strips is not None:
        args += strips
        specs += [tiled(*t.shape) for t in strips]
    if not first:
        args.append(coef)
        specs.append(tiled(12, 8, LEV, 128))
    if addend is not None:
        args += addend
        specs += [tiled(*t.shape) for t in addend]
    if result == "native":
        shapes, outs = [struct(8, 256, 128)], [native(8)]
    else:
        count = 10 if result == "both" else 8
        shapes, outs = [struct(4, count, LEV, 128)], [tiled(4, count, LEV, 128)]
    if first:
        shapes.append(struct(12, 8, LEV, 128))
        outs.append(tiled(12, 8, LEV, 128))
    return pl.pallas_call(
        partial(
            advect_kernel,
            adjoint=adjoint,
            apart=strips is not None,
            first=first,
            result=result,
            addend=addend is not None,
        ),
        grid=(TILES,),
        in_specs=specs,
        out_specs=outs,
        out_shape=shapes,
        scratch_shapes=[pltpu.VMEM((MAXSTEP, 12, 8, 128), F32)],
        compiler_params=pltpu.CompilerParams(vmem_limit_bytes=VMEM_LIMIT),
        name="advect_" + result + ("_adjoint" if adjoint else ""),
    )(*args)


def split(x):
    high = x.astype(BF16)
    return high, (x - high.astype(F32)).astype(BF16)


def dot(x, y, dims):
    return lax.dot_general(x, y, ((dims[:1], dims[1:]), ((), ())), preferred_element_type=F32)


def dot3(x, y, dims):
    return dot(x[0], y[0], dims) + (dot(x[0], y[1], dims) + dot(x[1], y[0], dims))


def observe_kernel(
    meta, cells, owners, field0, field1, fetched, ah, al, eh, el, weight, g0, g1, strip, first, second
):
    even = meta[1] == 1
    square = (SND, SND)
    row_id = lax.broadcasted_iota(I32, square, 0)
    lane_id = lax.broadcasted_iota(I32, square, 1)
    absorb = (ah[...], al[...])
    emission = (eh[...], el[...])
    for k, (field, out) in enumerate(((field0, g0), (field1, g1))):
        cell = jnp.sum(
            jnp.where(row_id == lane_id, jnp.broadcast_to(cells[k : k + 1, :], square), 0),
            axis=1,
            keepdims=True,
        )
        owner = owners[k]
        owner_row = jnp.sum(
            jnp.where(row_id == lane_id, jnp.broadcast_to(owner, square), 0), axis=0, keepdims=True
        )
        earlier = (owner == owner_row) & (lane_id < row_id)
        rank = jnp.sum(jnp.where(earlier, 1, 0), axis=1, keepdims=True)
        picks = [(cell == lane_id + 128 * r).astype(F32).astype(BF16) for r in range(4)]
        high = jnp.zeros((SND, 512), F32)
        low = jnp.zeros((SND, 512), F32)
        for r in range(4):
            xh, xl = split(field[r, 0:VARS].reshape(VARS * LEV, 128))
            high = high + dot(picks[r], xh, (1, 1))
            low = low + dot(picks[r], xl, (1, 1))
        column = (high.astype(BF16), low.astype(BF16))
        optical = dot3(column, absorb, (1, 0))
        bright = dot3(column, emission, (1, 0))
        decay = jnp.exp(-jnp.abs(optical))
        inverse = 1.0 / (1.0 + decay)
        rest = decay * inverse
        positive = optical >= 0
        passing = jnp.where(positive, rest, inverse)
        opaque = jnp.where(positive, inverse, rest)
        choices = [((owner == lane_id) & (rank == q)).astype(F32).astype(BF16) for q in range(3)]
        parts = []
        for c in range(4):
            part = jnp.zeros(square, F32)
            for q in range(3):
                oh, ol = split(fetched[pl.ds(12 * k + 4 * q + c, SND, stride=24), :])
                part = part + (dot(choices[q], oh, (1, 0)) + dot(choices[q], ol, (1, 0)))
            parts.append(part)
        wanted = jnp.concatenate(parts, axis=1)
        evolved = passing * bright
        departure = weight[...] * (evolved - wanted)
        to_bright = departure * passing
        to_optical = -(departure * evolved * opaque)
        column = dot3(split(to_optical), absorb, (1, 1)) + dot3(split(to_bright), emission, (1, 1))
        ch, cl = split(column)
        for r in range(4):
            placed = dot(ch, picks[r], (0, 0)) + dot(cl, picks[r], (0, 0))
            out[r] = placed.reshape(VARS, LEV, 128)

    def strips_of(t, carry):
        level = pl.ds(pl.multiple_of(t * 8, 8), 8)
        for b in range(4):
            out = g1 if b < 2 else g0
            strips = []
            for r in range(4):
                s = own_strip(lambda g: out[r, 4 * (b % 2) + g, level, :], 4)
                strip[r, b, level, :] = s
                strips.append(s)

            def write(p, q):
                first[b, level, :] = p
                second[b, level, :] = q

            pack_strips(strips, even, write)
        return carry

    lax.fori_loop(0, TILES, strips_of, 0)


def observe(meta, *args):
    return pl.pallas_call(
        observe_kernel,
        in_specs=[SMEM_SPEC] + [pl.BlockSpec(memory_space=pltpu.VMEM)] * len(args),
        out_shape=[
            struct(4, 8, LEV, 128),
            struct(4, 8, LEV, 128),
            struct(4, 4, LEV, 128),
            struct(4, LEV, 128),
            struct(4, LEV, 128),
        ],
        compiler_params=pltpu.CompilerParams(vmem_limit_bytes=VMEM_LIMIT),
        name="observe",
    )(meta, *args)


def swap(x, axis, parity, wrap):
    devices = lax.axis_size(axis)
    pairs = []
    for i in range(parity, devices, 2):
        if i + 1 < devices or wrap:
            j = (i + 1) % devices
            pairs += [(i, j), (j, i)]
    return lax.ppermute(x, axis, pairs)


def lat_swap(x):
    return swap(x, "lat", 1, False), swap(x, "lat", 0, False)


def lon_swap(first, second):
    return swap(second, "lon", 1, True), swap(first, "lon", 0, True)


def select_channels(channel_list, absorb_table, emit_table, obs_weight):
    hit = jnp.arange(obs_weight.shape[0], dtype=I32)[:, None] == channel_list[None, :]
    picker = hit.astype(BF16)

    def pick(table):
        high = lax.reduce_precision(table, 8, 7)
        low = lax.reduce_precision(table - high, 8, 7)
        take = lambda part: jnp.dot(part.astype(BF16), picker, preferred_element_type=F32).astype(BF16)
        return take(high), take(low)

    weight = jnp.sum(jnp.where(hit, obs_weight[:, None], 0.0), axis=0)[None, :]
    return (*pick(absorb_table), *pick(emit_table), weight)


def per_device(
    state, winds, diffusivity, sounding_cell, sounding_owner, step_counts, channel_list, absorb_table, emit_table,
    obs_weight, observed,
):
    lat = lax.axis_index("lat")
    lon = lax.axis_index("lon")
    flags = jnp.stack([1 - lon % 2, 1 - lat % 2, (lat < lax.axis_size("lat") - 1).astype(I32)]).astype(I32)
    meta = [jnp.concatenate([step_counts[k : k + 1], flags]) for k in range(2)]

    main, strip, first, second = pack(
        meta[0], state.reshape(8, 256, 128), winds.reshape(2, 256, 128), diffusivity
    )
    lon1, lon0 = lon_swap(first, second)
    lat1, lat0 = lat_swap(main)
    devices = observed.shape[2]
    sent = jnp.transpose(observed[:, 0], (1, 0, 2, 3)).reshape(devices, 24, 128)
    fetched = lax.all_to_all(sent, ("lon", "lat"), split_axis=0, concat_axis=0, tiled=True)
    channels = select_channels(channel_list, absorb_table, emit_table, obs_weight)
    (strips,) = complete(meta[0], strip, lon0, lon1, 1)
    slat1, slat0 = lat_swap(strips)

    both0, coef = advect(meta[0], (main, lat0, lat1), (strips, slat0, slat1), None, False, "both")
    lat1, lat0 = lat_swap(both0)
    (field1,) = advect(meta[1], (both0, lat0, lat1), None, coef, False, "main")

    g0, g1, strip, first, second = observe(
        meta[0], sounding_cell, sounding_owner, both0, field1, fetched.reshape(devices * 24, 128), *channels
    )
    lon1, lon0 = lon_swap(first, second)
    lat1, lat0 = lat_swap(g1)
    strips1, strips0 = complete(meta[0], strip, lon0, lon1, 2)
    slat1, slat0 = lat_swap(strips1)
    (both,) = advect(
        meta[1], (g1, lat0, lat1), (strips1, slat0, slat1), coef, True, "both", (g0, strips0)
    )
    lat1, lat0 = lat_swap(both)
    (result,) = advect(meta[0], (both, lat0, lat1), None, coef, True, "native")
    return result.reshape(state.shape)


def solution(mesh):
    return jax.shard_map(
        per_device,
        mesh=mesh,
        in_specs=(
            P(None, None, "lat", "lon"),
            P(None, None, "lat", "lon"),
            P("lat", "lon"),
            P(None, ("lon", "lat")),
            P(None, ("lon", "lat"), None),
            P(),
            P(),
            P(),
            P(),
            P(),
            P(None, ("lon", "lat"), None, None, None),
        ),
        out_specs=P(None, None, "lat", "lon"),
        check_vma=False,
    )
```

```python
from functools import partial

import jax
import jax.numpy as jnp
from jax import lax
from jax.experimental import pallas as pl
from jax.experimental.pallas import tpu as pltpu
from jax.sharding import PartitionSpec as P

F32 = jnp.float32
BF16 = jnp.bfloat16
I32 = jnp.int32
VARS = 8
LEV = 64
TILES = 8
MAXSTEP = 4
SND = 128


def struct(*shape, dtype=F32):
    return jax.ShapeDtypeStruct(shape, dtype)


def tiled(grid, *shape):
    zeros = (0,) * (len(shape) - 2)
    return pl.BlockSpec((*shape[:-2], shape[-2] // grid, shape[-1]), lambda t: (*zeros, t, 0))


def whole(shape):
    return pl.BlockSpec(shape, lambda *_: (0,) * len(shape))


SMEM_SPEC = pl.BlockSpec(memory_space=pltpu.SMEM)


def params(mebibytes):
    return pltpu.CompilerParams(vmem_limit_bytes=mebibytes * 1024 * 1024)


def lanes():
    return lax.broadcasted_iota(I32, (8, 128), 1)


def roll(x, shift):
    shift = shift % 128
    return x if shift == 0 else pltpu.roll(x, shift, 1)


def level_tiles(count, body):
    def step(t, carry):
        body(t, pl.ds(pl.multiple_of(t * 8, 8), 8))
        return carry

    lax.fori_loop(0, count, step, 0)


def lon_even():
    return lax.axis_index("lon") % 2 == 0


def lat_even():
    return lax.axis_index("lat") % 2 == 0


def own_strip(load, count):
    lane = lanes()
    strip = jnp.zeros((8, 128), F32)
    for g in range(count):
        x = load(g)
        base = 32 * g
        strip = jnp.where((lane >= base + 8) & (lane < base + 16), roll(x, base + 8), strip)
        strip = jnp.where((lane >= base + 16) & (lane < base + 24), roll(x, base + 24), strip)
    return strip


def pack_strips(strips, even):
    lane = lanes() % 32
    east = jnp.zeros((8, 128), F32)
    west = jnp.zeros((8, 128), F32)
    for r in range(4):
        here = (lane >= 8 * r) & (lane < 8 * r + 8)
        east = jnp.where(here, roll(strips[r], 8 * r - 16), east)
        west = jnp.where(here, roll(strips[r], 8 * r - 8), west)
    return jnp.where(even, east, west), jnp.where(even, west, east)


def pack_kernel(state, winds, diff, main, strip, first, second, *, grid):
    even = lon_even()
    flip = jnp.where(lat_even(), 3, 0)

    def body(t, level):
        strips = [[] for _ in range(3)]
        for p in range(4):
            r = jnp.abs(flip - p)
            source = pl.ds(t * 32 + r, 8, stride=4)
            row = [state[v, source, :] for v in range(VARS)] + [winds[v, source, :] for v in range(2)]
            row.append(jnp.broadcast_to(diff[pl.ds(r, 1), :], (8, 128)))
            for v in range(11):
                main[p, v, level, :] = row[v]
            for b in range(3):
                s = own_strip(lambda g: row[4 * b + g], 4 if b < 2 else 3)
                strip[p, b, level, :] = s
                strips[b].append(s)
        for b in range(3):
            first[b, level, :], second[b, level, :] = pack_strips(strips[b], even)

    level_tiles(TILES // grid, body)


def pack(state, winds, diff, grid=2):
    shapes = [(4, 11, LEV, 128), (4, 3, LEV, 128), (3, LEV, 128), (3, LEV, 128)]
    return pl.pallas_call(
        partial(pack_kernel, grid=grid),
        grid=(grid,),
        in_specs=[tiled(grid, 8, 256, 128), tiled(grid, 2, 256, 128), whole((4, 128))],
        out_specs=[tiled(grid, *s) for s in shapes],
        out_shape=[struct(*s) for s in shapes],
        compiler_params=params(16),
        name="pack",
    )(state, winds, diff)


def complete_kernel(strip, first, second, *outs, grid):
    even = lon_even()
    blocks = strip.shape[1]
    split = blocks // len(outs)

    def body(t, level):
        lane = lanes() % 32
        for b in range(blocks):
            one, two = first[b, level, :], second[b, level, :]
            east = jnp.where(even, one, two)
            west = jnp.where(even, two, one)
            for r in range(4):
                full = jnp.where(lane < 8, roll(west, -8 * r), strip[r, b, level, :])
                outs[b // split][r, b % split, level, :] = jnp.where(lane >= 24, roll(east, 24 - 8 * r), full)

    level_tiles(TILES // grid, body)


def complete(strip, first, second, parts, grid=1):
    blocks = strip.shape[1]
    split = blocks // parts
    return pl.pallas_call(
        partial(complete_kernel, grid=grid),
        grid=(grid,),
        in_specs=[tiled(grid, 4, blocks, LEV, 128), tiled(grid, blocks, LEV, 128), tiled(grid, blocks, LEV, 128)],
        out_specs=[tiled(grid, 4, split, LEV, 128)] * parts,
        out_shape=[struct(4, split, LEV, 128)] * parts,
        compiler_params=params(16),
        name="complete",
    )(strip, first, second)


def march(field, steps, coef, open_side, adjoint, edge, record):
    lane = lanes()
    for k in range(steps):
        reach = steps - 1 - k
        new = {}
        before = None
        for i in range(3 - reach, 8 + reach):
            f = field[i]
            u, w = coef(i, 2), coef(i, 3)
            if adjoint:
                rise = field[i + 1] - f
                here, passed = u * rise, w * rise
            else:
                here = passed = u * f + w * field[i + 1]
            if before is not None:
                a, b = coef(i, 0), coef(i, 1)
                east = roll(f, -1)
                if edge is not None:
                    rim = edge(k, i)
                    east = jnp.where(lane == 127, rim, east)
                if adjoint:
                    slope = east - f
                    flux = b * slope
                else:
                    flux = a * f + b * east
                shifted = roll(flux, 1)
                if edge is not None:
                    shifted = jnp.where(lane == 0, rim, shifted)
                else:
                    record(k, i, jnp.where(lane % 32 == 25, roll(flux, 18), f))
                if adjoint:
                    value = f + a * slope + shifted + here + before
                else:
                    value = f - (flux - shifted) - (here - before)
                if i >= 8:
                    value = value * open_side
                new[i] = value
            before = passed
        field = new
    return field


def advect_kernel(*refs, adjoint, slot, apart, first, result, addend, grid):
    refs = list(refs)
    counts = refs.pop(0)
    own, r0, r1 = refs[:3]
    refs = refs[3:]
    if apart:
        sown, s0, s1 = refs[:3]
        refs = refs[3:]
        base = 0
    else:
        sown, s0, s1 = own, r0, r1
        base = VARS
    if not first:
        coef_in = refs.pop(0)
    if addend:
        add_main, add_strip = refs[:2]
        refs = refs[2:]
    out = refs.pop(0)
    if first:
        coef_in = refs.pop(0)
    rims = refs.pop(0)
    lat = lax.axis_index("lat")
    flipped = lat % 2 == 0
    flip = jnp.where(flipped, 3, 0)
    open_side = jnp.where((lat > 0) & (lat < lax.axis_size("lat") - 1), 1.0, 0.0).astype(F32)

    def fetch(tile, intra, inter, i, v, level):
        if i < 4:
            return intra[3 - i, v, level, :]
        if i < 8:
            return tile[i - 4, v, level, :]
        return inter[11 - i, v, level, :]

    def prepare(level):
        lane = lanes()
        below = [None, None]
        for i in reversed(range(12)):
            packed = fetch(sown, s0, s1, i, 2, level)
            spread = []
            for g in range(3):
                one = jnp.where(lane < 32, roll(packed, -32 * g), 0.0)
                one = one + roll(one, 32)
                spread.append(one + roll(one, 64))
            plain = [fetch(own, r0, r1, i, VARS + v, level) for v in range(3)]
            for n, (w0, w1, dd) in enumerate((plain, spread)):
                c, d = w1 * 0.5 + dd, w1 * 0.5 - dd
                coef_in[i, 4 * n, level, :] = w0 * 0.5 + dd
                coef_in[i, 4 * n + 1, level, :] = w0 * 0.5 - dd
                if below[n] is None:
                    below[n] = (jnp.zeros_like(c), jnp.zeros_like(c))
                coef_in[i, 4 * n + 2, level, :] = jnp.where(flipped, -below[n][1], c)
                coef_in[i, 4 * n + 3, level, :] = jnp.where(flipped, -below[n][0], d)
                below[n] = (c, d)

    def run(steps):
        def block(t, level):
            if first:
                prepare(level)
            for b in range(2):
                strips = {i: fetch(sown, s0, s1, i, base + b, level) for i in range(4 - steps, 8 + steps)}

                def record(k, i, value):
                    rims[k, i] = value

                def edge(g):
                    return lambda k, i: roll(rims[k, i], 103 - 32 * g)

                strips = march(
                    strips, steps, lambda i, n: coef_in[i, 4 + n, level, :], open_side, adjoint, None, record
                )
                if result == "both":
                    for r in range(4):
                        value = strips[4 + r]
                        value = value + add_strip[r, b, level, :] if addend else value
                        out[r, VARS + b, level, :] = value
                for g in range(4):
                    v = 4 * b + g
                    field = {i: fetch(own, r0, r1, i, v, level) for i in range(4 - steps, 8 + steps)}
                    field = march(
                        field, steps, lambda i, n: coef_in[i, n, level, :], open_side, adjoint, edge(g), None
                    )
                    for r in range(4):
                        value = field[4 + r] + add_main[r, v, level, :] if addend else field[4 + r]
                        if result == "native":
                            out[v, pl.ds(t * 32 + jnp.abs(flip - r), 8, stride=4), :] = value
                        else:
                            out[r, v, level, :] = value

        level_tiles(TILES // grid, block)

    for steps in range(1, MAXSTEP + 1):
        pl.when(counts[slot] == steps)(partial(run, steps))


def advect(counts, slot, tile, strips, coef, adjoint, result, addend=None, grid=2):
    first = coef is None
    args = [*tile]
    if strips is not None:
        args += strips
    if not first:
        args.append(coef)
    if addend is not None:
        args += addend
    if result == "native":
        shapes = [(8, 256, 128)]
    else:
        shapes = [(4, 10 if result == "both" else 8, LEV, 128)]
    if first:
        shapes.append((12, 8, LEV, 128))
    return pl.pallas_call(
        partial(
            advect_kernel,
            adjoint=adjoint,
            slot=slot,
            apart=strips is not None,
            first=first,
            result=result,
            addend=addend is not None,
            grid=grid,
        ),
        grid=(grid,),
        in_specs=[SMEM_SPEC] + [tiled(grid, *x.shape) for x in args],
        out_specs=[tiled(grid, *s) for s in shapes],
        out_shape=[struct(*s) for s in shapes],
        scratch_shapes=[pltpu.VMEM((MAXSTEP, 12, 8, 128), F32)],
        compiler_params=params(24),
        name="advect_" + result + ("_adjoint" if adjoint else ""),
    )(counts, *args)


def split(x):
    high = x.astype(BF16)
    return high, (x - high.astype(F32)).astype(BF16)


def dot(x, y, dims):
    return lax.dot_general(x, y, ((dims[:1], dims[1:]), ((), ())), preferred_element_type=F32)


def dot3(x, y, dims):
    return dot(x[0], y[0], dims) + (dot(x[0], y[1], dims) + dot(x[1], y[0], dims))


def observe_kernel(
    cells, owners, field0, field1, fetched, ah, al, eh, el, weight, g0, g1, strip, first, second
):
    even = lon_even()
    flip = jnp.where(lat_even(), 3, 0)
    square = (SND, SND)
    row_id = lax.broadcasted_iota(I32, square, 0)
    lane_id = lax.broadcasted_iota(I32, square, 1)
    absorb = (ah[...], al[...])
    emission = (eh[...], el[...])
    for k, (field, out) in enumerate(((field0, g0), (field1, g1))):
        cell = jnp.sum(
            jnp.where(row_id == lane_id, jnp.broadcast_to(cells[k : k + 1, :], square), 0),
            axis=1,
            keepdims=True,
        )
        owner = owners[k]
        owner_row = jnp.sum(
            jnp.where(row_id == lane_id, jnp.broadcast_to(owner, square), 0), axis=0, keepdims=True
        )
        earlier = (owner == owner_row) & (lane_id < row_id)
        rank = jnp.sum(jnp.where(earlier, 1, 0), axis=1, keepdims=True)
        picks = [(cell == lane_id + 128 * jnp.abs(flip - r)).astype(F32).astype(BF16) for r in range(4)]
        high = jnp.zeros((SND, 512), F32)
        low = jnp.zeros((SND, 512), F32)
        for r in range(4):
            xh, xl = split(field[r, 0:VARS].reshape(VARS * LEV, 128))
            high = high + dot(picks[r], xh, (1, 1))
            low = low + dot(picks[r], xl, (1, 1))
        column = (high.astype(BF16), low.astype(BF16))
        optical = dot3(column, absorb, (1, 0))
        bright = dot3(column, emission, (1, 0))
        decay = jnp.exp(-jnp.abs(optical))
        inverse = 1.0 / (1.0 + decay)
        rest = decay * inverse
        positive = optical >= 0
        passing = jnp.where(positive, rest, inverse)
        opaque = jnp.where(positive, inverse, rest)
        choices = [((owner == lane_id) & (rank == q)).astype(F32).astype(BF16) for q in range(3)]
        parts = []
        for c in range(4):
            part = jnp.zeros(square, F32)
            for q in range(3):
                oh, ol = split(fetched[pl.ds(12 * k + 4 * q + c, SND, stride=24), :])
                part = part + (dot(choices[q], oh, (1, 0)) + dot(choices[q], ol, (1, 0)))
            parts.append(part)
        wanted = jnp.concatenate(parts, axis=1)
        evolved = passing * bright
        departure = weight[...] * (evolved - wanted)
        to_bright = departure * passing
        to_optical = -(departure * evolved * opaque)
        column = dot3(split(to_optical), absorb, (1, 1)) + dot3(split(to_bright), emission, (1, 1))
        ch, cl = split(column)
        for r in range(4):
            placed = dot(ch, picks[r], (0, 0)) + dot(cl, picks[r], (0, 0))
            out[r] = placed.reshape(VARS, LEV, 128)

    def strips_of(t, level):
        for b in range(4):
            out = g1 if b < 2 else g0
            strips = []
            for r in range(4):
                s = own_strip(lambda g: out[r, 4 * (b % 2) + g, level, :], 4)
                strip[r, b, level, :] = s
                strips.append(s)
            first[b, level, :], second[b, level, :] = pack_strips(strips, even)

    level_tiles(TILES, strips_of)


def observe(*args):
    shapes = [(4, 8, LEV, 128), (4, 8, LEV, 128), (4, 4, LEV, 128), (4, LEV, 128), (4, LEV, 128)]
    return pl.pallas_call(
        observe_kernel,
        in_specs=[pl.BlockSpec(memory_space=pltpu.VMEM)] * len(args),
        out_shape=[struct(*s) for s in shapes],
        compiler_params=params(32),
        name="observe",
    )(*args)


def swap(x, axis, parity, wrap):
    devices = lax.axis_size(axis)
    pairs = []
    for i in range(parity, devices, 2):
        if i + 1 < devices or wrap:
            j = (i + 1) % devices
            pairs += [(i, j), (j, i)]
    return lax.ppermute(x, axis, pairs)


def lat_swap(x):
    return swap(x, "lat", 1, False), swap(x, "lat", 0, False)


def lon_swap(first, second):
    return swap(second, "lon", 1, True), swap(first, "lon", 0, True)


def select_channels(channel_list, absorb_table, emit_table, obs_weight):
    hit = jnp.arange(obs_weight.shape[0], dtype=I32)[:, None] == channel_list[None, :]
    picker = hit.astype(BF16)

    def pick(table):
        high = lax.reduce_precision(table, 8, 7)
        low = lax.reduce_precision(table - high, 8, 7)
        take = lambda part: jnp.dot(part.astype(BF16), picker, preferred_element_type=F32).astype(BF16)
        return take(high), take(low)

    weight = jnp.sum(jnp.where(hit, obs_weight[:, None], 0.0), axis=0)[None, :]
    return (*pick(absorb_table), *pick(emit_table), weight)


def per_device(
    state, winds, diffusivity, sounding_cell, sounding_owner, step_counts, channel_list, absorb_table, emit_table,
    obs_weight, observed,
):
    main, strip, first, second = pack(state.reshape(8, 256, 128), winds.reshape(2, 256, 128), diffusivity)
    lon1, lon0 = lon_swap(first, second)
    lat1, lat0 = lat_swap(main)
    devices = observed.shape[2]
    sent = jnp.transpose(observed[:, 0], (1, 0, 2, 3)).reshape(devices, 24, 128)
    fetched = lax.all_to_all(sent, ("lon", "lat"), split_axis=0, concat_axis=0, tiled=True)
    channels = select_channels(channel_list, absorb_table, emit_table, obs_weight)
    (strips,) = complete(strip, lon0, lon1, 1)
    slat1, slat0 = lat_swap(strips)

    both0, coef = advect(step_counts, 0, (main, lat0, lat1), (strips, slat0, slat1), None, False, "both")
    lat1, lat0 = lat_swap(both0)
    (field1,) = advect(step_counts, 1, (both0, lat0, lat1), None, coef, False, "main")

    g0, g1, strip, first, second = observe(
        sounding_cell, sounding_owner, both0, field1, fetched.reshape(devices * 24, 128), *channels
    )
    lon1, lon0 = lon_swap(first, second)
    lat1, lat0 = lat_swap(g1)
    strips1, strips0 = complete(strip, lon0, lon1, 2)
    slat1, slat0 = lat_swap(strips1)
    (both,) = advect(
        step_counts, 1, (g1, lat0, lat1), (strips1, slat0, slat1), coef, True, "both", (g0, strips0)
    )
    lat1, lat0 = lat_swap(both)
    (result,) = advect(step_counts, 0, (both, lat0, lat1), None, coef, True, "native")
    return result.reshape(state.shape)


def solution(mesh):
    return jax.shard_map(
        per_device,
        mesh=mesh,
        in_specs=(
            P(None, None, "lat", "lon"),
            P(None, None, "lat", "lon"),
            P("lat", "lon"),
            P(None, ("lon", "lat")),
            P(None, ("lon", "lat"), None),
            P(),
            P(),
            P(),
            P(),
            P(),
            P(None, ("lon", "lat"), None, None, None),
        ),
        out_specs=P(None, None, "lat", "lon"),
        check_vma=False,
    )
```

```python
from functools import partial

import jax
import jax.numpy as jnp
from jax import lax
from jax.experimental import pallas as pl
from jax.experimental.pallas import tpu as pltpu
from jax.sharding import PartitionSpec as P

F32 = jnp.float32
BF16 = jnp.bfloat16
I32 = jnp.int32
VARS = 8
LEV = 64
TILES = 8
MAXSTEP = 4
SND = 128


def struct(*shape, dtype=F32):
    return jax.ShapeDtypeStruct(shape, dtype)


def tiled(grid, *shape):
    zeros = (0,) * (len(shape) - 2)
    return pl.BlockSpec((*shape[:-2], shape[-2] // grid, shape[-1]), lambda t: (*zeros, t, 0))


def whole(shape):
    return pl.BlockSpec(shape, lambda *_: (0,) * len(shape))


SMEM_SPEC = pl.BlockSpec(memory_space=pltpu.SMEM)


def params(mebibytes):
    return pltpu.CompilerParams(vmem_limit_bytes=mebibytes * 1024 * 1024)


def in_hbm(*arrays):
    return [pltpu.with_memory_space_constraint(x, pltpu.HBM) for x in arrays]


def lanes():
    return lax.broadcasted_iota(I32, (8, 128), 1)


def roll(x, shift):
    shift = shift % 128
    return x if shift == 0 else pltpu.roll(x, shift, 1)


def level_tiles(count, body):
    def step(t, carry):
        body(t, pl.ds(pl.multiple_of(t * 8, 8), 8))
        return carry

    lax.fori_loop(0, count, step, 0)


def lon_even():
    return lax.axis_index("lon") % 2 == 0


def lat_even():
    return lax.axis_index("lat") % 2 == 0


def own_strip(load, count):
    lane = lanes()
    strip = jnp.zeros((8, 128), F32)
    for g in range(count):
        x = load(g)
        base = 32 * g
        strip = jnp.where((lane >= base + 8) & (lane < base + 16), roll(x, base + 8), strip)
        strip = jnp.where((lane >= base + 16) & (lane < base + 24), roll(x, base + 24), strip)
    return strip


def pack_strips(strips, even):
    lane = lanes() % 32
    east = jnp.zeros((8, 128), F32)
    west = jnp.zeros((8, 128), F32)
    for r in range(4):
        here = (lane >= 8 * r) & (lane < 8 * r + 8)
        east = jnp.where(here, roll(strips[r], 8 * r - 16), east)
        west = jnp.where(here, roll(strips[r], 8 * r - 8), west)
    return jnp.where(even, east, west), jnp.where(even, west, east)


def pack_kernel(state, winds, diff, main, strip, first, second, *, grid):
    even = lon_even()
    flip = jnp.where(lat_even(), 3, 0)

    def body(t, level):
        strips = [[] for _ in range(3)]
        for p in range(4):
            r = jnp.abs(flip - p)
            source = pl.ds(t * 32 + r, 8, stride=4)
            row = [state[v, source, :] for v in range(VARS)] + [winds[v, source, :] for v in range(2)]
            row.append(jnp.broadcast_to(diff[pl.ds(r, 1), :], (8, 128)))
            for v in range(11):
                main[p, v, level, :] = row[v]
            for b in range(3):
                s = own_strip(lambda g: row[4 * b + g], 4 if b < 2 else 3)
                strip[p, b, level, :] = s
                strips[b].append(s)
        for b in range(3):
            first[b, level, :], second[b, level, :] = pack_strips(strips[b], even)

    level_tiles(TILES // grid, body)


def pack(state, winds, diff, grid=2):
    shapes = [(4, 11, LEV, 128), (4, 3, LEV, 128), (3, LEV, 128), (3, LEV, 128)]
    return pl.pallas_call(
        partial(pack_kernel, grid=grid),
        grid=(grid,),
        in_specs=[tiled(grid, 8, 256, 128), tiled(grid, 2, 256, 128), whole((4, 128))],
        out_specs=[tiled(grid, *s) for s in shapes],
        out_shape=[struct(*s) for s in shapes],
        compiler_params=params(16),
        name="pack",
    )(*in_hbm(state, winds), diff)


def complete_kernel(strip, first, second, *outs, grid):
    even = lon_even()
    blocks = strip.shape[1]
    split = blocks // len(outs)

    def body(t, level):
        lane = lanes() % 32
        for b in range(blocks):
            one, two = first[b, level, :], second[b, level, :]
            east = jnp.where(even, one, two)
            west = jnp.where(even, two, one)
            for r in range(4):
                full = jnp.where(lane < 8, roll(west, -8 * r), strip[r, b, level, :])
                outs[b // split][r, b % split, level, :] = jnp.where(lane >= 24, roll(east, 24 - 8 * r), full)

    level_tiles(TILES // grid, body)


def complete(strip, first, second, parts, grid=1):
    blocks = strip.shape[1]
    split = blocks // parts
    return pl.pallas_call(
        partial(complete_kernel, grid=grid),
        grid=(grid,),
        in_specs=[tiled(grid, 4, blocks, LEV, 128), tiled(grid, blocks, LEV, 128), tiled(grid, blocks, LEV, 128)],
        out_specs=[tiled(grid, 4, split, LEV, 128)] * parts,
        out_shape=[struct(4, split, LEV, 128)] * parts,
        compiler_params=params(16),
        name="complete",
    )(*in_hbm(strip, first, second))


def march(field, steps, coef, open_side, adjoint, edge, record):
    lane = lanes()
    for k in range(steps):
        reach = steps - 1 - k
        new = {}
        before = None
        for i in range(3 - reach, 8 + reach):
            f = field[i]
            u, w = coef(i, 2), coef(i, 3)
            if adjoint:
                rise = field[i + 1] - f
                here, passed = u * rise, w * rise
            else:
                here = passed = u * f + w * field[i + 1]
            if before is not None:
                a, b = coef(i, 0), coef(i, 1)
                east = roll(f, -1)
                if edge is not None:
                    rim = edge(k, i)
                    east = jnp.where(lane == 127, rim, east)
                if adjoint:
                    slope = east - f
                    flux = b * slope
                else:
                    flux = a * f + b * east
                shifted = roll(flux, 1)
                if edge is not None:
                    shifted = jnp.where(lane == 0, rim, shifted)
                else:
                    record(k, i, jnp.where(lane % 32 == 25, roll(flux, 18), f))
                if adjoint:
                    value = f + a * slope + shifted + here + before
                else:
                    value = f - (flux - shifted) - (here - before)
                if i >= 8:
                    value = value * open_side
                new[i] = value
            before = passed
        field = new
    return field


def advect_kernel(*refs, adjoint, steps, apart, first, result, addend, grid):
    refs = list(refs)
    if steps is None:
        counts = refs.pop(0)
    own, r0, r1 = refs[:3]
    refs = refs[3:]
    if apart:
        sown, s0, s1 = refs[:3]
        refs = refs[3:]
        base = 0
    else:
        sown, s0, s1 = own, r0, r1
        base = VARS
    if not first:
        coef_in = refs.pop(0)
    if addend:
        add_main, add_strip = refs[:2]
        refs = refs[2:]
    out = refs.pop(0)
    if first:
        coef_in = refs.pop(0)
    rims = refs.pop(0)
    lat = lax.axis_index("lat")
    flipped = lat % 2 == 0
    flip = jnp.where(flipped, 3, 0)
    open_side = jnp.where((lat > 0) & (lat < lax.axis_size("lat") - 1), 1.0, 0.0).astype(F32)

    def fetch(tile, intra, inter, i, v, level):
        if i < 4:
            return intra[3 - i, v, level, :]
        if i < 8:
            return tile[i - 4, v, level, :]
        return inter[inter.shape[0] + 7 - i, v, level, :]

    def prepare(level):
        lane = lanes()
        below = [None, None]
        for i in reversed(range(12)):
            packed = fetch(sown, s0, s1, i, 2, level)
            spread = []
            for g in range(3):
                one = jnp.where(lane < 32, roll(packed, -32 * g), 0.0)
                one = one + roll(one, 32)
                spread.append(one + roll(one, 64))
            plain = [fetch(own, r0, r1, i, VARS + v, level) for v in range(3)]
            for n, (w0, w1, dd) in enumerate((plain, spread)):
                c, d = w1 * 0.5 + dd, w1 * 0.5 - dd
                coef_in[i, 4 * n, level, :] = w0 * 0.5 + dd
                coef_in[i, 4 * n + 1, level, :] = w0 * 0.5 - dd
                if below[n] is None:
                    below[n] = (jnp.zeros_like(c), jnp.zeros_like(c))
                coef_in[i, 4 * n + 2, level, :] = jnp.where(flipped, -below[n][1], c)
                coef_in[i, 4 * n + 3, level, :] = jnp.where(flipped, -below[n][0], d)
                below[n] = (c, d)

    def run(steps):
        def block(t, level):
            if first:
                prepare(level)

            def record(k, i, value):
                rims[k, i] = value

            def edge(g):
                return lambda k, i: roll(rims[k, i], 103 - 32 * g)

            def group(b, carry):
                strips = {i: fetch(sown, s0, s1, i, base + b, level) for i in range(4 - steps, 8 + steps)}
                strips = march(
                    strips, steps, lambda i, n: coef_in[i, 4 + n, level, :], open_side, adjoint, None, record
                )
                if result == "both":
                    for r in range(4):
                        value = strips[4 + r]
                        value = value + add_strip[r, b, level, :] if addend else value
                        out[r, VARS + b, level, :] = value
                for g in range(4):
                    v = 4 * b + g
                    field = {i: fetch(own, r0, r1, i, v, level) for i in range(4 - steps, 8 + steps)}
                    field = march(
                        field, steps, lambda i, n: coef_in[i, n, level, :], open_side, adjoint, edge(g), None
                    )
                    for r in range(4):
                        value = field[4 + r] + add_main[r, v, level, :] if addend else field[4 + r]
                        if result == "native":
                            out[v, pl.ds(t * 32 + jnp.abs(flip - r), 8, stride=4), :] = value
                        else:
                            out[r, v, level, :] = value
                return carry

            lax.fori_loop(0, 2, group, 0)

        level_tiles(TILES // grid, block)

    if steps is None:
        for n in range(1, MAXSTEP + 1):
            pl.when(counts[0] == n)(partial(run, n))
    else:
        run(steps)


def advect(steps, tile, strips, coef, adjoint, result, addend=None, grid=2):
    first = coef is None
    args = [*tile]
    if strips is not None:
        args += strips
    if not first:
        args.append(coef)
    if addend is not None:
        args += addend
    if result == "native":
        shapes = [(8, 256, 128)]
    else:
        shapes = [(4, 10 if result == "both" else 8, LEV, 128)]
    if first:
        shapes.append((12, 8, LEV, 128))
    static = isinstance(steps, int)
    return pl.pallas_call(
        partial(
            advect_kernel,
            adjoint=adjoint,
            steps=steps if static else None,
            apart=strips is not None,
            first=first,
            result=result,
            addend=addend is not None,
            grid=grid,
        ),
        grid=(grid,),
        in_specs=([] if static else [SMEM_SPEC]) + [tiled(grid, *x.shape) for x in args],
        out_specs=[tiled(grid, *s) for s in shapes],
        out_shape=[struct(*s) for s in shapes],
        scratch_shapes=[pltpu.VMEM((MAXSTEP, 12, 8, 128), F32)],
        compiler_params=params(24),
        name="advect_" + result + ("_adjoint" if adjoint else ""),
    )(*([] if static else [steps]), *in_hbm(*args))


def split(x):
    high = x.astype(BF16)
    return high, (x - high.astype(F32)).astype(BF16)


def dot(x, y, dims):
    return lax.dot_general(x, y, ((dims[:1], dims[1:]), ((), ())), preferred_element_type=F32)


def dot3(x, y, dims):
    return dot(x[0], y[0], dims) + (dot(x[0], y[1], dims) + dot(x[1], y[0], dims))


def relayout_kernel(observed, sent):
    homes = observed.shape[3]
    for k in range(2):
        for q in range(3):
            for c in range(4):
                sent[pl.ds(12 * k + 4 * q + c, homes, stride=24), :] = observed[k, 0, q, :, pl.ds(128 * c, 128)]


def relayout(observed):
    turned = jnp.transpose(observed, (0, 1, 3, 2, 4))
    homes = turned.shape[3]
    sent = pl.pallas_call(
        relayout_kernel,
        grid=(1,),
        in_specs=[whole(turned.shape)],
        out_specs=whole((homes * 24, 128)),
        out_shape=struct(homes * 24, 128),
        compiler_params=params(16),
        name="relayout",
    )(*in_hbm(turned))
    return sent.reshape(homes, 24, 128)


PADDED = 640


def observe_kernel(cells, owners, channels, weight, *refs):
    hbm, refs = refs[:5], refs[5:]
    (g0, g1, strip, first, second), refs = refs[:5], refs[5:]
    (field0, fetched, absorb_table, emit_table, field1), refs = refs[:5], refs[5:]
    high_absorb, low_absorb, high_emit, low_emit, sems = refs
    copies = [
        pltpu.make_async_copy(source, target, sems.at[n])
        for n, (source, target) in enumerate(
            zip((hbm[0].at[:, pl.ds(0, VARS)], *hbm[1:]), (field0, absorb_table, emit_table, fetched, field1), strict=True)
        )
    ]
    for copy in copies:
        copy.start()

    even = lon_even()
    flip = jnp.where(lat_even(), 3, 0)
    square = (SND, SND)
    row_id = lax.broadcasted_iota(I32, square, 0)
    lane_id = lax.broadcasted_iota(I32, square, 1)
    entry = lax.broadcasted_iota(I32, (PADDED, channels.shape[1]), 0)
    listed = (entry == channels[...]).astype(F32).astype(BF16)
    times = dot(jnp.ones((8, channels.shape[1]), BF16), listed, (1, 1))[0:1]
    weights = weight[...]

    def column_of(row):
        spread = jnp.where(row_id == lane_id, jnp.broadcast_to(row, square), 0)
        return jnp.sum(spread, axis=1, keepdims=True)

    def gather(field, picks):
        high = jnp.zeros((SND, VARS * LEV), F32)
        low = jnp.zeros((SND, VARS * LEV), F32)
        for r in range(4):
            xh, xl = split(field[r].reshape(VARS * LEV, 128))
            high = high + dot(picks[r], xh, (1, 1))
            low = low + dot(picks[r], xl, (1, 1))
        return high.astype(BF16), low.astype(BF16)

    def load_table(table, high, low):
        count = table.shape[0]
        full = count // 16 * 16
        high[pl.ds(0, full), :], low[pl.ds(0, full), :] = split(table[pl.ds(0, full), :])
        rest = jnp.zeros((PADDED - full, table.shape[1]), F32)
        if count > full:
            zeros = jnp.zeros((PADDED - count, table.shape[1]), F32)
            rest = jnp.concatenate([table[pl.ds(full, count - full), :], zeros], axis=0)
        high[pl.ds(full, PADDED - full), :], low[pl.ds(full, PADDED - full), :] = split(rest)

    for k, (field, out) in enumerate(((field0, g0), (field1, g1))):
        cell = column_of(cells[k : k + 1, :])
        owner_row = owners[k : k + 1, :]
        owner = column_of(owner_row)
        earlier = (owner == owner_row) & (lane_id < row_id)
        rank = jnp.sum(jnp.where(earlier, 1, 0), axis=1, keepdims=True)
        picks = [(cell == lane_id + 128 * jnp.abs(flip - r)).astype(F32).astype(BF16) for r in range(4)]
        copies[4 * k].wait()
        column = gather(field, picks)
        if k == 0:
            copies[1].wait()
            load_table(absorb_table, high_absorb, low_absorb)
            copies[2].wait()
            load_table(emit_table, high_emit, low_emit)
        absorb = (high_absorb[...], low_absorb[...])
        emission = (high_emit[...], low_emit[...])
        optical = dot3(column, absorb, (1, 1))
        bright = dot3(column, emission, (1, 1))
        decay = jnp.exp(-jnp.abs(optical))
        inverse = 1.0 / (1.0 + decay)
        rest = decay * inverse
        positive = optical >= 0
        passing = jnp.where(positive, rest, inverse)
        opaque = jnp.where(positive, inverse, rest)
        choices = [((owner == lane_id) & (rank == q)).astype(F32).astype(BF16) for q in range(3)]
        if k == 0:
            copies[3].wait()
        parts = []
        for c in range(4):
            part = [jnp.zeros(square, F32), jnp.zeros(square, F32)]
            for q in range(3):
                pieces = split(fetched[pl.ds(12 * k + 4 * q + c, SND, stride=24), :])
                part = [p + dot(choices[q], piece, (1, 0)) for p, piece in zip(part, pieces, strict=True)]
            parts.append(part)
        wanted = [jnp.concatenate([part[n] for part in parts], axis=1).astype(BF16) for n in range(2)]
        totals = dot(wanted[0], listed, (1, 1)) + dot(wanted[1], listed, (1, 1))
        evolved = passing * bright
        departure = weights * (times * evolved - totals)
        to_bright = departure * passing
        to_optical = -(departure * evolved * opaque)
        column = dot3(split(to_optical), absorb, (1, 0)) + dot3(split(to_bright), emission, (1, 0))
        ch, cl = split(column)
        for r in range(4):
            placed = dot(ch, picks[r], (0, 0)) + dot(cl, picks[r], (0, 0))
            out[r] = placed.reshape(VARS, LEV, 128)

    def strips_of(t, level):
        for b in range(4):
            out = g1 if b < 2 else g0
            strips = []
            for r in range(4):
                s = own_strip(lambda g: out[r, 4 * (b % 2) + g, level, :], 4)
                strip[r, b, level, :] = s
                strips.append(s)
            first[b, level, :], second[b, level, :] = pack_strips(strips, even)

    level_tiles(TILES, strips_of)


def observe(cells, owners, channels, weight, field0, absorb, emit, fetched, field1):
    shapes = [(4, 8, LEV, 128), (4, 8, LEV, 128), (4, 4, LEV, 128), (4, LEV, 128), (4, LEV, 128)]
    small = [cells, owners, channels, weight]
    field = (4, 8, LEV, 128)
    return pl.pallas_call(
        observe_kernel,
        grid=(1,),
        in_specs=[whole(x.shape) for x in small] + [pl.BlockSpec(memory_space=pltpu.HBM)] * 5,
        out_specs=[whole(s) for s in shapes],
        out_shape=[struct(*s) for s in shapes],
        scratch_shapes=[pltpu.VMEM(x, F32) for x in (field, fetched.shape, absorb.shape, emit.shape, field)]
        + [pltpu.VMEM((PADDED, absorb.shape[1]), BF16)] * 4
        + [pltpu.SemaphoreType.DMA((5,))],
        compiler_params=params(40),
        name="observe",
    )(*small, *in_hbm(field0, absorb, emit, fetched, field1))


def swap(x, axis, parity, wrap):
    devices = lax.axis_size(axis)
    pairs = []
    for i in range(parity, devices, 2):
        if i + 1 < devices or wrap:
            j = (i + 1) % devices
            pairs += [(i, j), (j, i)]
    return lax.ppermute(x, axis, pairs)


def lat_swap(x, width=4):
    beyond = swap(x[4 - width :], "lat", 1, False)
    return swap(x[:width], "lat", 0, False), beyond


def lon_swap(first, second):
    beyond = swap(second, "lon", 1, True)
    return swap(first, "lon", 0, True), beyond


def per_device(
    state, winds, diffusivity, sounding_cell, sounding_owner, step_counts, channel_list, absorb_table, emit_table,
    obs_weight, observed,
):
    def by_steps(slot, run):
        branches = [partial(run, width) for width in range(1, MAXSTEP + 1)]
        return lax.switch(step_counts[slot] - 1, branches)

    main, strip, first, second = pack(state.reshape(8, 256, 128), winds.reshape(2, 256, 128), diffusivity)
    received = lon_swap(first, second)
    halo = lat_swap(main)
    sent = relayout(observed)
    fetched = lax.all_to_all(sent, ("lon", "lat"), split_axis=0, concat_axis=0, tiled=True)
    (strips,) = complete(strip, *received, 1)
    both0, coef = advect(step_counts[:1], (main, *halo), (strips, *lat_swap(strips)), None, False, "both")

    def forward(width):
        return advect(width, (both0, *lat_swap(both0, width)), None, coef, False, "main")

    (field1,) = by_steps(1, forward)

    extra = PADDED - obs_weight.shape[0]
    g0, g1, strip, first, second = observe(
        sounding_cell,
        sounding_owner[:, :, 0],
        channel_list[None, :],
        jnp.pad(obs_weight, (0, extra))[None, :],
        both0,
        absorb_table.T,
        emit_table.T,
        fetched.reshape(-1, 128),
        field1,
    )

    def backward(width):
        received = lon_swap(first, second)
        halo = lat_swap(g1, width)
        strips1, strips0 = complete(strip, *received, 2)
        halo_strips = lat_swap(strips1, width)
        return advect(width, (g1, *halo), (strips1, *halo_strips), coef, True, "both", (g0, strips0))

    (both,) = by_steps(1, backward)

    def last(width):
        return advect(width, (both, *lat_swap(both, width)), None, coef, True, "native")

    (result,) = by_steps(0, last)
    return result.reshape(state.shape)


def solution(mesh):
    return jax.shard_map(
        per_device,
        mesh=mesh,
        in_specs=(
            P(None, None, "lat", "lon"),
            P(None, None, "lat", "lon"),
            P("lat", "lon"),
            P(None, ("lon", "lat")),
            P(None, ("lon", "lat"), None),
            P(),
            P(),
            P(),
            P(),
            P(),
            P(None, ("lon", "lat"), None, None, None),
        ),
        out_specs=P(None, None, "lat", "lon"),
        check_vma=False,
    )
```

```python
from functools import partial

import jax
import jax.numpy as jnp
from jax import lax
from jax.experimental import pallas as pl
from jax.experimental.pallas import tpu as pltpu
from jax.sharding import PartitionSpec as P

F32 = jnp.float32
BF16 = jnp.bfloat16
I32 = jnp.int32
VARS = 8
SPAN = 16
RIM_SPAN = 32
LEV = 64
TILES = 8
MAXSTEP = 4
SND = 128


def struct(*shape, dtype=F32):
    return jax.ShapeDtypeStruct(shape, dtype)


def tiled(grid, *shape):
    zeros = (0,) * (len(shape) - 2)
    return pl.BlockSpec((*shape[:-2], shape[-2] // grid, shape[-1]), lambda t: (*zeros, t, 0))


def whole(shape):
    return pl.BlockSpec(shape, lambda *_: (0,) * len(shape))


VMEM_SPEC = pl.BlockSpec(memory_space=pltpu.VMEM)
SMEM_SPEC = pl.BlockSpec(memory_space=pltpu.SMEM)


def params(mebibytes):
    return pltpu.CompilerParams(vmem_limit_bytes=mebibytes * 1024 * 1024)


def in_hbm(*arrays):
    return [pltpu.with_memory_space_constraint(x, pltpu.HBM) for x in arrays]


def lanes():
    return lax.broadcasted_iota(I32, (8, 128), 1)


def roll(x, shift):
    shift = shift % 128
    return x if shift == 0 else pltpu.roll(x, shift, 1)


def level_tiles(count, body, span=8):
    def step(t, carry):
        body(t, pl.ds(pl.multiple_of(t * span, span), span))
        return carry

    lax.fori_loop(0, count, step, 0)


def lon_even():
    return lax.axis_index("lon") % 2 == 0


def lat_even():
    return lax.axis_index("lat") % 2 == 0


def own_strip(load, count):
    lane = lanes()
    strip = jnp.zeros((8, 128), F32)
    for g in range(count):
        x = load(g)
        base = 32 * g
        strip = jnp.where((lane >= base + 8) & (lane < base + 16), roll(x, base + 8), strip)
        strip = jnp.where((lane >= base + 16) & (lane < base + 24), roll(x, base + 24), strip)
    return strip


def pack_strips(strips, even):
    lane = lanes() % 32
    east = jnp.zeros((8, 128), F32)
    west = jnp.zeros((8, 128), F32)
    for r in range(4):
        here = (lane >= 8 * r) & (lane < 8 * r + 8)
        east = jnp.where(here, roll(strips[r], 8 * r - 16), east)
        west = jnp.where(here, roll(strips[r], 8 * r - 8), west)
    return jnp.where(even, east, west), jnp.where(even, west, east)


def pack_kernel(state, winds, diff, main, strip, first, second, *, grid):
    even = lon_even()
    flip = jnp.where(lat_even(), 3, 0)

    def body(t, level):
        strips = [[] for _ in range(3)]
        for p in range(4):
            r = jnp.abs(flip - p)
            source = pl.ds(t * 32 + r, 8, stride=4)
            row = [state[v, source, :] for v in range(VARS)] + [winds[v, source, :] for v in range(2)]
            row.append(jnp.broadcast_to(diff[pl.ds(r, 1), :], (8, 128)))
            for v in range(11):
                main[p, v, level, :] = row[v]
            for b in range(3):
                s = own_strip(lambda g: row[4 * b + g], 4 if b < 2 else 3)
                strip[p, b, level, :] = s
                strips[b].append(s)
        for b in range(3):
            first[b, level, :], second[b, level, :] = pack_strips(strips[b], even)

    level_tiles(TILES // grid, body)


def pack(state, winds, diff, grid=2):
    shapes = [(4, 11, LEV, 128), (4, 3, LEV, 128), (3, LEV, 128), (3, LEV, 128)]
    return pl.pallas_call(
        partial(pack_kernel, grid=grid),
        grid=(grid,),
        in_specs=[tiled(grid, 8, 256, 128), tiled(grid, 2, 256, 128), whole((4, 128))],
        out_specs=[tiled(grid, *s) for s in shapes],
        out_shape=[struct(*s) for s in shapes],
        compiler_params=params(16),
        name="pack",
    )(*in_hbm(state, winds), diff)


def complete_kernel(strip, first, second, *outs):
    even = lon_even()
    blocks = strip.shape[1]
    split = blocks // len(outs)

    def body(t, level):
        lane = lax.broadcasted_iota(I32, (SPAN, 128), 1) % 32
        for b in range(blocks):
            one, two = first[b, level, :], second[b, level, :]
            east = jnp.where(even, one, two)
            west = jnp.where(even, two, one)
            for r in range(4):
                full = jnp.where(lane < 8, roll(west, -8 * r), strip[r, b, level, :])
                outs[b // split][r, b % split, level, :] = jnp.where(lane >= 24, roll(east, 24 - 8 * r), full)

    level_tiles(LEV // SPAN, body, SPAN)


def complete(strip, first, second, parts):
    split = strip.shape[1] // parts
    return pl.pallas_call(
        complete_kernel,
        in_specs=[VMEM_SPEC] * 3,
        out_specs=[VMEM_SPEC] * parts,
        out_shape=[struct(4, split, LEV, 128)] * parts,
        compiler_params=params(4),
        name="complete",
    )(strip, first, second)


def coefficient_kernel(own, r0, r1, sown, s0, s1, forward, adjoint, work):
    lat = lax.axis_index("lat")
    flipped = lat % 2 == 0
    open_side = jnp.where((lat > 0) & (lat < lax.axis_size("lat") - 1), 1.0, 0.0).astype(F32)

    def fetch(tile, intra, inter, i, v, level):
        if i < 4:
            return intra[3 - i, v, level, :]
        if i < 8:
            return tile[i - 4, v, level, :]
        return inter[11 - i, v, level, :]

    def body(t, level):
        lane = lanes()
        after = [None, None]
        for i in reversed(range(12)):
            packed = fetch(sown, s0, s1, i, 2, level)
            spread = []
            for g in range(3):
                one = jnp.where(lane < 32, roll(packed, -32 * g), 0.0)
                one = one + roll(one, 32)
                spread.append(one + roll(one, 64))
            plain = [fetch(own, r0, r1, i, VARS + v, level) for v in range(3)]
            for n, (w0, w1, dd) in enumerate((plain, spread)):
                a, b = w0 * 0.5 + dd, w0 * 0.5 - dd
                c, d = w1 * 0.5 + dd, w1 * 0.5 - dd
                a_west, b_west = roll(a, 1), roll(b, 1)
                if n == 0:
                    rim = roll(spread[0], 121) * 0.5
                    rim_diff = roll(spread[2], 121)
                    a_west = jnp.where(lane == 0, rim + rim_diff, a_west)
                    b_west = jnp.where(lane == 0, rim - rim_diff, b_west)
                zero = jnp.zeros_like(c)
                below = after[n] or (zero, zero)
                u = jnp.where(flipped, -below[1], c)
                w = jnp.where(flipped, -below[0], d)
                after[n] = (c, d)
                for m, value in enumerate((1.0 - a + b_west - u, a, b, a_west, b_west, u, w)):
                    work[i, n, m] = value
        for i in range(1, 12):
            for n in range(2):
                centre, a, b, a_west, b_west, u, w = (work[i, n, m] for m in range(7))
                u_before, w_before = work[i - 1, n, 5], work[i - 1, n, 6]
                centre = centre + w_before
                sets = (centre, -b, a_west, -w, u_before), (centre, a, -b_west, u, -w_before)
                for out, values in zip((forward, adjoint), sets, strict=True):
                    for m, value in enumerate(values):
                        out[i, 5 * n + m, level, :] = value * open_side if i >= 8 else value

    level_tiles(TILES, body)


def coefficients(tile, strips):
    return pl.pallas_call(
        coefficient_kernel,
        in_specs=[VMEM_SPEC] * 6,
        out_specs=[VMEM_SPEC] * 2,
        out_shape=[struct(12, 10, LEV, 128)] * 2,
        scratch_shapes=[pltpu.VMEM((12, 2, 7, 8, 128), F32)],
        compiler_params=params(8),
        name="coefficients",
    )(*tile, *strips)


def advect_kernel(*refs, steps, apart, result, addend):
    refs = list(refs)
    if steps is None:
        counts = refs.pop(0)
    own, r0, r1 = refs[:3]
    refs = refs[3:]
    if apart:
        sown, s0, s1 = refs[:3]
        refs = refs[3:]
        base = 0
    else:
        sown, s0, s1 = own, r0, r1
        base = VARS
    coef = refs.pop(0)
    if addend:
        add_main, add_strip = refs[:2]
        refs = refs[2:]
    out = refs.pop(0)
    *work, rims = refs
    flip = jnp.where(lat_even(), 3, 0)

    def fetch(tile, intra, inter, i, v, level):
        if i < 4:
            return intra[3 - i, v, level, :]
        if i < 8:
            return tile[i - 4, v, level, :]
        return inter[inter.shape[0] + 7 - i, v, level, :]

    def run(steps):
        for k in range(steps):
            reach = steps - 1 - k
            last = reach == 0

            def load(i, v, level):
                if k == 0:
                    if v < VARS:
                        return fetch(own, r0, r1, i, v, level)
                    return fetch(sown, s0, s1, i, base + v - VARS, level)
                return work[(k - 1) % 2][i, v, level, :]

            def store(i, v, level, t, value):
                if not last:
                    work[k % 2][i, v, level, :] = value
                    return
                r = i - 4
                if addend:
                    value = value + (add_main[r, v, level, :] if v < VARS else add_strip[r, v - VARS, level, :])
                if result == "native":
                    out[v, pl.ds(t * 4 * SPAN + jnp.abs(flip - r), SPAN, stride=4), :] = value
                else:
                    out[r, v, level, :] = value

            rows = range(4 - reach, 8 + reach)

            def stencil(i, n, v, level, f, east, west):
                value = coef[i, n, level, :] * f
                value = value + coef[i, n + 1, level, :] * east
                value = value + coef[i, n + 2, level, :] * west
                value = value + coef[i, n + 3, level, :] * load(i + 1, v, level)
                return value + coef[i, n + 4, level, :] * load(i - 1, v, level)

            def outer(t, level):
                lane = lax.broadcasted_iota(I32, (RIM_SPAN, 128), 1)
                for b in range(2):
                    ends = {}
                    for i in rows:
                        f = load(i, VARS + b, level)
                        ends[i] = jnp.where(lane % 32 == 25, roll(f, 18), f)
                    for g in range(4):
                        for i in rows:
                            rims[i, 4 * b + g, level, :] = roll(ends[i], 103 - 32 * g)

            def inner(t, level):
                lane = lax.broadcasted_iota(I32, (SPAN, 128), 1)
                for v in range(VARS if last and result != "both" else VARS + 2):
                    for i in rows:
                        f = load(i, v, level)
                        east, west = roll(f, -1), roll(f, 1)
                        if v < VARS:
                            rim = rims[i, v, level, :]
                            east = jnp.where(lane == 127, rim, east)
                            west = jnp.where(lane == 0, rim, west)
                        store(i, v, level, t, stencil(i, 0 if v < VARS else 5, v, level, f, east, west))

            level_tiles(LEV // RIM_SPAN, outer, RIM_SPAN)
            level_tiles(LEV // SPAN, inner, SPAN)

    if steps is None:
        for n in range(1, MAXSTEP + 1):
            pl.when(counts[0] == n)(partial(run, n))
    else:
        run(steps)


def advect(steps, tile, strips, coef, result, addend=None):
    args = [*tile]
    if strips is not None:
        args += strips
    args.append(coef)
    if addend is not None:
        args += addend
    if result == "native":
        shape = (8, 256, 128)
    else:
        shape = (4, 10 if result == "both" else 8, LEV, 128)
    static = isinstance(steps, int)
    return pl.pallas_call(
        partial(
            advect_kernel,
            steps=steps if static else None,
            apart=strips is not None,
            result=result,
            addend=addend is not None,
        ),
        in_specs=([] if static else [SMEM_SPEC]) + [VMEM_SPEC] * len(args),
        out_specs=VMEM_SPEC,
        out_shape=struct(*shape),
        scratch_shapes=[pltpu.VMEM((12, 10, LEV, 128), F32)] * 2 + [pltpu.VMEM((12, 8, LEV, 128), F32)],
        compiler_params=params(24),
        name="advect_" + result,
    )(*([] if static else [steps]), *args)


def split(x):
    high = x.astype(BF16)
    return high, (x - high.astype(F32)).astype(BF16)


def dot(x, y, dims):
    return lax.dot_general(x, y, ((dims[:1], dims[1:]), ((), ())), preferred_element_type=F32)


def dot3(x, y, dims):
    return dot(x[0], y[0], dims) + (dot(x[0], y[1], dims) + dot(x[1], y[0], dims))


def relayout_kernel(observed, sent):
    homes = observed.shape[3]
    for k in range(2):
        for q in range(3):
            for c in range(4):
                sent[pl.ds(12 * k + 4 * q + c, homes, stride=24), :] = observed[k, 0, q, :, pl.ds(128 * c, 128)]


def relayout(observed):
    turned = jnp.transpose(observed, (0, 1, 3, 2, 4))
    homes = turned.shape[3]
    sent = pl.pallas_call(
        relayout_kernel,
        grid=(1,),
        in_specs=[whole(turned.shape)],
        out_specs=whole((homes * 24, 128)),
        out_shape=struct(homes * 24, 128),
        compiler_params=params(16),
        name="relayout",
    )(*in_hbm(turned))
    return sent.reshape(homes, 24, 128)


PADDED = 640


def observe_kernel(cells, owners, channels, weight, *refs):
    (field0, field1), hbm, refs = refs[:2], refs[2:5], refs[5:]
    (g0, g1, strip, first, second), refs = refs[:5], refs[5:]
    (absorb_table, emit_table, fetched), refs = refs[:3], refs[3:]
    high_absorb, low_absorb, high_emit, low_emit, sems = refs
    copies = [
        pltpu.make_async_copy(source, target, sems.at[n])
        for n, (source, target) in enumerate(zip(hbm, (absorb_table, emit_table, fetched), strict=True))
    ]
    for copy in copies:
        copy.start()

    even = lon_even()
    flip = jnp.where(lat_even(), 3, 0)
    square = (SND, SND)
    row_id = lax.broadcasted_iota(I32, square, 0)
    lane_id = lax.broadcasted_iota(I32, square, 1)
    entry = lax.broadcasted_iota(I32, (PADDED, channels.shape[1]), 0)
    listed = (entry == channels[...]).astype(F32).astype(BF16)
    times = dot(jnp.ones((8, channels.shape[1]), BF16), listed, (1, 1))[0:1]
    weights = weight[...]

    def column_of(row):
        spread = jnp.where(row_id == lane_id, jnp.broadcast_to(row, square), 0)
        return jnp.sum(spread, axis=1, keepdims=True)

    def gather(field, picks):
        high = jnp.zeros((SND, VARS * LEV), F32)
        low = jnp.zeros((SND, VARS * LEV), F32)
        for r in range(4):
            xh, xl = split(field[r, 0:VARS].reshape(VARS * LEV, 128))
            high = high + dot(picks[r], xh, (1, 1))
            low = low + dot(picks[r], xl, (1, 1))
        return high.astype(BF16), low.astype(BF16)

    def load_table(table, high, low):
        count = table.shape[0]
        full = count // 16 * 16
        high[pl.ds(0, full), :], low[pl.ds(0, full), :] = split(table[pl.ds(0, full), :])
        rest = jnp.zeros((PADDED - full, table.shape[1]), F32)
        if count > full:
            zeros = jnp.zeros((PADDED - count, table.shape[1]), F32)
            rest = jnp.concatenate([table[pl.ds(full, count - full), :], zeros], axis=0)
        high[pl.ds(full, PADDED - full), :], low[pl.ds(full, PADDED - full), :] = split(rest)

    for k, (field, out) in enumerate(((field0, g0), (field1, g1))):
        cell = column_of(cells[k : k + 1, :])
        owner_row = owners[k : k + 1, :]
        owner = column_of(owner_row)
        earlier = (owner == owner_row) & (lane_id < row_id)
        rank = jnp.sum(jnp.where(earlier, 1, 0), axis=1, keepdims=True)
        picks = [(cell == lane_id + 128 * jnp.abs(flip - r)).astype(F32).astype(BF16) for r in range(4)]
        column = gather(field, picks)
        if k == 0:
            copies[0].wait()
            load_table(absorb_table, high_absorb, low_absorb)
            copies[1].wait()
            load_table(emit_table, high_emit, low_emit)
        absorb = (high_absorb[...], low_absorb[...])
        emission = (high_emit[...], low_emit[...])
        optical = dot3(column, absorb, (1, 1))
        bright = dot3(column, emission, (1, 1))
        decay = jnp.exp(-jnp.abs(optical))
        inverse = 1.0 / (1.0 + decay)
        rest = decay * inverse
        positive = optical >= 0
        passing = jnp.where(positive, rest, inverse)
        opaque = jnp.where(positive, inverse, rest)
        choices = [((owner == lane_id) & (rank == q)).astype(F32).astype(BF16) for q in range(3)]
        if k == 0:
            copies[2].wait()
        parts = []
        for c in range(4):
            part = [jnp.zeros(square, F32), jnp.zeros(square, F32)]
            for q in range(3):
                pieces = split(fetched[pl.ds(12 * k + 4 * q + c, SND, stride=24), :])
                part = [p + dot(choices[q], piece, (1, 0)) for p, piece in zip(part, pieces, strict=True)]
            parts.append(part)
        wanted = [jnp.concatenate([part[n] for part in parts], axis=1).astype(BF16) for n in range(2)]
        totals = dot(wanted[0], listed, (1, 1)) + dot(wanted[1], listed, (1, 1))
        evolved = passing * bright
        departure = weights * (times * evolved - totals)
        to_bright = departure * passing
        to_optical = -(departure * evolved * opaque)
        column = dot3(split(to_optical), absorb, (1, 0)) + dot3(split(to_bright), emission, (1, 0))
        ch, cl = split(column)
        for r in range(4):
            placed = dot(ch, picks[r], (0, 0)) + dot(cl, picks[r], (0, 0))
            out[r] = placed.reshape(VARS, LEV, 128)

    def strips_of(t, level):
        for b in range(4):
            out = g1 if b < 2 else g0
            strips = []
            for r in range(4):
                s = own_strip(lambda g: out[r, 4 * (b % 2) + g, level, :], 4)
                strip[r, b, level, :] = s
                strips.append(s)
            first[b, level, :], second[b, level, :] = pack_strips(strips, even)

    level_tiles(TILES, strips_of)


def observe(cells, owners, channels, weight, field0, field1, absorb, emit, fetched):
    shapes = [(4, 8, LEV, 128), (4, 8, LEV, 128), (4, 4, LEV, 128), (4, LEV, 128), (4, LEV, 128)]
    return pl.pallas_call(
        observe_kernel,
        in_specs=[VMEM_SPEC] * 6 + [pl.BlockSpec(memory_space=pltpu.HBM)] * 3,
        out_specs=[VMEM_SPEC] * 5,
        out_shape=[struct(*s) for s in shapes],
        scratch_shapes=[pltpu.VMEM(x.shape, F32) for x in (absorb, emit, fetched)]
        + [pltpu.VMEM((PADDED, absorb.shape[1]), BF16)] * 4
        + [pltpu.SemaphoreType.DMA((3,))],
        compiler_params=params(20),
        name="observe",
    )(cells, owners, channels, weight, field0, field1, *in_hbm(absorb, emit, fetched))


def swap(x, axis, parity, wrap):
    devices = lax.axis_size(axis)
    pairs = []
    for i in range(parity, devices, 2):
        if i + 1 < devices or wrap:
            j = (i + 1) % devices
            pairs += [(i, j), (j, i)]
    return lax.ppermute(x, axis, pairs)


def lat_swap(x, width=4):
    beyond = swap(x[4 - width :], "lat", 1, False)
    return swap(x[:width], "lat", 0, False), beyond


def lon_swap(first, second):
    beyond = swap(second, "lon", 1, True)
    return swap(first, "lon", 0, True), beyond


def per_device(
    state, winds, diffusivity, sounding_cell, sounding_owner, step_counts, channel_list, absorb_table, emit_table,
    obs_weight, observed,
):
    def by_steps(slot, run):
        branches = [partial(run, width) for width in range(1, MAXSTEP + 1)]
        return lax.switch(step_counts[slot] - 1, branches)

    main, strip, first, second = pack(state.reshape(8, 256, 128), winds.reshape(2, 256, 128), diffusivity)
    received = lon_swap(first, second)
    halo = lat_swap(main)
    sent, received = lax.optimization_barrier((relayout(observed), received))
    (strip,) = complete(strip, *received, 1)
    fetched = lax.all_to_all(sent, ("lon", "lat"), split_axis=0, concat_axis=0, tiled=True)
    tile, strips = (main, *halo), (strip, *lat_swap(strip))
    onward, backward_coef = coefficients(tile, strips)
    both0 = advect(step_counts[:1], tile, strips, onward, "both")

    field1 = advect(step_counts[1:], (both0, *lat_swap(both0)), None, onward, "main")

    extra = PADDED - obs_weight.shape[0]
    g0, g1, strip, first, second = observe(
        sounding_cell,
        sounding_owner[:, :, 0],
        channel_list[None, :],
        jnp.pad(obs_weight, (0, extra))[None, :],
        both0,
        field1,
        absorb_table.T,
        emit_table.T,
        fetched.reshape(-1, 128),
    )

    def backward(width):
        received = lon_swap(first, second)
        halo = lat_swap(g1, width)
        strips1, strips0 = complete(strip, *received, 2)
        halo_strips = lat_swap(strips1, width)
        return advect(width, (g1, *halo), (strips1, *halo_strips), backward_coef, "both", (g0, strips0))

    both = by_steps(1, backward)

    def last(width):
        return advect(width, (both, *lat_swap(both, width)), None, backward_coef, "native")

    result = by_steps(0, last)
    return result.reshape(state.shape)


def solution(mesh):
    return jax.shard_map(
        per_device,
        mesh=mesh,
        in_specs=(
            P(None, None, "lat", "lon"),
            P(None, None, "lat", "lon"),
            P("lat", "lon"),
            P(None, ("lon", "lat")),
            P(None, ("lon", "lat"), None),
            P(),
            P(),
            P(),
            P(),
            P(),
            P(None, ("lon", "lat"), None, None, None),
        ),
        out_specs=P(None, None, "lat", "lon"),
        check_vma=False,
    )
```

```python
from functools import partial

import jax
import jax.numpy as jnp
from jax import lax
from jax.experimental import pallas as pl
from jax.experimental.pallas import tpu as pltpu
from jax.sharding import PartitionSpec as P

F32 = jnp.float32
BF16 = jnp.bfloat16
I32 = jnp.int32
VARS = 8
SPAN = 32
STRIP_SPAN = 16
LEV = 64
MAXSTEP = 4
SND = 128


def struct(*shape, dtype=F32):
    return jax.ShapeDtypeStruct(shape, dtype)


def tiled(grid, *shape):
    zeros = (0,) * (len(shape) - 2)
    return pl.BlockSpec((*shape[:-2], shape[-2] // grid, shape[-1]), lambda t: (*zeros, t, 0))


def whole(shape):
    return pl.BlockSpec(shape, lambda *_: (0,) * len(shape))


VMEM_SPEC = pl.BlockSpec(memory_space=pltpu.VMEM)
SMEM_SPEC = pl.BlockSpec(memory_space=pltpu.SMEM)


def params(mebibytes):
    return pltpu.CompilerParams(vmem_limit_bytes=mebibytes * 1024 * 1024)


def in_hbm(*arrays):
    return [pltpu.with_memory_space_constraint(x, pltpu.HBM) for x in arrays]


def lanes():
    return lax.broadcasted_iota(I32, (STRIP_SPAN, 128), 1)


def roll(x, shift):
    shift = shift % 128
    return x if shift == 0 else pltpu.roll(x, shift, 1)


def level_tiles(count, body, span=8):
    def step(t, carry):
        body(t, pl.ds(pl.multiple_of(t * span, span), span))
        return carry

    lax.fori_loop(0, count, step, 0)


def lon_even():
    return lax.axis_index("lon") % 2 == 0


def lat_even():
    return lax.axis_index("lat") % 2 == 0


def own_strip(load, count):
    lane = lanes()
    strip = jnp.zeros((STRIP_SPAN, 128), F32)
    for g in range(count):
        x = load(g)
        base = 32 * g
        strip = jnp.where((lane >= base + 8) & (lane < base + 16), roll(x, base + 8), strip)
        strip = jnp.where((lane >= base + 16) & (lane < base + 24), roll(x, base + 24), strip)
    return strip


def pack_strips(strips, even):
    lane = lanes() % 32
    east = jnp.zeros((STRIP_SPAN, 128), F32)
    west = jnp.zeros((STRIP_SPAN, 128), F32)
    for r in range(4):
        here = (lane >= 8 * r) & (lane < 8 * r + 8)
        east = jnp.where(here, roll(strips[r], 8 * r - 16), east)
        west = jnp.where(here, roll(strips[r], 8 * r - 8), west)
    return jnp.where(even, east, west), jnp.where(even, west, east)


def pack_kernel(state, winds, diff, main, strip, first, second, *, grid):
    even = lon_even()
    flip = jnp.where(lat_even(), 3, 0)

    def body(t, level):
        strips = [[] for _ in range(3)]
        for p in range(4):
            r = jnp.abs(flip - p)
            source = pl.ds(t * 4 * STRIP_SPAN + r, STRIP_SPAN, stride=4)
            row = [state[v, source, :] for v in range(VARS)] + [winds[v, source, :] for v in range(2)]
            row.append(jnp.broadcast_to(diff[pl.ds(r, 1), :], (STRIP_SPAN, 128)))
            for v in range(11):
                main[p, v, level, :] = row[v]
            for b in range(3):
                s = own_strip(lambda g: row[4 * b + g], 4 if b < 2 else 3)
                strip[p, b, level, :] = s
                strips[b].append(s)
        for b in range(3):
            first[b, level, :], second[b, level, :] = pack_strips(strips[b], even)

    level_tiles(LEV // STRIP_SPAN // grid, body, STRIP_SPAN)


def pack(state, winds, diff, grid=2):
    shapes = [(4, 11, LEV, 128), (4, 3, LEV, 128), (3, LEV, 128), (3, LEV, 128)]
    return pl.pallas_call(
        partial(pack_kernel, grid=grid),
        grid=(grid,),
        in_specs=[tiled(grid, 8, 256, 128), tiled(grid, 2, 256, 128), whole((4, 128))],
        out_specs=[tiled(grid, *s) for s in shapes],
        out_shape=[struct(*s) for s in shapes],
        compiler_params=params(16),
        name="pack",
    )(*in_hbm(state, winds), diff)


def complete_kernel(strip, first, second, *outs):
    even = lon_even()
    blocks = strip.shape[1]
    split = blocks // len(outs)

    def body(t, level):
        lane = lax.broadcasted_iota(I32, (SPAN, 128), 1) % 32
        for b in range(blocks):
            one, two = first[b, level, :], second[b, level, :]
            east = jnp.where(even, one, two)
            west = jnp.where(even, two, one)
            for r in range(4):
                full = jnp.where(lane < 8, roll(west, -8 * r), strip[r, b, level, :])
                outs[b // split][r, b % split, level, :] = jnp.where(lane >= 24, roll(east, 24 - 8 * r), full)

    level_tiles(LEV // SPAN, body, SPAN)


def complete(strip, first, second, parts):
    split = strip.shape[1] // parts
    return pl.pallas_call(
        complete_kernel,
        in_specs=[VMEM_SPEC] * 3,
        out_specs=[VMEM_SPEC] * parts,
        out_shape=[struct(4, split, LEV, 128)] * parts,
        compiler_params=params(4),
        name="complete",
    )(strip, first, second)


def coefficient_kernel(own, r0, r1, sown, s0, s1, out, work, *, adjoint):
    lat = lax.axis_index("lat")
    flipped = lat % 2 == 0
    open_side = jnp.where((lat > 0) & (lat < lax.axis_size("lat") - 1), 1.0, 0.0).astype(F32)

    def fetch(tile, intra, inter, i, v, level):
        if i < 4:
            return intra[3 - i, v, level, :]
        if i < 8:
            return tile[i - 4, v, level, :]
        return inter[11 - i, v, level, :]

    def body(t, level):
        lane = lax.broadcasted_iota(I32, (SPAN, 128), 1)
        after = [None, None]
        for i in reversed(range(12)):
            packed = fetch(sown, s0, s1, i, 2, level)
            spread = []
            for g in range(3):
                one = jnp.where(lane < 32, roll(packed, -32 * g), 0.0)
                one = one + roll(one, 32)
                spread.append(one + roll(one, 64))
            plain = [fetch(own, r0, r1, i, VARS + v, level) for v in range(3)]
            for n, (w0, w1, dd) in enumerate((plain, spread)):
                a, b = w0 * 0.5 + dd, w0 * 0.5 - dd
                c, d = w1 * 0.5 + dd, w1 * 0.5 - dd
                a_west, b_west = roll(a, 1), roll(b, 1)
                if n == 0:
                    rim = roll(spread[0], 121) * 0.5
                    rim_diff = roll(spread[2], 121)
                    a_west = jnp.where(lane == 0, rim + rim_diff, a_west)
                    b_west = jnp.where(lane == 0, rim - rim_diff, b_west)
                zero = jnp.zeros_like(c)
                below = after[n] or (zero, zero)
                u = jnp.where(flipped, -below[1], c)
                w = jnp.where(flipped, -below[0], d)
                after[n] = (c, d)
                values = (a, -b_west, u) if adjoint else (-b, a_west, -w)
                for m, value in enumerate((1.0 - a + b_west - u, *values, u, w)):
                    work[i, n, m] = value
        for i in range(1, 12):
            for n in range(2):
                u_before, w_before = work[i - 1, n, 4], work[i - 1, n, 5]
                values = [work[i, n, m] for m in range(4)] + [-w_before if adjoint else u_before]
                values[0] = values[0] + w_before
                for m, value in enumerate(values):
                    out[i, 5 * n + m, level, :] = value * open_side if i >= 8 else value

    level_tiles(LEV // SPAN, body, SPAN)


def coefficients(tile, strips, adjoint):
    return pl.pallas_call(
        partial(coefficient_kernel, adjoint=adjoint),
        in_specs=[VMEM_SPEC] * 6,
        out_specs=VMEM_SPEC,
        out_shape=struct(12, 10, LEV, 128),
        scratch_shapes=[pltpu.VMEM((12, 2, 6, SPAN, 128), F32)],
        compiler_params=params(8),
        name="coefficients_adjoint" if adjoint else "coefficients",
    )(*tile, *strips)


def advect_kernel(*refs, steps, apart, result, addend):
    refs = list(refs)
    steps = refs.pop(0)[0] if steps is None else steps
    own, r0, r1 = refs[:3]
    refs = refs[3:]
    strips = ()
    if apart:
        strips, refs = refs[:3], refs[3:]
    coef = refs.pop(0)
    if addend:
        add_main, add_strip = refs[:2]
        refs = refs[2:]
    out, *work = refs
    flip = jnp.where(lat_even(), 3, 0)
    width = r0.shape[0]

    def place(target, sources, offset, count):
        tile, intra, inter = sources

        def halo(j, carry):
            target[3 - j, offset : offset + count] = intra[j, 0:count]
            target[8 + j, offset : offset + count] = inter[width - 1 - j, 0:count]
            return carry

        def inside(j, carry):
            target[4 + j, offset : offset + count] = tile[j, 0:count]
            return carry

        lax.fori_loop(0, width, halo, 0)
        lax.fori_loop(0, 4, inside, 0)

    def start(target):
        if apart:
            place(target, (own, r0, r1), 0, VARS)
            place(target, strips, VARS, 2)
        else:
            place(target, (own, r0, r1), 0, VARS + 2)

    def when(condition, run):
        if isinstance(condition, bool):
            if condition:
                run()
        else:
            pl.when(condition)(run)

    for n in range(2):
        when(steps % 2 != n, partial(start, work[n]))
    lane = lax.broadcasted_iota(I32, (LEV, 128), 1)

    def row(now, i, last, store):
        def stencil(n, v, f, east, west):
            value = coef[i, n] * f
            value = value + coef[i, n + 1] * east
            value = value + coef[i, n + 2] * west
            value = value + coef[i, n + 3] * now[i + 1, v]
            return value + coef[i, n + 4] * now[i - 1, v]

        for b in range(2):
            f = now[i, VARS + b]
            ends = jnp.where(lane % 32 == 25, roll(f, 18), f)
            if not last or result == "both":
                store(VARS + b, stencil(5, VARS + b, f, roll(f, -1), roll(f, 1)))
            for g in range(4):
                v = 4 * b + g
                f = now[i, v]
                rim = roll(ends, 103 - 32 * g)
                east = jnp.where(lane == 127, rim, roll(f, -1))
                west = jnp.where(lane == 0, rim, roll(f, 1))
                store(v, stencil(0, v, f, east, west))

    def step(reach):
        def one(i, carry):
            def store(v, value):
                work[1 - reach % 2][i, v] = value

            row(work[reach % 2], i, False, store)
            return carry

        lax.fori_loop(4 - reach, 8 + reach, one, 0)

    for reach in (3, 2, 1):
        when(steps > reach, partial(step, reach))

    def final(r, carry):
        def store(v, value):
            if addend:
                value = value + (add_main[r, v] if v < VARS else add_strip[r, v - VARS])
            if result == "native":
                out[v, pl.ds(jnp.abs(flip - r), LEV, stride=4), :] = value
            else:
                out[r, v] = value

        row(work[0], 4 + r, True, store)
        return carry

    lax.fori_loop(0, 4, final, 0)


def advect(steps, tile, strips, coef, result, addend=None):
    args = [*tile]
    if strips is not None:
        args += strips
    args.append(coef)
    if addend is not None:
        args += addend
    if result == "native":
        shape = (8, 256, 128)
    else:
        shape = (4, 10 if result == "both" else 8, LEV, 128)
    static = isinstance(steps, int)
    return pl.pallas_call(
        partial(
            advect_kernel,
            steps=steps if static else None,
            apart=strips is not None,
            result=result,
            addend=addend is not None,
        ),
        in_specs=([] if static else [SMEM_SPEC]) + [VMEM_SPEC] * len(args),
        out_specs=VMEM_SPEC,
        out_shape=struct(*shape),
        scratch_shapes=[pltpu.VMEM((12, 10, LEV, 128), F32)] * 2,
        compiler_params=params(16),
        name="advect_" + result,
    )(*([] if static else [steps]), *args)


def split(x):
    high = x.astype(BF16)
    return high, (x - high.astype(F32)).astype(BF16)


def dot(x, y, dims):
    return lax.dot_general(x, y, ((dims[:1], dims[1:]), ((), ())), preferred_element_type=F32)


def dot3(x, y, dims):
    return dot(x[0], y[0], dims) + (dot(x[0], y[1], dims) + dot(x[1], y[0], dims))


def relayout_kernel(observed, sent):
    homes = observed.shape[3]
    for k in range(2):
        for q in range(3):
            for c in range(4):
                sent[pl.ds(12 * k + 4 * q + c, homes, stride=24), :] = observed[k, 0, q, :, pl.ds(128 * c, 128)]


def relayout(observed):
    turned = jnp.transpose(observed, (0, 1, 3, 2, 4))
    homes = turned.shape[3]
    sent = pl.pallas_call(
        relayout_kernel,
        grid=(1,),
        in_specs=[whole(turned.shape)],
        out_specs=whole((homes * 24, 128)),
        out_shape=struct(homes * 24, 128),
        compiler_params=params(16),
        name="relayout",
    )(*in_hbm(turned))
    return sent.reshape(homes, 24, 128)


PADDED = 640


def column_of(row):
    square = (SND, SND)
    here = lax.broadcasted_iota(I32, square, 0) == lax.broadcasted_iota(I32, square, 1)
    return jnp.sum(jnp.where(here, jnp.broadcast_to(row, square), 0), axis=1, keepdims=True)


def load_table(table, high, low):
    count = table.shape[0]
    full = count // 16 * 16
    high[pl.ds(0, full), :], low[pl.ds(0, full), :] = split(table[pl.ds(0, full), :])
    rest = jnp.zeros((PADDED - full, table.shape[1]), F32)
    if count > full:
        zeros = jnp.zeros((PADDED - count, table.shape[1]), F32)
        rest = jnp.concatenate([table[pl.ds(full, count - full), :], zeros], axis=0)
    high[pl.ds(full, PADDED - full), :], low[pl.ds(full, PADDED - full), :] = split(rest)


def observe_kernel(cells, owners, channels, weight, field, *refs, slot):
    if slot == 0:
        hbm, refs = refs[:3], refs[3:]
        (out, strip, first, second, *tables), refs = refs[:8], refs[8:]
        (absorb_table, emit_table, fetched), sems = refs[:3], refs[3]
        targets = (absorb_table, emit_table, fetched)
    else:
        tables, hbm, before, refs = refs[:4], refs[4:5], refs[5:8], refs[8:]
        (out, strip, first, second), (fetched, sems) = refs[:4], refs[4:]
        targets = (fetched,)
    copies = [
        pltpu.make_async_copy(source, target, sems.at[n])
        for n, (source, target) in enumerate(zip(hbm, targets, strict=True))
    ]
    for copy in copies:
        copy.start()

    flip = jnp.where(lat_even(), 3, 0)
    square = (SND, SND)
    row_id = lax.broadcasted_iota(I32, square, 0)
    lane_id = lax.broadcasted_iota(I32, square, 1)
    entry = lax.broadcasted_iota(I32, (PADDED, channels.shape[1]), 0)
    listed = (entry == channels[...]).astype(F32).astype(BF16)
    times = dot(jnp.ones((8, channels.shape[1]), BF16), listed, (1, 1))[0:1]
    cell = column_of(cells[slot : slot + 1, :])
    owner_row = owners[slot : slot + 1, :]
    owner = column_of(owner_row)
    earlier = (owner == owner_row) & (lane_id < row_id)
    rank = jnp.sum(jnp.where(earlier, 1, 0), axis=1, keepdims=True)
    picks = [(cell == lane_id + 128 * jnp.abs(flip - r)).astype(F32).astype(BF16) for r in range(4)]
    pieces = [jnp.zeros((SND, VARS * LEV), F32)] * 2
    for r in range(4):
        x = split(field[r, 0:VARS].reshape(VARS * LEV, 128))
        pieces = [piece + dot(picks[r], part, (1, 1)) for piece, part in zip(pieces, x, strict=True)]
    column = [piece.astype(BF16) for piece in pieces]
    if slot == 0:
        for n, table in enumerate((absorb_table, emit_table)):
            copies[n].wait()
            load_table(table, tables[2 * n], tables[2 * n + 1])
    absorb = (tables[0][...], tables[1][...])
    emission = (tables[2][...], tables[3][...])
    optical = dot3(column, absorb, (1, 1))
    bright = dot3(column, emission, (1, 1))
    decay = jnp.exp(-jnp.abs(optical))
    inverse = 1.0 / (1.0 + decay)
    rest = decay * inverse
    positive = optical >= 0
    passing = jnp.where(positive, rest, inverse)
    opaque = jnp.where(positive, inverse, rest)
    choices = [((owner == lane_id) & (rank == q)).astype(F32).astype(BF16) for q in range(3)]
    copies[-1].wait()
    parts = []
    for c in range(4):
        part = [jnp.zeros(square, F32)] * 2
        for q in range(3):
            seen = split(fetched[pl.ds(12 * slot + 4 * q + c, SND, stride=24), :])
            part = [p + dot(choices[q], x, (1, 0)) for p, x in zip(part, seen, strict=True)]
        parts.append(part)
    wanted = [jnp.concatenate([part[n] for part in parts], axis=1).astype(BF16) for n in range(2)]
    totals = dot(wanted[0], listed, (1, 1)) + dot(wanted[1], listed, (1, 1))
    evolved = passing * bright
    departure = weight[...] * (times * evolved - totals)
    to_bright = departure * passing
    to_optical = -(departure * evolved * opaque)
    column = dot3(split(to_optical), absorb, (1, 0)) + dot3(split(to_bright), emission, (1, 0))
    ch, cl = split(column)
    for r in range(4):
        placed = dot(ch, picks[r], (0, 0)) + dot(cl, picks[r], (0, 0))
        out[r] = placed.reshape(VARS, LEV, 128)

    even = lon_even()
    if slot == 1:
        strip[:, 2:4] = before[0][...]
        first[2:4] = before[1][...]
        second[2:4] = before[2][...]

    def strips_of(t, level):
        for b in range(2):
            strips = []
            for r in range(4):
                s = own_strip(lambda g: out[r, 4 * b + g, level, :], 4)
                strip[r, b, level, :] = s
                strips.append(s)
            first[b, level, :], second[b, level, :] = pack_strips(strips, even)

    level_tiles(LEV // STRIP_SPAN, strips_of, STRIP_SPAN)


def observe(slot, small, field, tables, fetched, before):
    count = 2 if slot == 0 else 4
    shapes = [struct(4, 8, LEV, 128), struct(4, count, LEV, 128)] + [struct(count, LEV, 128)] * 2
    moved = [fetched]
    if slot == 0:
        moved = [*tables, fetched]
        tables = []
        shapes += [struct(PADDED, VARS * LEV, dtype=BF16)] * 4
    hbm_spec = pl.BlockSpec(memory_space=pltpu.HBM)
    return pl.pallas_call(
        partial(observe_kernel, slot=slot),
        in_specs=[VMEM_SPEC] * (len(small) + 1 + len(tables)) + [hbm_spec] * len(moved) + [VMEM_SPEC] * len(before),
        out_specs=[VMEM_SPEC] * len(shapes),
        out_shape=shapes,
        scratch_shapes=[pltpu.VMEM(x.shape, F32) for x in moved] + [pltpu.SemaphoreType.DMA((len(moved),))],
        compiler_params=params(16),
        name="observe",
    )(*small, field, *tables, *in_hbm(*moved), *before)


def swap(x, axis, parity, wrap):
    devices = lax.axis_size(axis)
    pairs = []
    for i in range(parity, devices, 2):
        if i + 1 < devices or wrap:
            j = (i + 1) % devices
            pairs += [(i, j), (j, i)]
    return lax.ppermute(x, axis, pairs)


def lat_swap(x, width=4):
    beyond = swap(x[4 - width :], "lat", 1, False)
    return swap(x[:width], "lat", 0, False), beyond


def lon_swap(first, second):
    beyond = swap(second, "lon", 1, True)
    return swap(first, "lon", 0, True), beyond


def per_device(
    state, winds, diffusivity, sounding_cell, sounding_owner, step_counts, channel_list, absorb_table, emit_table,
    obs_weight, observed,
):
    def by_steps(slot, run):
        branches = [partial(run, width) for width in range(1, MAXSTEP + 1)]
        return lax.switch(step_counts[slot] - 1, branches)

    main, strip, first, second = pack(state.reshape(8, 256, 128), winds.reshape(2, 256, 128), diffusivity)
    received = lon_swap(first, second)
    halo = lat_swap(main)
    sent, received = lax.optimization_barrier((relayout(observed), received))
    (strip,) = complete(strip, *received, 1)
    fetched = lax.all_to_all(sent, ("lon", "lat"), split_axis=0, concat_axis=0, tiled=True)
    tile, strips = (main, *halo), (strip, *lat_swap(strip))
    onward = coefficients(tile, strips, False)
    both0 = advect(step_counts[:1], tile, strips, onward, "both")
    halo = lat_swap(both0)
    halo_strips, both0 = lax.optimization_barrier((strips, both0))
    backward_coef = coefficients(tile, halo_strips, True)

    extra = PADDED - obs_weight.shape[0]
    padded_weight = jnp.pad(obs_weight, (0, extra))[None, :]
    small = [sounding_cell, sounding_owner[:, :, 0], channel_list[None, :], padded_weight]
    fetched = fetched.reshape(-1, 128)
    g0, *edges, th0, tl0, th1, tl1 = observe(0, small, both0, [absorb_table.T, emit_table.T], fetched, [])
    both0, backward_coef, g0 = lax.optimization_barrier((both0, backward_coef, g0))
    field1 = advect(step_counts[1:], (both0, *halo), None, onward, "main")
    g1, strip, first, second = observe(1, small, field1, [th0, tl0, th1, tl1], fetched, edges)

    def backward(width):
        received = lon_swap(first, second)
        halo = lat_swap(g1, width)
        strips1, strips0 = complete(strip, *received, 2)
        halo_strips = lat_swap(strips1, width)
        return advect(width, (g1, *halo), (strips1, *halo_strips), backward_coef, "both", (g0, strips0))

    both = by_steps(1, backward)

    def last(width):
        return advect(width, (both, *lat_swap(both, width)), None, backward_coef, "native")

    result = by_steps(0, last)
    return result.reshape(state.shape)


def solution(mesh):
    return jax.shard_map(
        per_device,
        mesh=mesh,
        in_specs=(
            P(None, None, "lat", "lon"),
            P(None, None, "lat", "lon"),
            P("lat", "lon"),
            P(None, ("lon", "lat")),
            P(None, ("lon", "lat"), None),
            P(),
            P(),
            P(),
            P(),
            P(),
            P(None, ("lon", "lat"), None, None, None),
        ),
        out_specs=P(None, None, "lat", "lon"),
        check_vma=False,
    )
```

```python
from functools import partial

import jax
import jax.numpy as jnp
from jax import lax
from jax.experimental import pallas as pl
from jax.experimental.pallas import tpu as pltpu
from jax.sharding import PartitionSpec as P

F32 = jnp.float32
BF16 = jnp.bfloat16
I32 = jnp.int32
VARS = 8
SPAN = 32
STRIP_SPAN = 16
LEV = 64
MAXSTEP = 4
SND = 128


def struct(*shape, dtype=F32):
    return jax.ShapeDtypeStruct(shape, dtype)


def tiled(grid, *shape):
    zeros = (0,) * (len(shape) - 2)
    return pl.BlockSpec((*shape[:-2], shape[-2] // grid, shape[-1]), lambda t: (*zeros, t, 0))


def whole(shape):
    return pl.BlockSpec(shape, lambda *_: (0,) * len(shape))


VMEM_SPEC = pl.BlockSpec(memory_space=pltpu.VMEM)
SMEM_SPEC = pl.BlockSpec(memory_space=pltpu.SMEM)


def params(mebibytes):
    return pltpu.CompilerParams(vmem_limit_bytes=mebibytes * 1024 * 1024)


def in_hbm(*arrays):
    return [pltpu.with_memory_space_constraint(x, pltpu.HBM) for x in arrays]


def lanes():
    return lax.broadcasted_iota(I32, (STRIP_SPAN, 128), 1)


def roll(x, shift):
    shift = shift % 128
    return x if shift == 0 else pltpu.roll(x, shift, 1)


def level_tiles(count, body, span=8):
    def step(t, carry):
        body(t, pl.ds(pl.multiple_of(t * span, span), span))
        return carry

    lax.fori_loop(0, count, step, 0)


def lon_even():
    return lax.axis_index("lon") % 2 == 0


def lat_even():
    return lax.axis_index("lat") % 2 == 0


def own_strip(load, count):
    lane = lanes()
    strip = jnp.zeros((STRIP_SPAN, 128), F32)
    for g in range(count):
        x = load(g)
        base = 32 * g
        strip = jnp.where((lane >= base + 8) & (lane < base + 16), roll(x, base + 8), strip)
        strip = jnp.where((lane >= base + 16) & (lane < base + 24), roll(x, base + 24), strip)
    return strip


def pack_strips(strips, even):
    lane = lanes() % 32
    east = jnp.zeros((STRIP_SPAN, 128), F32)
    west = jnp.zeros((STRIP_SPAN, 128), F32)
    for r in range(4):
        here = (lane >= 8 * r) & (lane < 8 * r + 8)
        east = jnp.where(here, roll(strips[r], 8 * r - 16), east)
        west = jnp.where(here, roll(strips[r], 8 * r - 8), west)
    return jnp.where(even, east, west), jnp.where(even, west, east)


def pack_kernel(state, winds, diff, main, strip, first, second, *, grid):
    even = lon_even()
    flip = jnp.where(lat_even(), 3, 0)

    def body(t, level):
        strips = [[] for _ in range(3)]
        for p in range(4):
            r = jnp.abs(flip - p)
            source = pl.ds(t * 4 * STRIP_SPAN + r, STRIP_SPAN, stride=4)
            row = [state[v, source, :] for v in range(VARS)] + [winds[v, source, :] for v in range(2)]
            row.append(jnp.broadcast_to(diff[pl.ds(r, 1), :], (STRIP_SPAN, 128)))
            for v in range(11):
                main[p, v, level, :] = row[v]
            for b in range(3):
                s = own_strip(lambda g: row[4 * b + g], 4 if b < 2 else 3)
                strip[p, b, level, :] = s
                strips[b].append(s)
        for b in range(3):
            first[b, level, :], second[b, level, :] = pack_strips(strips[b], even)

    level_tiles(LEV // STRIP_SPAN // grid, body, STRIP_SPAN)


def pack(state, winds, diff, grid=2):
    shapes = [(4, 11, LEV, 128), (4, 3, LEV, 128), (3, LEV, 128), (3, LEV, 128)]
    return pl.pallas_call(
        partial(pack_kernel, grid=grid),
        grid=(grid,),
        in_specs=[tiled(grid, 8, 256, 128), tiled(grid, 2, 256, 128), whole((4, 128))],
        out_specs=[tiled(grid, *s) for s in shapes],
        out_shape=[struct(*s) for s in shapes],
        compiler_params=params(16),
        name="pack",
    )(*in_hbm(state, winds), diff)


def complete_kernel(strip, first, second, *outs):
    even = lon_even()
    blocks = strip.shape[1]
    split = blocks // len(outs)

    def body(t, level):
        lane = lax.broadcasted_iota(I32, (SPAN, 128), 1) % 32
        for b in range(blocks):
            one, two = first[b, level, :], second[b, level, :]
            east = jnp.where(even, one, two)
            west = jnp.where(even, two, one)
            for r in range(4):
                full = jnp.where(lane < 8, roll(west, -8 * r), strip[r, b, level, :])
                outs[b // split][r, b % split, level, :] = jnp.where(lane >= 24, roll(east, 24 - 8 * r), full)

    level_tiles(LEV // SPAN, body, SPAN)


def complete(strip, first, second, parts):
    split = strip.shape[1] // parts
    return pl.pallas_call(
        complete_kernel,
        in_specs=[VMEM_SPEC] * 3,
        out_specs=[VMEM_SPEC] * parts,
        out_shape=[struct(4, split, LEV, 128)] * parts,
        compiler_params=params(4),
        name="complete",
    )(strip, first, second)


def open_to_next_chip():
    lat = lax.axis_index("lat")
    return jnp.where((lat > 0) & (lat < lax.axis_size("lat") - 1), 1.0, 0.0).astype(F32)


def each_row(first, last, body):
    def step(i, carry):
        body(i)
        return carry

    lax.fori_loop(first, last, step, 0)


def coefficient_kernel(own, r0, r1, sown, s0, s1, out, raw):
    flipped = lat_even()
    open_side = open_to_next_chip()
    lane = lax.broadcasted_iota(I32, (LEV, 128), 1)

    def fill(i, main, strip):
        packed = strip[2]
        spread = []
        for g in range(3):
            one = jnp.where(lane < 32, roll(packed, -32 * g), 0.0)
            one = one + roll(one, 32)
            spread.append(one + roll(one, 64))
        plain = [main[VARS], main[VARS + 1], main[VARS + 2]]
        for n, (w0, w1, dd) in enumerate((plain, spread)):
            half = w0 * 0.5
            half_west, dd_west = roll(half, 1), roll(dd, 1)
            if n == 0:
                half_west = jnp.where(lane == 0, roll(spread[0], 121) * 0.5, half_west)
                dd_west = jnp.where(lane == 0, roll(spread[2], 121), dd_west)
            a, b = half + dd, half - dd
            a_west, b_west = half_west + dd_west, half_west - dd_west
            half = w1 * 0.5
            for m, value in enumerate((a, b_west, half + dd, half - dd)):
                raw[i, 4 * n + m] = value
            out[i, 5 * n] = 1.0 - a + b_west
            out[i, 5 * n + 1] = -b
            out[i, 5 * n + 2] = a_west

    each_row(0, 4, lambda j: fill(3 - j, r0.at[j], s0.at[j]))
    each_row(0, 4, lambda j: fill(4 + j, own.at[j], sown.at[j]))
    each_row(0, 4, lambda j: fill(8 + j, r1.at[3 - j], s1.at[3 - j]))

    def interface(i):
        for n in range(2):
            c, d = raw[i, 4 * n + 2], raw[i, 4 * n + 3]
            c_next, d_next = raw[i + 1, 4 * n + 2], raw[i + 1, 4 * n + 3]
            raw[i, 4 * n + 2] = jnp.where(flipped, -d_next, c)
            raw[i, 4 * n + 3] = jnp.where(flipped, -c_next, d)

    each_row(0, 11, interface)

    def combine(i):
        scale = jnp.where(i >= 8, open_side, 1.0)
        for n in range(2):
            u, w = raw[i, 4 * n + 2], raw[i, 4 * n + 3]
            u_before, w_before = raw[i - 1, 4 * n + 2], raw[i - 1, 4 * n + 3]
            out[i, 5 * n] = (out[i, 5 * n] - u + w_before) * scale
            out[i, 5 * n + 1] = out[i, 5 * n + 1] * scale
            out[i, 5 * n + 2] = out[i, 5 * n + 2] * scale
            out[i, 5 * n + 3] = -w * scale
            out[i, 5 * n + 4] = u_before * scale

    each_row(1, 11, combine)


def coefficients(tile, strips):
    return pl.pallas_call(
        coefficient_kernel,
        in_specs=[VMEM_SPEC] * 6,
        out_specs=[VMEM_SPEC] * 2,
        out_shape=[struct(12, 10, LEV, 128), struct(12, 8, LEV, 128)],
        compiler_params=params(4),
        name="coefficients",
    )(*tile, *strips)


def adjoint_kernel(forward, raw, out):
    open_side = open_to_next_chip()

    def combine(i):
        scale = jnp.where(i >= 8, open_side, 1.0)
        for n in range(2):
            out[i, 5 * n] = forward[i, 5 * n]
            out[i, 5 * n + 1] = raw[i, 4 * n] * scale
            out[i, 5 * n + 2] = -raw[i, 4 * n + 1] * scale
            out[i, 5 * n + 3] = raw[i, 4 * n + 2] * scale
            out[i, 5 * n + 4] = -raw[i - 1, 4 * n + 3] * scale

    each_row(1, 11, combine)


def adjoint_coefficients(forward, raw):
    return pl.pallas_call(
        adjoint_kernel,
        in_specs=[VMEM_SPEC] * 2,
        out_specs=VMEM_SPEC,
        out_shape=struct(12, 10, LEV, 128),
        compiler_params=params(4),
        name="adjoint_coefficients",
    )(forward, raw)


def advect_kernel(*refs, steps, apart, result, addend):
    refs = list(refs)
    steps = refs.pop(0)[0] if steps is None else steps
    own, r0, r1 = refs[:3]
    refs = refs[3:]
    strips = ()
    if apart:
        strips, refs = refs[:3], refs[3:]
    coef = refs.pop(0)
    if addend:
        add_main, add_strip = refs[:2]
        refs = refs[2:]
    out, *work, shift = refs
    source = lax.broadcasted_iota(I32, (256, 256), 0) % 128
    target = lax.broadcasted_iota(I32, (256, 256), 1)
    chosen = jnp.where(target < 128, target + 1, target + 127) % 128
    shift[...] = (source == chosen).astype(F32).astype(BF16)
    flip = jnp.where(lat_even(), 3, 0)
    width = r0.shape[0]

    def place(target, sources, offset, count):
        tile, intra, inter = sources

        def halo(j, carry):
            target[3 - j, offset : offset + count] = intra[j, 0:count]
            target[8 + j, offset : offset + count] = inter[width - 1 - j, 0:count]
            return carry

        def inside(j, carry):
            target[4 + j, offset : offset + count] = tile[j, 0:count]
            return carry

        lax.fori_loop(0, width, halo, 0)
        lax.fori_loop(0, 4, inside, 0)

    def start(target):
        if apart:
            place(target, (own, r0, r1), 0, VARS)
            place(target, strips, VARS, 2)
        else:
            place(target, (own, r0, r1), 0, VARS + 2)

    def when(condition, run):
        if isinstance(condition, bool):
            if condition:
                run()
        else:
            pl.when(condition)(run)

    for n in range(2):
        when(steps % 2 != n, partial(start, work[n]))
    lane = lax.broadcasted_iota(I32, (LEV, 128), 1)

    def row(now, i, last, store):
        def stencil(n, v, f, east, west):
            value = coef[i, n] * f
            value = value + coef[i, n + 1] * east
            value = value + coef[i, n + 2] * west
            value = value + coef[i, n + 3] * now[i + 1, v]
            return value + coef[i, n + 4] * now[i - 1, v]

        wanted = VARS + (0 if last and result != "both" else 2)
        halves = split(now[i, 0:wanted].reshape(wanted * LEV, 128))
        moved = dot(jnp.concatenate(halves, axis=1), shift[...], (1, 0))
        moved = moved.reshape(wanted, LEV, 256)
        for b in range(2):
            f = now[i, VARS + b]
            ends = jnp.where(lane % 32 == 25, roll(f, 18), f)
            for v in (VARS + b, *range(4 * b, 4 * b + 4)):
                if v >= wanted:
                    continue
                f = now[i, v]
                east, west = moved[v, :, :128], moved[v, :, 128:]
                if v < VARS:
                    rim = roll(ends, 103 - 32 * (v % 4))
                    east = jnp.where(lane == 127, rim, east)
                    west = jnp.where(lane == 0, rim, west)
                store(v, stencil(5 if v >= VARS else 0, v, f, east, west))

    def step(reach):
        def one(i, carry):
            def store(v, value):
                work[1 - reach % 2][i, v] = value

            row(work[reach % 2], i, False, store)
            return carry

        lax.fori_loop(4 - reach, 8 + reach, one, 0)

    for reach in (3, 2, 1):
        when(steps > reach, partial(step, reach))

    def final(r, carry):
        def store(v, value):
            if addend:
                value = value + (add_main[r, v] if v < VARS else add_strip[r, v - VARS])
            if result == "native":
                out[v, pl.ds(jnp.abs(flip - r), LEV, stride=4), :] = value
            else:
                out[r, v] = value

        row(work[0], 4 + r, True, store)
        return carry

    lax.fori_loop(0, 4, final, 0)


def advect(steps, tile, strips, coef, result, addend=None):
    args = [*tile]
    if strips is not None:
        args += strips
    args.append(coef)
    if addend is not None:
        args += addend
    if result == "native":
        shape = (8, 256, 128)
    else:
        shape = (4, 10 if result == "both" else 8, LEV, 128)
    static = isinstance(steps, int)
    return pl.pallas_call(
        partial(
            advect_kernel,
            steps=steps if static else None,
            apart=strips is not None,
            result=result,
            addend=addend is not None,
        ),
        in_specs=([] if static else [SMEM_SPEC]) + [VMEM_SPEC] * len(args),
        out_specs=VMEM_SPEC,
        out_shape=struct(*shape),
        scratch_shapes=[pltpu.VMEM((12, 10, LEV, 128), F32)] * 2 + [pltpu.VMEM((256, 256), BF16)],
        compiler_params=params(14),
        name="advect_" + result,
    )(*([] if static else [steps]), *args)


def split(x):
    high = x.astype(BF16)
    return high, (x - high.astype(F32)).astype(BF16)


def dot(x, y, dims):
    return lax.dot_general(x, y, ((dims[:1], dims[1:]), ((), ())), preferred_element_type=F32)


def dot3(x, y, dims):
    return dot(x[0], y[0], dims) + (dot(x[0], y[1], dims) + dot(x[1], y[0], dims))


def relayout_kernel(observed, sent):
    homes = observed.shape[3]
    for k in range(2):
        for q in range(3):
            for c in range(4):
                sent[pl.ds(12 * k + 4 * q + c, homes, stride=24), :] = observed[k, 0, q, :, pl.ds(128 * c, 128)]


def relayout(observed):
    turned = jnp.transpose(observed, (0, 1, 3, 2, 4))
    homes = turned.shape[3]
    sent = pl.pallas_call(
        relayout_kernel,
        grid=(1,),
        in_specs=[whole(turned.shape)],
        out_specs=whole((homes * 24, 128)),
        out_shape=struct(homes * 24, 128),
        compiler_params=params(16),
        name="relayout",
    )(*in_hbm(turned))
    return sent.reshape(homes, 24, 128)


PADDED = 640


def column_of(row):
    square = (SND, SND)
    here = lax.broadcasted_iota(I32, square, 0) == lax.broadcasted_iota(I32, square, 1)
    return jnp.sum(jnp.where(here, jnp.broadcast_to(row, square), 0), axis=1, keepdims=True)


def load_table(table, high, low):
    count = table.shape[0]
    full = count // 16 * 16
    high[pl.ds(0, full), :], low[pl.ds(0, full), :] = split(table[pl.ds(0, full), :])
    rest = jnp.zeros((PADDED - full, table.shape[1]), F32)
    if count > full:
        zeros = jnp.zeros((PADDED - count, table.shape[1]), F32)
        rest = jnp.concatenate([table[pl.ds(full, count - full), :], zeros], axis=0)
    high[pl.ds(full, PADDED - full), :], low[pl.ds(full, PADDED - full), :] = split(rest)


def observe_kernel(cells, owners, channels, weight, field, *refs, slot):
    if slot == 0:
        hbm, refs = refs[:3], refs[3:]
        (out, strip, first, second, *tables), refs = refs[:8], refs[8:]
        (absorb_table, emit_table, fetched), sems = refs[:3], refs[3]
        targets = (absorb_table, emit_table, fetched)
    else:
        tables, hbm, before, refs = refs[:4], refs[4:5], refs[5:8], refs[8:]
        (out, strip, first, second), (fetched, sems) = refs[:4], refs[4:]
        targets = (fetched,)
    copies = [
        pltpu.make_async_copy(source, target, sems.at[n])
        for n, (source, target) in enumerate(zip(hbm, targets, strict=True))
    ]
    for copy in copies:
        copy.start()

    flip = jnp.where(lat_even(), 3, 0)
    square = (SND, SND)
    row_id = lax.broadcasted_iota(I32, square, 0)
    lane_id = lax.broadcasted_iota(I32, square, 1)
    entry = lax.broadcasted_iota(I32, (PADDED, channels.shape[1]), 0)
    listed = (entry == channels[...]).astype(F32).astype(BF16)
    times = dot(jnp.ones((8, channels.shape[1]), BF16), listed, (1, 1))[0:1]
    cell = column_of(cells[slot : slot + 1, :])
    owner_row = owners[slot : slot + 1, :]
    owner = column_of(owner_row)
    earlier = (owner == owner_row) & (lane_id < row_id)
    rank = jnp.sum(jnp.where(earlier, 1, 0), axis=1, keepdims=True)
    picks = [(cell == lane_id + 128 * jnp.abs(flip - r)).astype(F32).astype(BF16) for r in range(4)]
    pieces = [jnp.zeros((SND, VARS * LEV), F32)] * 2
    for r in range(4):
        x = split(field[r, 0:VARS].reshape(VARS * LEV, 128))
        pieces = [piece + dot(picks[r], part, (1, 1)) for piece, part in zip(pieces, x, strict=True)]
    column = [piece.astype(BF16) for piece in pieces]
    if slot == 0:
        for n, table in enumerate((absorb_table, emit_table)):
            copies[n].wait()
            load_table(table, tables[2 * n], tables[2 * n + 1])
    absorb = (tables[0][...], tables[1][...])
    emission = (tables[2][...], tables[3][...])
    optical = dot3(column, absorb, (1, 1))
    bright = dot3(column, emission, (1, 1))
    decay = jnp.exp(-jnp.abs(optical))
    inverse = 1.0 / (1.0 + decay)
    rest = decay * inverse
    positive = optical >= 0
    passing = jnp.where(positive, rest, inverse)
    opaque = jnp.where(positive, inverse, rest)
    choices = [((owner == lane_id) & (rank == q)).astype(F32).astype(BF16) for q in range(3)]
    copies[-1].wait()
    parts = []
    for c in range(4):
        part = [jnp.zeros(square, F32)] * 2
        for q in range(3):
            seen = split(fetched[pl.ds(12 * slot + 4 * q + c, SND, stride=24), :])
            part = [p + dot(choices[q], x, (1, 0)) for p, x in zip(part, seen, strict=True)]
        parts.append(part)
    wanted = [jnp.concatenate([part[n] for part in parts], axis=1).astype(BF16) for n in range(2)]
    totals = dot(wanted[0], listed, (1, 1)) + dot(wanted[1], listed, (1, 1))
    evolved = passing * bright
    departure = weight[...] * (times * evolved - totals)
    to_bright = departure * passing
    to_optical = -(departure * evolved * opaque)
    column = dot3(split(to_optical), absorb, (1, 0)) + dot3(split(to_bright), emission, (1, 0))
    ch, cl = split(column)
    for r in range(4):
        placed = dot(ch, picks[r], (0, 0)) + dot(cl, picks[r], (0, 0))
        out[r] = placed.reshape(VARS, LEV, 128)

    even = lon_even()
    if slot == 1:
        strip[:, 2:4] = before[0][...]
        first[2:4] = before[1][...]
        second[2:4] = before[2][...]

    def strips_of(t, level):
        for b in range(2):
            strips = []
            for r in range(4):
                s = own_strip(lambda g: out[r, 4 * b + g, level, :], 4)
                strip[r, b, level, :] = s
                strips.append(s)
            first[b, level, :], second[b, level, :] = pack_strips(strips, even)

    level_tiles(LEV // STRIP_SPAN, strips_of, STRIP_SPAN)


def observe(slot, small, field, tables, fetched, before):
    count = 2 if slot == 0 else 4
    shapes = [struct(4, 8, LEV, 128), struct(4, count, LEV, 128)] + [struct(count, LEV, 128)] * 2
    moved = [fetched]
    if slot == 0:
        moved = [*tables, fetched]
        tables = []
        shapes += [struct(PADDED, VARS * LEV, dtype=BF16)] * 4
    hbm_spec = pl.BlockSpec(memory_space=pltpu.HBM)
    return pl.pallas_call(
        partial(observe_kernel, slot=slot),
        in_specs=[VMEM_SPEC] * (len(small) + 1 + len(tables)) + [hbm_spec] * len(moved) + [VMEM_SPEC] * len(before),
        out_specs=[VMEM_SPEC] * len(shapes),
        out_shape=shapes,
        scratch_shapes=[pltpu.VMEM(x.shape, F32) for x in moved] + [pltpu.SemaphoreType.DMA((len(moved),))],
        compiler_params=params(10),
        name="observe",
    )(*small, field, *tables, *in_hbm(*moved), *before)


def swap(x, axis, parity, wrap):
    devices = lax.axis_size(axis)
    pairs = []
    for i in range(parity, devices, 2):
        if i + 1 < devices or wrap:
            j = (i + 1) % devices
            pairs += [(i, j), (j, i)]
    return lax.ppermute(x, axis, pairs)


def lat_swap(x, width=4):
    beyond = swap(x[4 - width :], "lat", 1, False)
    return swap(x[:width], "lat", 0, False), beyond


def lon_swap(first, second):
    beyond = swap(second, "lon", 1, True)
    return swap(first, "lon", 0, True), beyond


def per_device(
    state, winds, diffusivity, sounding_cell, sounding_owner, step_counts, channel_list, absorb_table, emit_table,
    obs_weight, observed,
):
    def by_steps(slot, run):
        branches = [partial(run, width) for width in range(1, MAXSTEP + 1)]
        return lax.switch(step_counts[slot] - 1, branches)

    main, strip, first, second = pack(state.reshape(8, 256, 128), winds.reshape(2, 256, 128), diffusivity)
    received = lon_swap(first, second)
    halo = lat_swap(main)
    sent, received = lax.optimization_barrier((relayout(observed), received))
    (strip,) = complete(strip, *received, 1)
    fetched = lax.all_to_all(sent, ("lon", "lat"), split_axis=0, concat_axis=0, tiled=True)
    tile, strips = (main, *halo), (strip, *lat_swap(strip))
    onward, raw = coefficients(tile, strips)
    both0 = advect(step_counts[:1], tile, strips, onward, "both")
    halo = lat_swap(both0)
    raw, both0 = lax.optimization_barrier((raw, both0))
    backward_coef = adjoint_coefficients(onward, raw)

    extra = PADDED - obs_weight.shape[0]
    padded_weight = jnp.pad(obs_weight, (0, extra))[None, :]
    small = [sounding_cell, sounding_owner[:, :, 0], channel_list[None, :], padded_weight]
    fetched = fetched.reshape(-1, 128)
    g0, *edges, th0, tl0, th1, tl1 = observe(0, small, both0, [absorb_table.T, emit_table.T], fetched, [])
    both0, backward_coef, g0 = lax.optimization_barrier((both0, backward_coef, g0))
    field1 = advect(step_counts[1:], (both0, *halo), None, onward, "main")
    g1, strip, first, second = observe(1, small, field1, [th0, tl0, th1, tl1], fetched, edges)

    def backward(width):
        received = lon_swap(first, second)
        halo = lat_swap(g1, width)
        strips1, strips0 = complete(strip, *received, 2)
        halo_strips = lat_swap(strips1, width)
        return advect(width, (g1, *halo), (strips1, *halo_strips), backward_coef, "both", (g0, strips0))

    both = by_steps(1, backward)

    def last(width):
        return advect(width, (both, *lat_swap(both, width)), None, backward_coef, "native")

    result = by_steps(0, last)
    return result.reshape(state.shape)


def solution(mesh):
    return jax.shard_map(
        per_device,
        mesh=mesh,
        in_specs=(
            P(None, None, "lat", "lon"),
            P(None, None, "lat", "lon"),
            P("lat", "lon"),
            P(None, ("lon", "lat")),
            P(None, ("lon", "lat"), None),
            P(),
            P(),
            P(),
            P(),
            P(),
            P(None, ("lon", "lat"), None, None, None),
        ),
        out_specs=P(None, None, "lat", "lon"),
        check_vma=False,
    )
```

```python
from functools import partial

import jax
import jax.numpy as jnp
from jax import lax
from jax.experimental import pallas as pl
from jax.experimental.pallas import tpu as pltpu
from jax.sharding import PartitionSpec as P

F32 = jnp.float32
BF16 = jnp.bfloat16
I32 = jnp.int32
VARS = 8
SPAN = 32
STRIP_SPAN = 32
LEV = 64
MAXSTEP = 4
SND = 128


def struct(*shape, dtype=F32):
    return jax.ShapeDtypeStruct(shape, dtype)


def tiled(grid, *shape):
    zeros = (0,) * (len(shape) - 2)
    return pl.BlockSpec((*shape[:-2], shape[-2] // grid, shape[-1]), lambda t: (*zeros, t, 0))


def whole(shape):
    return pl.BlockSpec(shape, lambda *_: (0,) * len(shape))


VMEM_SPEC = pl.BlockSpec(memory_space=pltpu.VMEM)
SMEM_SPEC = pl.BlockSpec(memory_space=pltpu.SMEM)


def params(mebibytes):
    return pltpu.CompilerParams(vmem_limit_bytes=mebibytes * 1024 * 1024)


def in_hbm(*arrays):
    return [pltpu.with_memory_space_constraint(x, pltpu.HBM) for x in arrays]


def lanes():
    return lax.broadcasted_iota(I32, (STRIP_SPAN, 128), 1)


def roll(x, shift):
    shift = shift % 128
    return x if shift == 0 else pltpu.roll(x, shift, 1)


def level_tiles(count, body, span=8):
    def step(t, carry):
        body(t, pl.ds(pl.multiple_of(t * span, span), span))
        return carry

    lax.fori_loop(0, count, step, 0)


def lon_even():
    return lax.axis_index("lon") % 2 == 0


def lat_even():
    return lax.axis_index("lat") % 2 == 0


def own_strip(load, count):
    lane = lanes()
    strip = jnp.zeros((STRIP_SPAN, 128), F32)
    for g in range(count):
        x = load(g)
        base = 32 * g
        strip = jnp.where((lane >= base + 8) & (lane < base + 16), roll(x, base + 8), strip)
        strip = jnp.where((lane >= base + 16) & (lane < base + 24), roll(x, base + 24), strip)
    return strip


def pack_strips(strips, even):
    lane = lanes() % 32
    east = jnp.zeros((STRIP_SPAN, 128), F32)
    west = jnp.zeros((STRIP_SPAN, 128), F32)
    for r in range(4):
        here = (lane >= 8 * r) & (lane < 8 * r + 8)
        east = jnp.where(here, roll(strips[r], 8 * r - 16), east)
        west = jnp.where(here, roll(strips[r], 8 * r - 8), west)
    return jnp.where(even, east, west), jnp.where(even, west, east)


def pack_kernel(state, winds, diff, main, strip, first, second, *, grid):
    even = lon_even()
    flip = jnp.where(lat_even(), 3, 0)

    def body(t, level):
        strips = [[] for _ in range(3)]
        for p in range(4):
            r = jnp.abs(flip - p)
            source = pl.ds(t * 4 * STRIP_SPAN + r, STRIP_SPAN, stride=4)
            row = [state[v, source, :] for v in range(VARS)] + [winds[v, source, :] for v in range(2)]
            row.append(jnp.broadcast_to(diff[pl.ds(r, 1), :], (STRIP_SPAN, 128)))
            for v in range(11):
                main[p, v, level, :] = row[v]
            for b in range(3):
                s = own_strip(lambda g: row[4 * b + g], 4 if b < 2 else 3)
                strip[p, b, level, :] = s
                strips[b].append(s)
        for b in range(3):
            first[b, level, :], second[b, level, :] = pack_strips(strips[b], even)

    level_tiles(LEV // STRIP_SPAN // grid, body, STRIP_SPAN)


def pack(state, winds, diff, grid=2):
    shapes = [(4, 11, LEV, 128), (4, 3, LEV, 128), (3, LEV, 128), (3, LEV, 128)]
    return pl.pallas_call(
        partial(pack_kernel, grid=grid),
        grid=(grid,),
        in_specs=[tiled(grid, 8, 256, 128), tiled(grid, 2, 256, 128), whole((4, 128))],
        out_specs=[tiled(grid, *s) for s in shapes],
        out_shape=[struct(*s) for s in shapes],
        compiler_params=params(16),
        name="pack",
    )(*in_hbm(state, winds), diff)


def complete_kernel(strip, first, second, *outs):
    even = lon_even()
    blocks = strip.shape[1]
    split = blocks // len(outs)

    def body(t, level):
        lane = lax.broadcasted_iota(I32, (SPAN, 128), 1) % 32
        for b in range(blocks):
            one, two = first[b, level, :], second[b, level, :]
            east = jnp.where(even, one, two)
            west = jnp.where(even, two, one)
            for r in range(4):
                full = jnp.where(lane < 8, roll(west, -8 * r), strip[r, b, level, :])
                outs[b // split][r, b % split, level, :] = jnp.where(lane >= 24, roll(east, 24 - 8 * r), full)

    level_tiles(LEV // SPAN, body, SPAN)


def complete(strip, first, second, parts):
    split = strip.shape[1] // parts
    return pl.pallas_call(
        complete_kernel,
        in_specs=[VMEM_SPEC] * 3,
        out_specs=[VMEM_SPEC] * parts,
        out_shape=[struct(4, split, LEV, 128)] * parts,
        compiler_params=params(4),
        name="complete",
    )(strip, first, second)


def open_to_next_chip():
    lat = lax.axis_index("lat")
    return jnp.where((lat > 0) & (lat < lax.axis_size("lat") - 1), 1.0, 0.0).astype(F32)


def each_row(first, last, body):
    def step(i, carry):
        body(i)
        return carry

    lax.fori_loop(first, last, step, 0)


def coefficient_kernel(own, r0, r1, sown, s0, s1, out, raw):
    flipped = lat_even()
    open_side = open_to_next_chip()
    lane = lax.broadcasted_iota(I32, (LEV, 128), 1)

    def fill(i, main, strip):
        packed = strip[2]
        spread = []
        for g in range(3):
            one = jnp.where(lane < 32, roll(packed, -32 * g), 0.0)
            one = one + roll(one, 32)
            spread.append(one + roll(one, 64))
        plain = [main[VARS], main[VARS + 1], main[VARS + 2]]
        for n, (w0, w1, dd) in enumerate((plain, spread)):
            half = w0 * 0.5
            half_west, dd_west = roll(half, 1), roll(dd, 1)
            if n == 0:
                half_west = jnp.where(lane == 0, roll(spread[0], 121) * 0.5, half_west)
                dd_west = jnp.where(lane == 0, roll(spread[2], 121), dd_west)
            lat_half = w1 * 0.5
            values = half + dd, half - dd, half_west + dd_west, half_west - dd_west, lat_half + dd, lat_half - dd
            for m, value in enumerate(values):
                raw[i, 6 * n + m] = value

    for first, target, main, strip in ((0, 3, r0, s0), (4, 4, own, sown), (8, 11, r1, s1)):
        way = 1 if first == 4 else -1

        def two(j):
            for q in (2 * j, 2 * j + 1):
                row = 3 - q if first == 8 else q
                fill(first + q if first == 8 else target + way * q, main.at[row], strip.at[row])

        each_row(0, 2, two)

    def combine(i):
        scale = jnp.where(i >= 8, open_side, 1.0)
        for n in range(2):
            a, b, a_west, b_west = (raw[i, 6 * n + m] for m in range(4))
            u, w = interface(raw, flipped, i, n)
            u_before, w_before = interface(raw, flipped, i - 1, n)
            values = 1.0 - a + b_west - u + w_before, -b, a_west, -w, u_before
            for m, value in enumerate(values):
                out[i, 5 * n + m] = value * scale

    each_row(1, 11, combine)


def interface(raw, flipped, i, n):
    u = jnp.where(flipped, -raw[i + 1, 6 * n + 5], raw[i, 6 * n + 4])
    w = jnp.where(flipped, -raw[i + 1, 6 * n + 4], raw[i, 6 * n + 5])
    return u, w


def coefficients(tile, strips):
    return pl.pallas_call(
        coefficient_kernel,
        in_specs=[VMEM_SPEC] * 6,
        out_specs=[VMEM_SPEC] * 2,
        out_shape=[struct(12, 10, LEV, 128), struct(12, 12, LEV, 128)],
        compiler_params=params(4),
        name="coefficients",
    )(*tile, *strips)


def adjoint_kernel(forward, raw, out):
    flipped = lat_even()
    open_side = open_to_next_chip()

    def combine(i):
        scale = jnp.where(i >= 8, open_side, 1.0)
        for n in range(2):
            out[i, 5 * n] = forward[i, 5 * n]
            out[i, 5 * n + 1] = raw[i, 6 * n] * scale
            out[i, 5 * n + 2] = -raw[i, 6 * n + 3] * scale
            out[i, 5 * n + 3] = interface(raw, flipped, i, n)[0] * scale
            out[i, 5 * n + 4] = -interface(raw, flipped, i - 1, n)[1] * scale

    each_row(1, 11, combine)


def adjoint_coefficients(forward, raw):
    return pl.pallas_call(
        adjoint_kernel,
        in_specs=[VMEM_SPEC] * 2,
        out_specs=VMEM_SPEC,
        out_shape=struct(12, 10, LEV, 128),
        compiler_params=params(4),
        name="adjoint_coefficients",
    )(forward, raw)


def advect_kernel(*refs, steps, apart, result, addend):
    refs = list(refs)
    steps = refs.pop(0)[0] if steps is None else steps
    own, r0, r1 = refs[:3]
    refs = refs[3:]
    strips = ()
    if apart:
        strips, refs = refs[:3], refs[3:]
    coef = refs.pop(0)
    if addend:
        add_main, add_strip = refs[:2]
        refs = refs[2:]
    out, *work, shift = refs
    source = lax.broadcasted_iota(I32, (256, 256), 0) % 128
    target = lax.broadcasted_iota(I32, (256, 256), 1)
    chosen = jnp.where(target < 128, target + 1, target + 127) % 128
    shift[...] = (source == chosen).astype(F32).astype(BF16)
    flip = jnp.where(lat_even(), 3, 0)
    width = r0.shape[0]

    def place(target, sources, offset, count):
        tile, intra, inter = sources

        def halo(j, carry):
            target[3 - j, offset : offset + count] = intra[j, 0:count]
            target[8 + j, offset : offset + count] = inter[width - 1 - j, 0:count]
            return carry

        def inside(j, carry):
            target[4 + j, offset : offset + count] = tile[j, 0:count]
            return carry

        lax.fori_loop(0, width, halo, 0)
        lax.fori_loop(0, 4, inside, 0)

    def start(target):
        if apart:
            place(target, (own, r0, r1), 0, VARS)
            place(target, strips, VARS, 2)
        else:
            place(target, (own, r0, r1), 0, VARS + 2)

    def when(condition, run):
        if isinstance(condition, bool):
            if condition:
                run()
        else:
            pl.when(condition)(run)

    for n in range(2):
        when(steps % 2 != n, partial(start, work[n]))
    lane = lax.broadcasted_iota(I32, (LEV, 128), 1)

    def row(now, i, last, store):
        def stencil(n, v, f, east, west):
            value = coef[i, n] * f
            value = value + coef[i, n + 1] * east
            value = value + coef[i, n + 2] * west
            value = value + coef[i, n + 3] * now[i + 1, v]
            return value + coef[i, n + 4] * now[i - 1, v]

        wanted = VARS + (0 if last and result != "both" else 2)
        halves = split(now[i, 0:wanted].reshape(wanted * LEV, 128))
        moved = dot(jnp.concatenate(halves, axis=1), shift[...], (1, 0))
        moved = moved.reshape(wanted, LEV, 256)
        for b in range(2):
            f = now[i, VARS + b]
            ends = jnp.where(lane % 32 == 25, roll(f, 18), f)
            for v in (VARS + b, *range(4 * b, 4 * b + 4)):
                if v >= wanted:
                    continue
                f = now[i, v]
                east, west = moved[v, :, :128], moved[v, :, 128:]
                if v < VARS:
                    rim = roll(ends, 103 - 32 * (v % 4))
                    east = jnp.where(lane == 127, rim, east)
                    west = jnp.where(lane == 0, rim, west)
                store(v, stencil(5 if v >= VARS else 0, v, f, east, west))

    def step(reach):
        def two(j, carry):
            for i in (4 - reach + 2 * j, 5 - reach + 2 * j):

                def store(v, value):
                    work[1 - reach % 2][i, v] = value

                row(work[reach % 2], i, False, store)
            return carry

        lax.fori_loop(0, 2 + reach, two, 0)

    for reach in (3, 2, 1):
        when(steps > reach, partial(step, reach))

    def final(r, carry):
        def store(v, value):
            if addend:
                value = value + (add_main[r, v] if v < VARS else add_strip[r, v - VARS])
            if result == "native":
                out[v, pl.ds(jnp.abs(flip - r), LEV, stride=4), :] = value
            else:
                out[r, v] = value

        row(work[0], 4 + r, True, store)
        return carry

    lax.fori_loop(0, 4, final, 0)


def advect(steps, tile, strips, coef, result, addend=None):
    args = [*tile]
    if strips is not None:
        args += strips
    args.append(coef)
    if addend is not None:
        args += addend
    if result == "native":
        shape = (8, 256, 128)
    else:
        shape = (4, 10 if result == "both" else 8, LEV, 128)
    static = isinstance(steps, int)
    return pl.pallas_call(
        partial(
            advect_kernel,
            steps=steps if static else None,
            apart=strips is not None,
            result=result,
            addend=addend is not None,
        ),
        in_specs=([] if static else [SMEM_SPEC]) + [VMEM_SPEC] * len(args),
        out_specs=VMEM_SPEC,
        out_shape=struct(*shape),
        scratch_shapes=[pltpu.VMEM((12, 10, LEV, 128), F32)] * 2 + [pltpu.VMEM((256, 256), BF16)],
        compiler_params=params(14),
        name="advect_" + result,
    )(*([] if static else [steps]), *args)


def split(x):
    high = x.astype(BF16)
    return high, (x - high.astype(F32)).astype(BF16)


def dot(x, y, dims):
    return lax.dot_general(x, y, ((dims[:1], dims[1:]), ((), ())), preferred_element_type=F32)


def dot3(x, y, dims):
    return dot(x[0], y[0], dims) + (dot(x[0], y[1], dims) + dot(x[1], y[0], dims))


def relayout_kernel(observed, sent):
    homes = observed.shape[3]
    for k in range(2):
        for q in range(3):
            for c in range(4):
                sent[pl.ds(12 * k + 4 * q + c, homes, stride=24), :] = observed[k, 0, q, :, pl.ds(128 * c, 128)]


def relayout(observed):
    turned = jnp.transpose(observed, (0, 1, 3, 2, 4))
    homes = turned.shape[3]
    sent = pl.pallas_call(
        relayout_kernel,
        grid=(1,),
        in_specs=[whole(turned.shape)],
        out_specs=whole((homes * 24, 128)),
        out_shape=struct(homes * 24, 128),
        compiler_params=params(16),
        name="relayout",
    )(*in_hbm(turned))
    return sent.reshape(homes, 24, 128)


PADDED = 640


def column_of(row):
    square = (SND, SND)
    here = lax.broadcasted_iota(I32, square, 0) == lax.broadcasted_iota(I32, square, 1)
    return jnp.sum(jnp.where(here, jnp.broadcast_to(row, square), 0), axis=1, keepdims=True)


def load_table(table, high, low):
    count = table.shape[0]
    full = count // 16 * 16
    high[pl.ds(0, full), :], low[pl.ds(0, full), :] = split(table[pl.ds(0, full), :])
    rest = jnp.zeros((PADDED - full, table.shape[1]), F32)
    if count > full:
        zeros = jnp.zeros((PADDED - count, table.shape[1]), F32)
        rest = jnp.concatenate([table[pl.ds(full, count - full), :], zeros], axis=0)
    high[pl.ds(full, PADDED - full), :], low[pl.ds(full, PADDED - full), :] = split(rest)


def observe_kernel(cells, owners, channels, weight, field, *refs, slot):
    if slot == 0:
        hbm, refs = refs[:3], refs[3:]
        (out, strip, first, second, *tables), refs = refs[:8], refs[8:]
        (absorb_table, emit_table, fetched), sems = refs[:3], refs[3]
        targets = (absorb_table, emit_table, fetched)
    else:
        tables, hbm, before, refs = refs[:4], refs[4:5], refs[5:8], refs[8:]
        (out, strip, first, second), (fetched, sems) = refs[:4], refs[4:]
        targets = (fetched,)
    copies = [
        pltpu.make_async_copy(source, target, sems.at[n])
        for n, (source, target) in enumerate(zip(hbm, targets, strict=True))
    ]
    for copy in copies:
        copy.start()

    flip = jnp.where(lat_even(), 3, 0)
    square = (SND, SND)
    row_id = lax.broadcasted_iota(I32, square, 0)
    lane_id = lax.broadcasted_iota(I32, square, 1)
    entry = lax.broadcasted_iota(I32, (PADDED, channels.shape[1]), 0)
    listed = (entry == channels[...]).astype(F32).astype(BF16)
    times = dot(jnp.ones((8, channels.shape[1]), BF16), listed, (1, 1))[0:1]
    cell = column_of(cells[slot : slot + 1, :])
    owner_row = owners[slot : slot + 1, :]
    owner = column_of(owner_row)
    earlier = (owner == owner_row) & (lane_id < row_id)
    rank = jnp.sum(jnp.where(earlier, 1, 0), axis=1, keepdims=True)
    picks = [(cell == lane_id + 128 * jnp.abs(flip - r)).astype(F32).astype(BF16) for r in range(4)]
    pieces = [jnp.zeros((SND, VARS * LEV), F32)] * 2
    for r in range(4):
        x = split(field[r, 0:VARS].reshape(VARS * LEV, 128))
        pieces = [piece + dot(picks[r], part, (1, 1)) for piece, part in zip(pieces, x, strict=True)]
    column = [piece.astype(BF16) for piece in pieces]
    if slot == 0:
        for n, table in enumerate((absorb_table, emit_table)):
            copies[n].wait()
            load_table(table, tables[2 * n], tables[2 * n + 1])
    absorb = (tables[0][...], tables[1][...])
    emission = (tables[2][...], tables[3][...])
    optical = dot3(column, absorb, (1, 1))
    bright = dot3(column, emission, (1, 1))
    decay = jnp.exp(-jnp.abs(optical))
    inverse = 1.0 / (1.0 + decay)
    rest = decay * inverse
    positive = optical >= 0
    passing = jnp.where(positive, rest, inverse)
    opaque = jnp.where(positive, inverse, rest)
    choices = [((owner == lane_id) & (rank == q)).astype(F32).astype(BF16) for q in range(3)]
    copies[-1].wait()
    parts = []
    for c in range(4):
        part = [jnp.zeros(square, F32)] * 2
        for q in range(3):
            seen = split(fetched[pl.ds(12 * slot + 4 * q + c, SND, stride=24), :])
            part = [p + dot(choices[q], x, (1, 0)) for p, x in zip(part, seen, strict=True)]
        parts.append(part)
    wanted = [jnp.concatenate([part[n] for part in parts], axis=1).astype(BF16) for n in range(2)]
    totals = dot(wanted[0], listed, (1, 1)) + dot(wanted[1], listed, (1, 1))
    evolved = passing * bright
    departure = weight[...] * (times * evolved - totals)
    to_bright = departure * passing
    to_optical = -(departure * evolved * opaque)
    column = dot3(split(to_optical), absorb, (1, 0)) + dot3(split(to_bright), emission, (1, 0))
    ch, cl = split(column)
    for r in range(4):
        placed = dot(ch, picks[r], (0, 0)) + dot(cl, picks[r], (0, 0))
        out[r] = placed.reshape(VARS, LEV, 128)

    even = lon_even()
    if slot == 1:
        strip[:, 2:4] = before[0][...]
        first[2:4] = before[1][...]
        second[2:4] = before[2][...]

    def strips_of(t, level):
        for b in range(2):
            strips = []
            for r in range(4):
                s = own_strip(lambda g: out[r, 4 * b + g, level, :], 4)
                strip[r, b, level, :] = s
                strips.append(s)
            first[b, level, :], second[b, level, :] = pack_strips(strips, even)

    level_tiles(LEV // STRIP_SPAN, strips_of, STRIP_SPAN)


def observe(slot, small, field, tables, fetched, before):
    count = 2 if slot == 0 else 4
    shapes = [struct(4, 8, LEV, 128), struct(4, count, LEV, 128)] + [struct(count, LEV, 128)] * 2
    moved = [fetched]
    if slot == 0:
        moved = [*tables, fetched]
        tables = []
        shapes += [struct(PADDED, VARS * LEV, dtype=BF16)] * 4
    hbm_spec = pl.BlockSpec(memory_space=pltpu.HBM)
    return pl.pallas_call(
        partial(observe_kernel, slot=slot),
        in_specs=[VMEM_SPEC] * (len(small) + 1 + len(tables)) + [hbm_spec] * len(moved) + [VMEM_SPEC] * len(before),
        out_specs=[VMEM_SPEC] * len(shapes),
        out_shape=shapes,
        scratch_shapes=[pltpu.VMEM(x.shape, F32) for x in moved] + [pltpu.SemaphoreType.DMA((len(moved),))],
        compiler_params=params(10),
        name="observe",
    )(*small, field, *tables, *in_hbm(*moved), *before)


def swap(x, axis, parity, wrap):
    devices = lax.axis_size(axis)
    pairs = []
    for i in range(parity, devices, 2):
        if i + 1 < devices or wrap:
            j = (i + 1) % devices
            pairs += [(i, j), (j, i)]
    return lax.ppermute(x, axis, pairs)


def lat_swap(x, width=4):
    beyond = swap(x[4 - width :], "lat", 1, False)
    return swap(x[:width], "lat", 0, False), beyond


def lon_swap(first, second):
    beyond = swap(second, "lon", 1, True)
    return swap(first, "lon", 0, True), beyond


def per_device(
    state, winds, diffusivity, sounding_cell, sounding_owner, step_counts, channel_list, absorb_table, emit_table,
    obs_weight, observed,
):
    def by_steps(slot, run):
        branches = [partial(run, width) for width in range(1, MAXSTEP + 1)]
        return lax.switch(step_counts[slot] - 1, branches)

    main, strip, first, second = pack(state.reshape(8, 256, 128), winds.reshape(2, 256, 128), diffusivity)
    received = lon_swap(first, second)
    halo = lat_swap(main)
    sent, received = lax.optimization_barrier((relayout(observed), received))
    (strip,) = complete(strip, *received, 1)
    fetched = lax.all_to_all(sent, ("lon", "lat"), split_axis=0, concat_axis=0, tiled=True)
    tile, strips = (main, *halo), (strip, *lat_swap(strip))
    onward, raw = coefficients(tile, strips)
    both0 = advect(step_counts[:1], tile, strips, onward, "both")
    halo = lat_swap(both0)
    raw, both0 = lax.optimization_barrier((raw, both0))
    backward_coef = adjoint_coefficients(onward, raw)

    extra = PADDED - obs_weight.shape[0]
    padded_weight = jnp.pad(obs_weight, (0, extra))[None, :]
    small = [sounding_cell, sounding_owner[:, :, 0], channel_list[None, :], padded_weight]
    fetched = fetched.reshape(-1, 128)
    g0, *edges, th0, tl0, th1, tl1 = observe(0, small, both0, [absorb_table.T, emit_table.T], fetched, [])
    both0, backward_coef, g0 = lax.optimization_barrier((both0, backward_coef, g0))
    field1 = advect(step_counts[1:], (both0, *halo), None, onward, "main")
    g1, strip, first, second = observe(1, small, field1, [th0, tl0, th1, tl1], fetched, edges)

    def backward(width):
        received = lon_swap(first, second)
        halo = lat_swap(g1, width)
        strips1, strips0 = complete(strip, *received, 2)
        halo_strips = lat_swap(strips1, width)
        return advect(width, (g1, *halo), (strips1, *halo_strips), backward_coef, "both", (g0, strips0))

    both = by_steps(1, backward)

    def last(width):
        return advect(width, (both, *lat_swap(both, width)), None, backward_coef, "native")

    result = by_steps(0, last)
    return result.reshape(state.shape)


def solution(mesh):
    return jax.shard_map(
        per_device,
        mesh=mesh,
        in_specs=(
            P(None, None, "lat", "lon"),
            P(None, None, "lat", "lon"),
            P("lat", "lon"),
            P(None, ("lon", "lat")),
            P(None, ("lon", "lat"), None),
            P(),
            P(),
            P(),
            P(),
            P(),
            P(None, ("lon", "lat"), None, None, None),
        ),
        out_specs=P(None, None, "lat", "lon"),
        check_vma=False,
    )
```

```python
from functools import partial

import jax
import jax.numpy as jnp
from jax import lax
from jax.experimental import pallas as pl
from jax.experimental.pallas import tpu as pltpu
from jax.sharding import PartitionSpec as P

F32 = jnp.float32
BF16 = jnp.bfloat16
I32 = jnp.int32
VARS = 8
SPAN = 32
STRIP_SPAN = 32
LEV = 64
MAXSTEP = 4
SND = 128


def struct(*shape, dtype=F32):
    return jax.ShapeDtypeStruct(shape, dtype)


def tiled(grid, *shape):
    zeros = (0,) * (len(shape) - 2)
    return pl.BlockSpec((*shape[:-2], shape[-2] // grid, shape[-1]), lambda t: (*zeros, t, 0))


def whole(shape):
    return pl.BlockSpec(shape, lambda *_: (0,) * len(shape))


VMEM_SPEC = pl.BlockSpec(memory_space=pltpu.VMEM)
SMEM_SPEC = pl.BlockSpec(memory_space=pltpu.SMEM)


def params(mebibytes):
    return pltpu.CompilerParams(vmem_limit_bytes=mebibytes * 1024 * 1024)


def in_hbm(*arrays):
    return [pltpu.with_memory_space_constraint(x, pltpu.HBM) for x in arrays]


def lanes():
    return lax.broadcasted_iota(I32, (STRIP_SPAN, 128), 1)


def roll(x, shift):
    shift = shift % 128
    return x if shift == 0 else pltpu.roll(x, shift, 1)


def level_tiles(count, body, span=8):
    def step(t, carry):
        body(t, pl.ds(pl.multiple_of(t * span, span), span))
        return carry

    lax.fori_loop(0, count, step, 0)


def lon_even():
    return lax.axis_index("lon") % 2 == 0


def lat_even():
    return lax.axis_index("lat") % 2 == 0


def own_strip(load, count):
    lane = lanes()
    strip = jnp.zeros((STRIP_SPAN, 128), F32)
    for g in range(count):
        x = load(g)
        base = 32 * g
        strip = jnp.where((lane >= base + 8) & (lane < base + 16), roll(x, base + 8), strip)
        strip = jnp.where((lane >= base + 16) & (lane < base + 24), roll(x, base + 24), strip)
    return strip


def pack_strips(strips, even):
    lane = lanes() % 32
    east = jnp.zeros((STRIP_SPAN, 128), F32)
    west = jnp.zeros((STRIP_SPAN, 128), F32)
    for r in range(4):
        here = (lane >= 8 * r) & (lane < 8 * r + 8)
        east = jnp.where(here, roll(strips[r], 8 * r - 16), east)
        west = jnp.where(here, roll(strips[r], 8 * r - 8), west)
    return jnp.where(even, east, west), jnp.where(even, west, east)


def pack_kernel(state, winds, diff, main, strip, first, second, *, grid):
    even = lon_even()
    flip = jnp.where(lat_even(), 3, 0)

    def body(t, level):
        strips = [[] for _ in range(3)]
        for p in range(4):
            r = jnp.abs(flip - p)
            source = pl.ds(t * 4 * STRIP_SPAN + r, STRIP_SPAN, stride=4)
            row = [state[v, source, :] for v in range(VARS)] + [winds[v, source, :] for v in range(2)]
            row.append(jnp.broadcast_to(diff[pl.ds(r, 1), :], (STRIP_SPAN, 128)))
            for v in range(11):
                main[p, v, level, :] = row[v]
            for b in range(3):
                s = own_strip(lambda g: row[4 * b + g], 4 if b < 2 else 3)
                strip[p, b, level, :] = s
                strips[b].append(s)
        for b in range(3):
            first[b, level, :], second[b, level, :] = pack_strips(strips[b], even)

    level_tiles(LEV // STRIP_SPAN // grid, body, STRIP_SPAN)


def pack(state, winds, diff, grid=2):
    shapes = [(4, 11, LEV, 128), (4, 3, LEV, 128), (3, LEV, 128), (3, LEV, 128)]
    return pl.pallas_call(
        partial(pack_kernel, grid=grid),
        grid=(grid,),
        in_specs=[tiled(grid, 8, 256, 128), tiled(grid, 2, 256, 128), whole((4, 128))],
        out_specs=[tiled(grid, *s) for s in shapes],
        out_shape=[struct(*s) for s in shapes],
        compiler_params=params(16),
        name="pack",
    )(*in_hbm(state, winds, diff))


def complete_kernel(strip, first, second, *outs):
    even = lon_even()
    blocks = strip.shape[1]
    split = blocks // len(outs)

    def body(t, level):
        lane = lax.broadcasted_iota(I32, (SPAN, 128), 1) % 32
        for b in range(blocks):
            one, two = first[b, level, :], second[b, level, :]
            east = jnp.where(even, one, two)
            west = jnp.where(even, two, one)
            for r in range(4):
                full = jnp.where(lane < 8, roll(west, -8 * r), strip[r, b, level, :])
                outs[b // split][r, b % split, level, :] = jnp.where(lane >= 24, roll(east, 24 - 8 * r), full)

    level_tiles(LEV // SPAN, body, SPAN)


def complete(strip, first, second, parts):
    split = strip.shape[1] // parts
    return pl.pallas_call(
        complete_kernel,
        in_specs=[VMEM_SPEC] * 3,
        out_specs=[VMEM_SPEC] * parts,
        out_shape=[struct(4, split, LEV, 128)] * parts,
        compiler_params=params(4),
        name="complete",
    )(strip, first, second)


def open_to_next_chip():
    lat = lax.axis_index("lat")
    return jnp.where((lat > 0) & (lat < lax.axis_size("lat") - 1), 1.0, 0.0).astype(F32)


def each_row(first, last, body):
    def step(i, carry):
        body(i)
        return carry

    lax.fori_loop(first, last, step, 0)


def coefficient_kernel(own, r0, r1, sown, s0, s1, out, raw):
    flipped = lat_even()
    open_side = open_to_next_chip()
    lane = lax.broadcasted_iota(I32, (LEV, 128), 1)

    def fill(i, main, strip):
        packed = strip[2]
        spread = []
        for g in range(3):
            one = jnp.where(lane < 32, roll(packed, -32 * g), 0.0)
            one = one + roll(one, 32)
            spread.append(one + roll(one, 64))
        plain = [main[VARS], main[VARS + 1], main[VARS + 2]]
        for n, (w0, w1, dd) in enumerate((plain, spread)):
            half = w0 * 0.5
            half_west, dd_west = roll(half, 1), roll(dd, 1)
            if n == 0:
                half_west = jnp.where(lane == 0, roll(spread[0], 121) * 0.5, half_west)
                dd_west = jnp.where(lane == 0, roll(spread[2], 121), dd_west)
            lat_half = w1 * 0.5
            values = half + dd, half - dd, half_west + dd_west, half_west - dd_west, lat_half + dd, lat_half - dd
            for m, value in enumerate(values):
                raw[i, 6 * n + m] = value

    for first, target, main, strip in ((0, 3, r0, s0), (4, 4, own, sown), (8, 11, r1, s1)):
        way = 1 if first == 4 else -1

        def two(j):
            for q in (2 * j, 2 * j + 1):
                row = 3 - q if first == 8 else q
                fill(first + q if first == 8 else target + way * q, main.at[row], strip.at[row])

        each_row(0, 2, two)

    def combine(i):
        scale = jnp.where(i >= 8, open_side, 1.0)
        for n in range(2):
            a, b, a_west, b_west = (raw[i, 6 * n + m] for m in range(4))
            u, w = interface(raw, flipped, i, n)
            u_before, w_before = interface(raw, flipped, i - 1, n)
            values = 1.0 - a + b_west - u + w_before, -b, a_west, -w, u_before
            for m, value in enumerate(values):
                out[i, 5 * n + m] = value * scale

    each_row(1, 11, combine)


def interface(raw, flipped, i, n):
    u = jnp.where(flipped, -raw[i + 1, 6 * n + 5], raw[i, 6 * n + 4])
    w = jnp.where(flipped, -raw[i + 1, 6 * n + 4], raw[i, 6 * n + 5])
    return u, w


def coefficients(tile, strips):
    return pl.pallas_call(
        coefficient_kernel,
        in_specs=[VMEM_SPEC] * 6,
        out_specs=[VMEM_SPEC] * 2,
        out_shape=[struct(12, 10, LEV, 128), struct(12, 12, LEV, 128)],
        compiler_params=params(4),
        name="coefficients",
    )(*tile, *strips)


def adjoint_kernel(forward, raw, out):
    flipped = lat_even()
    open_side = open_to_next_chip()

    def combine(i):
        scale = jnp.where(i >= 8, open_side, 1.0)
        for n in range(2):
            out[i, 5 * n] = forward[i, 5 * n]
            out[i, 5 * n + 1] = raw[i, 6 * n] * scale
            out[i, 5 * n + 2] = -raw[i, 6 * n + 3] * scale
            out[i, 5 * n + 3] = interface(raw, flipped, i, n)[0] * scale
            out[i, 5 * n + 4] = -interface(raw, flipped, i - 1, n)[1] * scale

    each_row(1, 11, combine)


def adjoint_coefficients(forward, raw):
    return pl.pallas_call(
        adjoint_kernel,
        in_specs=[VMEM_SPEC] * 2,
        out_specs=VMEM_SPEC,
        out_shape=struct(12, 10, LEV, 128),
        compiler_params=params(4),
        name="adjoint_coefficients",
    )(forward, raw)


def advect_kernel(*refs, steps, apart, result, addend):
    refs = list(refs)
    steps = refs.pop(0)[0] if steps is None else steps
    own, r0, r1 = refs[:3]
    refs = refs[3:]
    strips = ()
    if apart:
        strips, refs = refs[:3], refs[3:]
    coef = refs.pop(0)
    if addend:
        add_main, add_strip = refs[:2]
        refs = refs[2:]
    out, *work, shift = refs
    source = lax.broadcasted_iota(I32, (256, 256), 0) % 128
    target = lax.broadcasted_iota(I32, (256, 256), 1)
    chosen = jnp.where(target < 128, target + 1, target + 127) % 128
    shift[...] = (source == chosen).astype(F32).astype(BF16)
    flip = jnp.where(lat_even(), 3, 0)
    width = r0.shape[0]

    def place(target, sources, offset, count):
        tile, intra, inter = sources

        def halo(j, carry):
            target[3 - j, offset : offset + count] = intra[j, 0:count]
            target[8 + j, offset : offset + count] = inter[width - 1 - j, 0:count]
            return carry

        def inside(j, carry):
            target[4 + j, offset : offset + count] = tile[j, 0:count]
            return carry

        lax.fori_loop(0, width, halo, 0)
        lax.fori_loop(0, 4, inside, 0)

    def start(target):
        if apart:
            place(target, (own, r0, r1), 0, VARS)
            place(target, strips, VARS, 2)
        else:
            place(target, (own, r0, r1), 0, VARS + 2)

    def when(condition, run):
        if isinstance(condition, bool):
            if condition:
                run()
        else:
            pl.when(condition)(run)

    for n in range(2):
        when(steps % 2 != n, partial(start, work[n]))
    lane = lax.broadcasted_iota(I32, (LEV, 128), 1)

    def row(now, i, last, store):
        def stencil(n, v, f, east, west):
            value = coef[i, n] * f
            value = value + coef[i, n + 1] * east
            value = value + coef[i, n + 2] * west
            value = value + coef[i, n + 3] * now[i + 1, v]
            return value + coef[i, n + 4] * now[i - 1, v]

        wanted = VARS + (0 if last and result != "both" else 2)
        halves = split(now[i, 0:wanted].reshape(wanted * LEV, 128))
        moved = dot(jnp.concatenate(halves, axis=1), shift[...], (1, 0))
        moved = moved.reshape(wanted, LEV, 256)
        for b in range(2):
            f = now[i, VARS + b]
            ends = jnp.where(lane % 32 == 25, roll(f, 18), f)
            for v in (VARS + b, *range(4 * b, 4 * b + 4)):
                if v >= wanted:
                    continue
                f = now[i, v]
                east, west = moved[v, :, :128], moved[v, :, 128:]
                if v < VARS:
                    rim = roll(ends, 103 - 32 * (v % 4))
                    east = jnp.where(lane == 127, rim, east)
                    west = jnp.where(lane == 0, rim, west)
                store(v, stencil(5 if v >= VARS else 0, v, f, east, west))

    def step(reach):
        def two(j, carry):
            for i in (4 - reach + 2 * j, 5 - reach + 2 * j):

                def store(v, value):
                    work[1 - reach % 2][i, v] = value

                row(work[reach % 2], i, False, store)
            return carry

        lax.fori_loop(0, 2 + reach, two, 0)

    for reach in (3, 2, 1):
        when(steps > reach, partial(step, reach))

    def final(r, carry):
        def store(v, value):
            if addend:
                value = value + (add_main[r, v] if v < VARS else add_strip[r, v - VARS])
            if result == "native":
                out[v, pl.ds(jnp.abs(flip - r), LEV, stride=4), :] = value
            else:
                out[r, v] = value

        row(work[0], 4 + r, True, store)
        return carry

    lax.fori_loop(0, 4, final, 0)


def advect(steps, tile, strips, coef, result, addend=None):
    args = [*tile]
    if strips is not None:
        args += strips
    args.append(coef)
    if addend is not None:
        args += addend
    if result == "native":
        shape = (8, 256, 128)
    else:
        shape = (4, 10 if result == "both" else 8, LEV, 128)
    static = isinstance(steps, int)
    return pl.pallas_call(
        partial(
            advect_kernel,
            steps=steps if static else None,
            apart=strips is not None,
            result=result,
            addend=addend is not None,
        ),
        in_specs=([] if static else [SMEM_SPEC]) + [VMEM_SPEC] * len(args),
        out_specs=VMEM_SPEC,
        out_shape=struct(*shape),
        scratch_shapes=[pltpu.VMEM((12, 10, LEV, 128), F32)] * 2 + [pltpu.VMEM((256, 256), BF16)],
        compiler_params=params(14),
        name="advect_" + result,
    )(*([] if static else [steps]), *args)


def split(x):
    high = x.astype(BF16)
    return high, (x - high.astype(F32)).astype(BF16)


def dot(x, y, dims):
    return lax.dot_general(x, y, ((dims[:1], dims[1:]), ((), ())), preferred_element_type=F32)


def dot3(x, y, dims):
    return dot(x[0], y[0], dims) + (dot(x[0], y[1], dims) + dot(x[1], y[0], dims))


def relayout_kernel(observed, sent):
    homes = observed.shape[3]
    for k in range(2):
        for q in range(3):
            for c in range(4):
                sent[pl.ds(12 * k + 4 * q + c, homes, stride=24), :] = observed[k, 0, q, :, pl.ds(128 * c, 128)]


def relayout(observed):
    turned = jnp.transpose(observed, (0, 1, 3, 2, 4))
    homes = turned.shape[3]
    sent = pl.pallas_call(
        relayout_kernel,
        grid=(1,),
        in_specs=[whole(turned.shape)],
        out_specs=whole((homes * 24, 128)),
        out_shape=struct(homes * 24, 128),
        compiler_params=params(16),
        name="relayout",
    )(*in_hbm(turned))
    return sent.reshape(homes, 24, 128)


PADDED = 640


def column_of(row):
    square = (SND, SND)
    here = lax.broadcasted_iota(I32, square, 0) == lax.broadcasted_iota(I32, square, 1)
    return jnp.sum(jnp.where(here, jnp.broadcast_to(row, square), 0), axis=1, keepdims=True)


def load_table(table, high, low):
    count = table.shape[0]
    full = count // 16 * 16
    high[pl.ds(0, full), :], low[pl.ds(0, full), :] = split(table[pl.ds(0, full), :])
    rest = jnp.zeros((PADDED - full, table.shape[1]), F32)
    if count > full:
        zeros = jnp.zeros((PADDED - count, table.shape[1]), F32)
        rest = jnp.concatenate([table[pl.ds(full, count - full), :], zeros], axis=0)
    high[pl.ds(full, PADDED - full), :], low[pl.ds(full, PADDED - full), :] = split(rest)


def observe_kernel(cells, owners, channels, weight, field, *refs, slot):
    flip = jnp.where(lat_even(), 3, 0)
    square = (SND, SND)
    row_id = lax.broadcasted_iota(I32, square, 0)
    lane_id = lax.broadcasted_iota(I32, square, 1)
    copies = []
    if slot == 0:
        hbm, refs = refs[:3], refs[3:]
        (out, strip, first, second, *tables, late_totals, late_times), refs = refs[:10], refs[10:]
        (absorb_table, emit_table, fetched), sems = refs[:3], refs[3]
        for n, target in enumerate((absorb_table, emit_table, fetched)):
            copies.append(pltpu.make_async_copy(hbm[n], target, sems.at[n]))
            copies[n].start()
        entry = lax.broadcasted_iota(I32, (PADDED, channels.shape[1]), 0)
        listed = (entry == channels[...]).astype(F32).astype(BF16)
        times = dot(jnp.ones((8, channels.shape[1]), BF16), listed, (1, 1))
        late_times[...] = times
        times = times[0:1]
    else:
        tables, early_totals, early_times = refs[:4], refs[4], refs[5]
        before, (out, strip, first, second) = refs[6:9], refs[9:13]
        times = early_times[0:1, :]

    def observed_totals(which):
        owner_row = owners[which : which + 1, :]
        owner = column_of(owner_row)
        earlier = (owner == owner_row) & (lane_id < row_id)
        rank = jnp.sum(jnp.where(earlier, 1, 0), axis=1, keepdims=True)
        choices = [((owner == lane_id) & (rank == q)).astype(F32).astype(BF16) for q in range(3)]
        parts = []
        for c in range(4):
            part = [jnp.zeros(square, F32)] * 2
            for q in range(3):
                seen = split(fetched[pl.ds(12 * which + 4 * q + c, SND, stride=24), :])
                part = [p + dot(choices[q], x, (1, 0)) for p, x in zip(part, seen, strict=True)]
            parts.append(part)
        wanted = [jnp.concatenate([part[n] for part in parts], axis=1).astype(BF16) for n in range(2)]
        return dot(wanted[0], listed, (1, 1)) + dot(wanted[1], listed, (1, 1))

    cell = column_of(cells[slot : slot + 1, :])
    picks = [(cell == lane_id + 128 * jnp.abs(flip - r)).astype(F32).astype(BF16) for r in range(4)]
    pieces = [jnp.zeros((SND, VARS * LEV), F32)] * 2
    for r in range(4):
        x = split(field[r, 0:VARS].reshape(VARS * LEV, 128))
        pieces = [piece + dot(picks[r], part, (1, 1)) for piece, part in zip(pieces, x, strict=True)]
    column = [piece.astype(BF16) for piece in pieces]
    if slot == 0:
        for n, table in enumerate((absorb_table, emit_table)):
            copies[n].wait()
            load_table(table, tables[2 * n], tables[2 * n + 1])
    absorb = (tables[0][...], tables[1][...])
    emission = (tables[2][...], tables[3][...])
    optical = dot3(column, absorb, (1, 1))
    bright = dot3(column, emission, (1, 1))
    decay = jnp.exp(-jnp.abs(optical))
    inverse = 1.0 / (1.0 + decay)
    rest = decay * inverse
    positive = optical >= 0
    passing = jnp.where(positive, rest, inverse)
    opaque = jnp.where(positive, inverse, rest)
    if slot == 0:
        copies[2].wait()
        totals = observed_totals(0)
        late_totals[...] = observed_totals(1)
    else:
        totals = early_totals[...]
    evolved = passing * bright
    departure = weight[...] * (times * evolved - totals)
    to_bright = departure * passing
    to_optical = -(departure * evolved * opaque)
    column = dot3(split(to_optical), absorb, (1, 0)) + dot3(split(to_bright), emission, (1, 0))
    ch, cl = split(column)
    for r in range(4):
        placed = dot(ch, picks[r], (0, 0)) + dot(cl, picks[r], (0, 0))
        out[r] = placed.reshape(VARS, LEV, 128)

    even = lon_even()
    if slot == 1:
        strip[:, 2:4] = before[0][...]
        first[2:4] = before[1][...]
        second[2:4] = before[2][...]

    def strips_of(t, level):
        for b in range(2):
            strips = []
            for r in range(4):
                s = own_strip(lambda g: out[r, 4 * b + g, level, :], 4)
                strip[r, b, level, :] = s
                strips.append(s)
            first[b, level, :], second[b, level, :] = pack_strips(strips, even)

    level_tiles(LEV // STRIP_SPAN, strips_of, STRIP_SPAN)


def observe(slot, small, field, inputs, before):
    count = 2 if slot == 0 else 4
    shapes = [struct(4, 8, LEV, 128), struct(4, count, LEV, 128)] + [struct(count, LEV, 128)] * 2
    scratch = []
    specs = [VMEM_SPEC] * len(inputs)
    if slot == 0:
        shapes += [struct(PADDED, VARS * LEV, dtype=BF16)] * 4 + [struct(SND, PADDED), struct(8, PADDED)]
        scratch = [pltpu.VMEM(x.shape, F32) for x in inputs] + [pltpu.SemaphoreType.DMA((len(inputs),))]
        specs = [pl.BlockSpec(memory_space=pltpu.HBM)] * len(inputs)
        inputs = in_hbm(*inputs)
    return pl.pallas_call(
        partial(observe_kernel, slot=slot),
        in_specs=[VMEM_SPEC] * (len(small) + 1) + specs + [VMEM_SPEC] * len(before),
        out_specs=[VMEM_SPEC] * len(shapes),
        out_shape=shapes,
        scratch_shapes=scratch,
        compiler_params=params(10),
        name="observe",
    )(*small, field, *inputs, *before)


def swap(x, axis, parity, wrap):
    devices = lax.axis_size(axis)
    pairs = []
    for i in range(parity, devices, 2):
        if i + 1 < devices or wrap:
            j = (i + 1) % devices
            pairs += [(i, j), (j, i)]
    return lax.ppermute(x, axis, pairs)


def lat_swap(x, width=4):
    beyond = swap(x[4 - width :], "lat", 1, False)
    return swap(x[:width], "lat", 0, False), beyond


def lon_swap(first, second):
    beyond = swap(second, "lon", 1, True)
    return swap(first, "lon", 0, True), beyond


def per_device(
    state, winds, diffusivity, sounding_cell, sounding_owner, step_counts, channel_list, absorb_table, emit_table,
    obs_weight, observed,
):
    def by_steps(slot, run):
        branches = [partial(run, width) for width in range(1, MAXSTEP + 1)]
        return lax.switch(step_counts[slot] - 1, branches)

    main, strip, first, second = pack(state.reshape(8, 256, 128), winds.reshape(2, 256, 128), diffusivity)
    received = lon_swap(first, second)
    halo = lat_swap(main)
    sent, received = lax.optimization_barrier((relayout(observed), received))
    (strip,) = complete(strip, *received, 1)
    fetched = lax.all_to_all(sent, ("lon", "lat"), split_axis=0, concat_axis=0, tiled=True)
    tile, strips = (main, *halo), (strip, *lat_swap(strip))
    onward, raw = coefficients(tile, strips)
    both0 = advect(step_counts[:1], tile, strips, onward, "both")
    halo = lat_swap(both0)
    late = raw, both0, obs_weight, sounding_owner
    raw, both0, obs_weight, sounding_owner = lax.optimization_barrier(late)
    backward_coef = adjoint_coefficients(onward, raw)

    extra = PADDED - obs_weight.shape[0]
    padded_weight = jnp.pad(obs_weight, (0, extra))[None, :]
    small = [sounding_cell, sounding_owner[:, :, 0], channel_list[None, :], padded_weight]
    tables = [absorb_table.T, emit_table.T, fetched.reshape(-1, 128)]
    g0, *rest = observe(0, small, both0, tables, [])
    both0, backward_coef, g0 = lax.optimization_barrier((both0, backward_coef, g0))
    field1 = advect(step_counts[1:], (both0, *halo), None, onward, "main")
    g1, strip, first, second = observe(1, small, field1, rest[3:], rest[:3])

    def backward(width):
        received = lon_swap(first, second)
        halo = lat_swap(g1, width)
        strips1, strips0 = complete(strip, *received, 2)
        halo_strips = lat_swap(strips1, width)
        return advect(width, (g1, *halo), (strips1, *halo_strips), backward_coef, "both", (g0, strips0))

    both = by_steps(1, backward)

    def last(width):
        return advect(width, (both, *lat_swap(both, width)), None, backward_coef, "native")

    result = by_steps(0, last)
    return result.reshape(state.shape)


def solution(mesh):
    return jax.shard_map(
        per_device,
        mesh=mesh,
        in_specs=(
            P(None, None, "lat", "lon"),
            P(None, None, "lat", "lon"),
            P("lat", "lon"),
            P(None, ("lon", "lat")),
            P(None, ("lon", "lat"), None),
            P(),
            P(),
            P(),
            P(),
            P(),
            P(None, ("lon", "lat"), None, None, None),
        ),
        out_specs=P(None, None, "lat", "lon"),
        check_vma=False,
    )
```

```python
from functools import partial

import jax
import jax.numpy as jnp
from jax import lax
from jax.experimental import pallas as pl
from jax.experimental.pallas import tpu as pltpu
from jax.sharding import PartitionSpec as P

F32 = jnp.float32
BF16 = jnp.bfloat16
I32 = jnp.int32
VARS = 8
SPAN = 32
STRIP_SPAN = 32
LEV = 64
MAXSTEP = 4
SND = 128


def struct(*shape, dtype=F32):
    return jax.ShapeDtypeStruct(shape, dtype)


def tiled(grid, *shape):
    zeros = (0,) * (len(shape) - 2)
    return pl.BlockSpec((*shape[:-2], shape[-2] // grid, shape[-1]), lambda t: (*zeros, t, 0))


def whole(shape):
    return pl.BlockSpec(shape, lambda *_: (0,) * len(shape))


VMEM_SPEC = pl.BlockSpec(memory_space=pltpu.VMEM)
SMEM_SPEC = pl.BlockSpec(memory_space=pltpu.SMEM)


def params(mebibytes):
    return pltpu.CompilerParams(vmem_limit_bytes=mebibytes * 1024 * 1024)


def in_hbm(*arrays):
    return [pltpu.with_memory_space_constraint(x, pltpu.HBM) for x in arrays]


def lanes():
    return lax.broadcasted_iota(I32, (STRIP_SPAN, 128), 1)


def roll(x, shift):
    shift = shift % 128
    return x if shift == 0 else pltpu.roll(x, shift, 1)


def level_tiles(count, body, span=8):
    def step(t, carry):
        body(t, pl.ds(pl.multiple_of(t * span, span), span))
        return carry

    lax.fori_loop(0, count, step, 0)


def lon_even():
    return lax.axis_index("lon") % 2 == 0


def lat_even():
    return lax.axis_index("lat") % 2 == 0


def own_strip(load, count):
    lane = lanes()
    strip = jnp.zeros((STRIP_SPAN, 128), F32)
    for g in range(count):
        x = load(g)
        base = 32 * g
        strip = jnp.where((lane >= base + 8) & (lane < base + 16), roll(x, base + 8), strip)
        strip = jnp.where((lane >= base + 16) & (lane < base + 24), roll(x, base + 24), strip)
    return strip


def pack_strips(strips, even):
    lane = lanes() % 32
    east = jnp.zeros((STRIP_SPAN, 128), F32)
    west = jnp.zeros((STRIP_SPAN, 128), F32)
    for r in range(4):
        here = (lane >= 8 * r) & (lane < 8 * r + 8)
        east = jnp.where(here, roll(strips[r], 8 * r - 16), east)
        west = jnp.where(here, roll(strips[r], 8 * r - 8), west)
    return jnp.where(even, east, west), jnp.where(even, west, east)


def pack_kernel(state, winds, diff, main, strip, first, second, *, grid):
    even = lon_even()
    flip = jnp.where(lat_even(), 3, 0)

    def body(t, level):
        strips = [[] for _ in range(3)]
        for p in range(4):
            r = jnp.abs(flip - p)
            source = pl.ds(t * 4 * STRIP_SPAN + r, STRIP_SPAN, stride=4)
            row = [state[v, source, :] for v in range(VARS)] + [winds[v, source, :] for v in range(2)]
            row.append(jnp.broadcast_to(diff[pl.ds(r, 1), :], (STRIP_SPAN, 128)))
            for v in range(11):
                main[p, v, level, :] = row[v]
            for b in range(3):
                s = own_strip(lambda g: row[4 * b + g], 4 if b < 2 else 3)
                strip[p, b, level, :] = s
                strips[b].append(s)
        for b in range(3):
            first[b, level, :], second[b, level, :] = pack_strips(strips[b], even)

    level_tiles(LEV // STRIP_SPAN // grid, body, STRIP_SPAN)


def pack(state, winds, diff, grid=2):
    shapes = [(4, 11, LEV, 128), (4, 3, LEV, 128), (3, LEV, 128), (3, LEV, 128)]
    return pl.pallas_call(
        partial(pack_kernel, grid=grid),
        grid=(grid,),
        in_specs=[tiled(grid, 8, 256, 128), tiled(grid, 2, 256, 128), whole((4, 128))],
        out_specs=[tiled(grid, *s) for s in shapes],
        out_shape=[struct(*s) for s in shapes],
        compiler_params=params(16),
        name="pack",
    )(*in_hbm(state, winds, diff))


def complete_kernel(strip, first, second, *outs):
    even = lon_even()
    blocks = strip.shape[1]
    split = blocks // len(outs)

    def body(t, level):
        lane = lax.broadcasted_iota(I32, (SPAN, 128), 1) % 32
        for b in range(blocks):
            one, two = first[b, level, :], second[b, level, :]
            east = jnp.where(even, one, two)
            west = jnp.where(even, two, one)
            for r in range(4):
                full = jnp.where(lane < 8, roll(west, -8 * r), strip[r, b, level, :])
                outs[b // split][r, b % split, level, :] = jnp.where(lane >= 24, roll(east, 24 - 8 * r), full)

    level_tiles(LEV // SPAN, body, SPAN)


def complete(strip, first, second, parts):
    split = strip.shape[1] // parts
    return pl.pallas_call(
        complete_kernel,
        in_specs=[VMEM_SPEC] * 3,
        out_specs=[VMEM_SPEC] * parts,
        out_shape=[struct(4, split, LEV, 128)] * parts,
        compiler_params=params(4),
        name="complete",
    )(strip, first, second)


def open_to_next_chip():
    lat = lax.axis_index("lat")
    return jnp.where((lat > 0) & (lat < lax.axis_size("lat") - 1), 1.0, 0.0).astype(F32)


def each_row(first, last, body):
    def step(i, carry):
        body(i)
        return carry

    lax.fori_loop(first, last, step, 0)


def coefficient_kernel(own, r0, r1, sown, s0, s1, out, raw, beside, beyond):
    flipped = lat_even()
    open_side = open_to_next_chip()
    lane = lax.broadcasted_iota(I32, (LEV, 128), 1)
    beside[...] = s0[:, 0:2]
    beyond[...] = s1[:, 0:2]

    def fill(i, main, strip):
        packed = strip[2]
        spread = []
        for g in range(3):
            one = jnp.where(lane < 32, roll(packed, -32 * g), 0.0)
            one = one + roll(one, 32)
            spread.append(one + roll(one, 64))
        plain = [main[VARS], main[VARS + 1], main[VARS + 2]]
        for n, (w0, w1, dd) in enumerate((plain, spread)):
            half = w0 * 0.5
            half_west, dd_west = roll(half, 1), roll(dd, 1)
            if n == 0:
                half_west = jnp.where(lane == 0, roll(spread[0], 121) * 0.5, half_west)
                dd_west = jnp.where(lane == 0, roll(spread[2], 121), dd_west)
            lat_half = w1 * 0.5
            values = half + dd, half - dd, half_west + dd_west, half_west - dd_west, lat_half + dd, lat_half - dd
            for m, value in enumerate(values):
                raw[i, 6 * n + m] = value

    for first, target, main, strip in ((0, 3, r0, s0), (4, 4, own, sown), (8, 11, r1, s1)):
        way = 1 if first == 4 else -1

        def two(j):
            for q in (2 * j, 2 * j + 1):
                row = 3 - q if first == 8 else q
                fill(first + q if first == 8 else target + way * q, main.at[row], strip.at[row])

        each_row(0, 2, two)

    def combine(i):
        scale = jnp.where(i >= 8, open_side, 1.0)
        for n in range(2):
            a, b, a_west, b_west = (raw[i, 6 * n + m] for m in range(4))
            u, w = interface(raw, flipped, i, n)
            u_before, w_before = interface(raw, flipped, i - 1, n)
            values = 1.0 - a + b_west - u + w_before, -b, a_west, -w, u_before
            for m, value in enumerate(values):
                out[i, 5 * n + m] = value * scale

    each_row(1, 11, combine)


def interface(raw, flipped, i, n):
    u = jnp.where(flipped, -raw[i + 1, 6 * n + 5], raw[i, 6 * n + 4])
    w = jnp.where(flipped, -raw[i + 1, 6 * n + 4], raw[i, 6 * n + 5])
    return u, w


def coefficients(tile, strips):
    return pl.pallas_call(
        coefficient_kernel,
        in_specs=[VMEM_SPEC] * 6,
        out_specs=[VMEM_SPEC] * 4,
        out_shape=[struct(12, 10, LEV, 128), struct(12, 12, LEV, 128)] + [struct(4, 2, LEV, 128)] * 2,
        compiler_params=params(4),
        name="coefficients",
    )(*tile, *strips)


def adjoint_kernel(forward, raw, out):
    flipped = lat_even()
    open_side = open_to_next_chip()

    def combine(i):
        scale = jnp.where(i >= 8, open_side, 1.0)
        for n in range(2):
            out[i, 5 * n] = forward[i, 5 * n]
            out[i, 5 * n + 1] = raw[i, 6 * n] * scale
            out[i, 5 * n + 2] = -raw[i, 6 * n + 3] * scale
            out[i, 5 * n + 3] = interface(raw, flipped, i, n)[0] * scale
            out[i, 5 * n + 4] = -interface(raw, flipped, i - 1, n)[1] * scale

    each_row(1, 11, combine)


def adjoint_coefficients(forward, raw):
    return pl.pallas_call(
        adjoint_kernel,
        in_specs=[VMEM_SPEC] * 2,
        out_specs=VMEM_SPEC,
        out_shape=struct(12, 10, LEV, 128),
        compiler_params=params(4),
        name="adjoint_coefficients",
    )(forward, raw)


def advect_kernel(*refs, steps, slot, apart, result, addend):
    refs = list(refs)
    steps = refs.pop(0)[slot] if steps is None else steps
    own, r0, r1 = refs[:3]
    refs = refs[3:]
    strips = ()
    if apart:
        strips, refs = refs[:3], refs[3:]
    coef = refs.pop(0)
    if addend:
        add_main, add_strip = refs[:2]
        refs = refs[2:]
    out, *work, shift = refs
    source = lax.broadcasted_iota(I32, (256, 256), 0) % 128
    target = lax.broadcasted_iota(I32, (256, 256), 1)
    chosen = jnp.where(target < 128, target + 1, target + 127) % 128
    shift[...] = (source == chosen).astype(F32).astype(BF16)
    flip = jnp.where(lat_even(), 3, 0)
    width = r0.shape[0]

    def place(target, sources, offset, count):
        tile, intra, inter = sources

        def halo(j, carry):
            target[3 - j, offset : offset + count] = intra[j, 0:count]
            target[8 + j, offset : offset + count] = inter[width - 1 - j, 0:count]
            return carry

        def inside(j, carry):
            target[4 + j, offset : offset + count] = tile[j, 0:count]
            return carry

        lax.fori_loop(0, width, halo, 0)
        lax.fori_loop(0, 4, inside, 0)

    def start(target):
        if apart:
            place(target, (own, r0, r1), 0, VARS)
            place(target, strips, VARS, 2)
        else:
            place(target, (own, r0, r1), 0, VARS + 2)

    def when(condition, run):
        if isinstance(condition, bool):
            if condition:
                run()
        else:
            pl.when(condition)(run)

    for n in range(2):
        when(steps % 2 != n, partial(start, work[n]))
    lane = lax.broadcasted_iota(I32, (LEV, 128), 1)

    def row(now, i, last, store):
        def stencil(n, v, f, east, west):
            value = coef[i, n] * f
            value = value + coef[i, n + 1] * east
            value = value + coef[i, n + 2] * west
            value = value + coef[i, n + 3] * now[i + 1, v]
            return value + coef[i, n + 4] * now[i - 1, v]

        wanted = VARS + (0 if last and result != "both" else 2)
        halves = split(now[i, 0:wanted].reshape(wanted * LEV, 128))
        moved = dot(jnp.concatenate(halves, axis=1), shift[...], (1, 0))
        moved = moved.reshape(wanted, LEV, 256)
        for b in range(2):
            f = now[i, VARS + b]
            ends = jnp.where(lane % 32 == 25, roll(f, 18), f)
            for v in (VARS + b, *range(4 * b, 4 * b + 4)):
                if v >= wanted:
                    continue
                f = now[i, v]
                east, west = moved[v, :, :128], moved[v, :, 128:]
                if v < VARS:
                    rim = roll(ends, 103 - 32 * (v % 4))
                    east = jnp.where(lane == 127, rim, east)
                    west = jnp.where(lane == 0, rim, west)
                store(v, stencil(5 if v >= VARS else 0, v, f, east, west))

    def step(reach):
        def two(j, carry):
            for i in (4 - reach + 2 * j, 5 - reach + 2 * j):

                def store(v, value):
                    work[1 - reach % 2][i, v] = value

                row(work[reach % 2], i, False, store)
            return carry

        lax.fori_loop(0, 2 + reach, two, 0)

    for reach in (3, 2, 1):
        when(steps > reach, partial(step, reach))

    def final(r, carry):
        def store(v, value):
            if addend:
                value = value + (add_main[r, v] if v < VARS else add_strip[r, v - VARS])
            if result == "native":
                out[v, pl.ds(jnp.abs(flip - r), LEV, stride=4), :] = value
            else:
                out[r, v] = value

        row(work[0], 4 + r, True, store)
        return carry

    lax.fori_loop(0, 4, final, 0)


def advect(steps, tile, strips, coef, result, addend=None, slot=0):
    args = [*tile]
    if strips is not None:
        args += strips
    args.append(coef)
    if addend is not None:
        args += addend
    if result == "native":
        shape = (8, 256, 128)
    else:
        shape = (4, 10 if result == "both" else 8, LEV, 128)
    static = isinstance(steps, int)
    return pl.pallas_call(
        partial(
            advect_kernel,
            steps=steps if static else None,
            slot=slot,
            apart=strips is not None,
            result=result,
            addend=addend is not None,
        ),
        in_specs=([] if static else [SMEM_SPEC]) + [VMEM_SPEC] * len(args),
        out_specs=VMEM_SPEC,
        out_shape=struct(*shape),
        scratch_shapes=[pltpu.VMEM((12, 10, LEV, 128), F32)] * 2 + [pltpu.VMEM((256, 256), BF16)],
        compiler_params=params(14),
        name="advect_" + result,
    )(*([] if static else [steps]), *args)


def split(x):
    high = x.astype(BF16)
    return high, (x - high.astype(F32)).astype(BF16)


def dot(x, y, dims):
    return lax.dot_general(x, y, ((dims[:1], dims[1:]), ((), ())), preferred_element_type=F32)


def dot3(x, y, dims):
    return dot(x[0], y[0], dims) + (dot(x[0], y[1], dims) + dot(x[1], y[0], dims))


def relayout_kernel(observed, sent):
    homes = observed.shape[3]
    for k in range(2):
        for q in range(3):
            for c in range(4):
                sent[pl.ds(12 * k + 4 * q + c, homes, stride=24), :] = observed[k, 0, q, :, pl.ds(128 * c, 128)]


def relayout(observed):
    turned = jnp.transpose(observed, (0, 1, 3, 2, 4))
    homes = turned.shape[3]
    sent = pl.pallas_call(
        relayout_kernel,
        grid=(1,),
        in_specs=[whole(turned.shape)],
        out_specs=whole((homes * 24, 128)),
        out_shape=struct(homes * 24, 128),
        compiler_params=params(16),
        name="relayout",
    )(*in_hbm(turned))
    return sent.reshape(homes, 24, 128)


PADDED = 640


def column_of(row):
    square = (SND, SND)
    here = lax.broadcasted_iota(I32, square, 0) == lax.broadcasted_iota(I32, square, 1)
    return jnp.sum(jnp.where(here, jnp.broadcast_to(row, square), 0), axis=1, keepdims=True)


def load_table(table, high, low):
    count = table.shape[0]
    full = count // 16 * 16
    high[pl.ds(0, full), :], low[pl.ds(0, full), :] = split(table[pl.ds(0, full), :])
    rest = jnp.zeros((PADDED - full, table.shape[1]), F32)
    if count > full:
        zeros = jnp.zeros((PADDED - count, table.shape[1]), F32)
        rest = jnp.concatenate([table[pl.ds(full, count - full), :], zeros], axis=0)
    high[pl.ds(full, PADDED - full), :], low[pl.ds(full, PADDED - full), :] = split(rest)


def observe_kernel(cells, owners, channels, weight, field, *refs, slot):
    flip = jnp.where(lat_even(), 3, 0)
    square = (SND, SND)
    row_id = lax.broadcasted_iota(I32, square, 0)
    lane_id = lax.broadcasted_iota(I32, square, 1)
    copies = []
    if slot == 0:
        hbm, refs = refs[:3], refs[3:]
        (out, strip, first, second, *tables, late_totals, late_times), refs = refs[:10], refs[10:]
        (absorb_table, emit_table, fetched), sems = refs[:3], refs[3]
        for n, target in enumerate((absorb_table, emit_table, fetched)):
            copies.append(pltpu.make_async_copy(hbm[n], target, sems.at[n]))
            copies[n].start()
        entry = lax.broadcasted_iota(I32, (PADDED, channels.shape[1]), 0)
        listed = (entry == channels[...]).astype(F32).astype(BF16)
        times = dot(jnp.ones((8, channels.shape[1]), BF16), listed, (1, 1))
        late_times[...] = times
        times = times[0:1]
    else:
        tables, early_totals, early_times = refs[:4], refs[4], refs[5]
        before, (out, strip, first, second) = refs[6:9], refs[9:13]
        times = early_times[0:1, :]

    def observed_totals(which):
        owner_row = owners[which : which + 1, :]
        owner = column_of(owner_row)
        earlier = (owner == owner_row) & (lane_id < row_id)
        rank = jnp.sum(jnp.where(earlier, 1, 0), axis=1, keepdims=True)
        choices = [((owner == lane_id) & (rank == q)).astype(F32).astype(BF16) for q in range(3)]
        parts = []
        for c in range(4):
            part = [jnp.zeros(square, F32)] * 2
            for q in range(3):
                seen = split(fetched[pl.ds(12 * which + 4 * q + c, SND, stride=24), :])
                part = [p + dot(choices[q], x, (1, 0)) for p, x in zip(part, seen, strict=True)]
            parts.append(part)
        wanted = [jnp.concatenate([part[n] for part in parts], axis=1).astype(BF16) for n in range(2)]
        return dot(wanted[0], listed, (1, 1)) + dot(wanted[1], listed, (1, 1))

    cell = column_of(cells[slot : slot + 1, :])
    picks = [(cell == lane_id + 128 * jnp.abs(flip - r)).astype(F32).astype(BF16) for r in range(4)]
    pieces = [jnp.zeros((SND, VARS * LEV), F32)] * 2
    for r in range(4):
        x = split(field[r, 0:VARS].reshape(VARS * LEV, 128))
        pieces = [piece + dot(picks[r], part, (1, 1)) for piece, part in zip(pieces, x, strict=True)]
    column = [piece.astype(BF16) for piece in pieces]
    if slot == 0:
        for n, table in enumerate((absorb_table, emit_table)):
            copies[n].wait()
            load_table(table, tables[2 * n], tables[2 * n + 1])
    absorb = (tables[0][...], tables[1][...])
    emission = (tables[2][...], tables[3][...])
    optical = dot3(column, absorb, (1, 1))
    bright = dot3(column, emission, (1, 1))
    decay = jnp.exp(-jnp.abs(optical))
    inverse = 1.0 / (1.0 + decay)
    rest = decay * inverse
    positive = optical >= 0
    passing = jnp.where(positive, rest, inverse)
    opaque = jnp.where(positive, inverse, rest)
    if slot == 0:
        copies[2].wait()
        totals = observed_totals(0)
        late_totals[...] = observed_totals(1)
    else:
        totals = early_totals[...]
    evolved = passing * bright
    departure = weight[...] * (times * evolved - totals)
    to_bright = departure * passing
    to_optical = -(departure * evolved * opaque)
    column = dot3(split(to_optical), absorb, (1, 0)) + dot3(split(to_bright), emission, (1, 0))
    ch, cl = split(column)
    for r in range(4):
        placed = dot(ch, picks[r], (0, 0)) + dot(cl, picks[r], (0, 0))
        out[r] = placed.reshape(VARS, LEV, 128)

    even = lon_even()
    if slot == 1:
        strip[:, 2:4] = before[0][...]
        first[2:4] = before[1][...]
        second[2:4] = before[2][...]

    def strips_of(t, level):
        for b in range(2):
            strips = []
            for r in range(4):
                s = own_strip(lambda g: out[r, 4 * b + g, level, :], 4)
                strip[r, b, level, :] = s
                strips.append(s)
            first[b, level, :], second[b, level, :] = pack_strips(strips, even)

    level_tiles(LEV // STRIP_SPAN, strips_of, STRIP_SPAN)


def observe(slot, small, field, inputs, before):
    count = 2 if slot == 0 else 4
    shapes = [struct(4, 8, LEV, 128), struct(4, count, LEV, 128)] + [struct(count, LEV, 128)] * 2
    scratch = []
    specs = [VMEM_SPEC] * len(inputs)
    if slot == 0:
        shapes += [struct(PADDED, VARS * LEV, dtype=BF16)] * 4 + [struct(SND, PADDED), struct(8, PADDED)]
        scratch = [pltpu.VMEM(x.shape, F32) for x in inputs] + [pltpu.SemaphoreType.DMA((len(inputs),))]
        specs = [pl.BlockSpec(memory_space=pltpu.HBM)] * len(inputs)
        inputs = in_hbm(*inputs)
    return pl.pallas_call(
        partial(observe_kernel, slot=slot),
        in_specs=[VMEM_SPEC] * (len(small) + 1) + specs + [VMEM_SPEC] * len(before),
        out_specs=[VMEM_SPEC] * len(shapes),
        out_shape=shapes,
        scratch_shapes=scratch,
        compiler_params=params(10),
        name="observe",
    )(*small, field, *inputs, *before)


def swap(x, axis, parity, wrap):
    devices = lax.axis_size(axis)
    pairs = []
    for i in range(parity, devices, 2):
        if i + 1 < devices or wrap:
            j = (i + 1) % devices
            pairs += [(i, j), (j, i)]
    return lax.ppermute(x, axis, pairs)


def lat_swap(x, width=4):
    beyond = swap(x[4 - width :], "lat", 1, False)
    return swap(x[:width], "lat", 0, False), beyond


def lon_swap(first, second):
    beyond = swap(second, "lon", 1, True)
    return swap(first, "lon", 0, True), beyond


def per_device(
    state, winds, diffusivity, sounding_cell, sounding_owner, step_counts, channel_list, absorb_table, emit_table,
    obs_weight, observed,
):
    def by_steps(slot, run):
        branches = [partial(run, width) for width in range(1, MAXSTEP + 1)]
        return lax.switch(step_counts[slot] - 1, branches)

    main, strip, first, second = pack(state.reshape(8, 256, 128), winds.reshape(2, 256, 128), diffusivity)
    received = lon_swap(first, second)
    halo = lat_swap(main)
    sent, received = lax.optimization_barrier((relayout(observed), received))
    (strip,) = complete(strip, *received, 1)
    fetched = lax.all_to_all(sent, ("lon", "lat"), split_axis=0, concat_axis=0, tiled=True)
    tile, strips = (main, *halo), (strip, *lat_swap(strip))
    onward, raw, *halo_strips = coefficients(tile, strips)
    strips = strips[0], *halo_strips
    both0 = advect(step_counts, tile, strips, onward, "both")
    halo = lat_swap(both0)
    late = raw, both0, obs_weight, sounding_owner
    raw, both0, obs_weight, sounding_owner = lax.optimization_barrier(late)
    backward_coef = adjoint_coefficients(onward, raw)

    extra = PADDED - obs_weight.shape[0]
    padded_weight = jnp.pad(obs_weight, (0, extra))[None, :]
    small = [sounding_cell, sounding_owner[:, :, 0], channel_list[None, :], padded_weight]
    tables = [absorb_table.T, emit_table.T, fetched.reshape(-1, 128)]
    g0, *rest = observe(0, small, both0, tables, [])
    both0, backward_coef, g0 = lax.optimization_barrier((both0, backward_coef, g0))
    field1 = advect(step_counts, (both0, *halo), None, onward, "main", slot=1)
    g1, strip, first, second = observe(1, small, field1, rest[3:], rest[:3])

    def backward(width):
        received = lon_swap(first, second)
        halo = lat_swap(g1, width)
        strips1, strips0 = complete(strip, *received, 2)
        halo_strips = lat_swap(strips1, width)
        return advect(width, (g1, *halo), (strips1, *halo_strips), backward_coef, "both", (g0, strips0))

    both = by_steps(1, backward)

    def last(width):
        return advect(width, (both, *lat_swap(both, width)), None, backward_coef, "native")

    result = by_steps(0, last)
    return result.reshape(state.shape)


def solution(mesh):
    return jax.shard_map(
        per_device,
        mesh=mesh,
        in_specs=(
            P(None, None, "lat", "lon"),
            P(None, None, "lat", "lon"),
            P("lat", "lon"),
            P(None, ("lon", "lat")),
            P(None, ("lon", "lat"), None),
            P(),
            P(),
            P(),
            P(),
            P(),
            P(None, ("lon", "lat"), None, None, None),
        ),
        out_specs=P(None, None, "lat", "lon"),
        check_vma=False,
    )
```

```python
from functools import partial

import jax
import jax.numpy as jnp
from jax import lax
from jax.experimental import pallas as pl
from jax.experimental.pallas import tpu as pltpu
from jax.sharding import PartitionSpec as P

F32 = jnp.float32
BF16 = jnp.bfloat16
I32 = jnp.int32
VARS = 8
SPAN = 32
STRIP_SPAN = 32
LEV = 64
MAXSTEP = 4
SND = 128


def struct(*shape, dtype=F32):
    return jax.ShapeDtypeStruct(shape, dtype)


def tiled(grid, *shape):
    zeros = (0,) * (len(shape) - 2)
    return pl.BlockSpec((*shape[:-2], shape[-2] // grid, shape[-1]), lambda t: (*zeros, t, 0))


def whole(shape):
    return pl.BlockSpec(shape, lambda *_: (0,) * len(shape))


VMEM_SPEC = pl.BlockSpec(memory_space=pltpu.VMEM)
SMEM_SPEC = pl.BlockSpec(memory_space=pltpu.SMEM)


def params(mebibytes):
    return pltpu.CompilerParams(vmem_limit_bytes=mebibytes * 1024 * 1024)


def in_hbm(*arrays):
    return [pltpu.with_memory_space_constraint(x, pltpu.HBM) for x in arrays]


def lanes():
    return lax.broadcasted_iota(I32, (STRIP_SPAN, 128), 1)


def roll(x, shift):
    shift = shift % 128
    return x if shift == 0 else pltpu.roll(x, shift, 1)


def level_tiles(count, body, span=8):
    def step(t, carry):
        body(t, pl.ds(pl.multiple_of(t * span, span), span))
        return carry

    lax.fori_loop(0, count, step, 0)


def lon_even():
    return lax.axis_index("lon") % 2 == 0


def lat_even():
    return lax.axis_index("lat") % 2 == 0


def own_strip(load, count):
    lane = lanes()
    strip = jnp.zeros((STRIP_SPAN, 128), F32)
    for g in range(count):
        x = load(g)
        base = 32 * g
        strip = jnp.where((lane >= base + 8) & (lane < base + 16), roll(x, base + 8), strip)
        strip = jnp.where((lane >= base + 16) & (lane < base + 24), roll(x, base + 24), strip)
    return strip


def pack_strips(strips, even):
    lane = lanes() % 32
    east = jnp.zeros((STRIP_SPAN, 128), F32)
    west = jnp.zeros((STRIP_SPAN, 128), F32)
    for r in range(4):
        here = (lane >= 8 * r) & (lane < 8 * r + 8)
        east = jnp.where(here, roll(strips[r], 8 * r - 16), east)
        west = jnp.where(here, roll(strips[r], 8 * r - 8), west)
    return jnp.where(even, east, west), jnp.where(even, west, east)


def pack_kernel(state, winds, diff, main, strip, first, second, *, grid):
    even = lon_even()
    flip = jnp.where(lat_even(), 3, 0)

    def body(t, level):
        strips = [[] for _ in range(3)]
        for p in range(4):
            r = jnp.abs(flip - p)
            source = pl.ds(t * 4 * STRIP_SPAN + r, STRIP_SPAN, stride=4)
            row = [state[v, source, :] for v in range(VARS)] + [winds[v, source, :] for v in range(2)]
            row.append(jnp.broadcast_to(diff[pl.ds(r, 1), :], (STRIP_SPAN, 128)))
            for v in range(11):
                main[p, v, level, :] = row[v]
            for b in range(3):
                s = own_strip(lambda g: row[4 * b + g], 4 if b < 2 else 3)
                strip[p, b, level, :] = s
                strips[b].append(s)
        for b in range(3):
            first[b, level, :], second[b, level, :] = pack_strips(strips[b], even)

    level_tiles(LEV // STRIP_SPAN // grid, body, STRIP_SPAN)


def pack(state, winds, diff, grid=2):
    shapes = [(4, 11, LEV, 128), (4, 3, LEV, 128), (3, LEV, 128), (3, LEV, 128)]
    return pl.pallas_call(
        partial(pack_kernel, grid=grid),
        grid=(grid,),
        in_specs=[tiled(grid, 8, 256, 128), tiled(grid, 2, 256, 128), whole((4, 128))],
        out_specs=[tiled(grid, *s) for s in shapes],
        out_shape=[struct(*s) for s in shapes],
        compiler_params=params(16),
        name="pack",
    )(*in_hbm(state, winds, diff))


def complete_kernel(strip, first, second, *outs):
    even = lon_even()
    blocks = strip.shape[1]
    split = blocks // len(outs)

    def body(t, level):
        lane = lax.broadcasted_iota(I32, (SPAN, 128), 1) % 32
        for b in range(blocks):
            one, two = first[b, level, :], second[b, level, :]
            east = jnp.where(even, one, two)
            west = jnp.where(even, two, one)
            for r in range(4):
                full = jnp.where(lane < 8, roll(west, -8 * r), strip[r, b, level, :])
                outs[b // split][r, b % split, level, :] = jnp.where(lane >= 24, roll(east, 24 - 8 * r), full)

    level_tiles(LEV // SPAN, body, SPAN)


def complete(strip, first, second, parts):
    split = strip.shape[1] // parts
    return pl.pallas_call(
        complete_kernel,
        in_specs=[VMEM_SPEC] * 3,
        out_specs=[VMEM_SPEC] * parts,
        out_shape=[struct(4, split, LEV, 128)] * parts,
        compiler_params=params(4),
        name="complete",
    )(strip, first, second)


def open_to_next_chip():
    lat = lax.axis_index("lat")
    return jnp.where((lat > 0) & (lat < lax.axis_size("lat") - 1), 1.0, 0.0).astype(F32)


def each_row(first, last, body):
    def step(i, carry):
        body(i)
        return carry

    lax.fori_loop(first, last, step, 0)


def coefficient_kernel(own, r0, r1, sown, s0, s1, out, raw, beside, beyond):
    flipped = lat_even()
    open_side = open_to_next_chip()
    lane = lax.broadcasted_iota(I32, (LEV, 128), 1)
    beside[...] = s0[:, 0:2]
    beyond[...] = s1[:, 0:2]

    def fill(i, main, strip):
        packed = strip[2]
        spread = []
        for g in range(3):
            one = jnp.where(lane < 32, roll(packed, -32 * g), 0.0)
            one = one + roll(one, 32)
            spread.append(one + roll(one, 64))
        plain = [main[VARS], main[VARS + 1], main[VARS + 2]]
        for n, (w0, w1, dd) in enumerate((plain, spread)):
            half = w0 * 0.5
            half_west, dd_west = roll(half, 1), roll(dd, 1)
            if n == 0:
                half_west = jnp.where(lane == 0, roll(spread[0], 121) * 0.5, half_west)
                dd_west = jnp.where(lane == 0, roll(spread[2], 121), dd_west)
            lat_half = w1 * 0.5
            values = half + dd, half - dd, half_west + dd_west, half_west - dd_west, lat_half + dd, lat_half - dd
            for m, value in enumerate(values):
                raw[i, 6 * n + m] = value

    for first, target, main, strip in ((0, 3, r0, s0), (4, 4, own, sown), (8, 11, r1, s1)):
        way = 1 if first == 4 else -1

        def two(j):
            for q in (2 * j, 2 * j + 1):
                row = 3 - q if first == 8 else q
                fill(first + q if first == 8 else target + way * q, main.at[row], strip.at[row])

        each_row(0, 2, two)

    def combine(i):
        scale = jnp.where(i >= 8, open_side, 1.0)
        for n in range(2):
            a, b, a_west, b_west = (raw[i, 6 * n + m] for m in range(4))
            u, w = interface(raw, flipped, i, n)
            u_before, w_before = interface(raw, flipped, i - 1, n)
            values = 1.0 - a + b_west - u + w_before, -b, a_west, -w, u_before
            for m, value in enumerate(values):
                out[i, 5 * n + m] = value * scale

    each_row(1, 11, combine)


def interface(raw, flipped, i, n):
    u = jnp.where(flipped, -raw[i + 1, 6 * n + 5], raw[i, 6 * n + 4])
    w = jnp.where(flipped, -raw[i + 1, 6 * n + 4], raw[i, 6 * n + 5])
    return u, w


def coefficients(tile, strips):
    return pl.pallas_call(
        coefficient_kernel,
        in_specs=[VMEM_SPEC] * 6,
        out_specs=[VMEM_SPEC] * 4,
        out_shape=[struct(12, 10, LEV, 128), struct(12, 12, LEV, 128)] + [struct(4, 2, LEV, 128)] * 2,
        compiler_params=params(4),
        name="coefficients",
    )(*tile, *strips)


def adjoint_kernel(forward, raw, out):
    flipped = lat_even()
    open_side = open_to_next_chip()

    def combine(i):
        scale = jnp.where(i >= 8, open_side, 1.0)
        for n in range(2):
            out[i, 5 * n] = forward[i, 5 * n]
            out[i, 5 * n + 1] = raw[i, 6 * n] * scale
            out[i, 5 * n + 2] = -raw[i, 6 * n + 3] * scale
            out[i, 5 * n + 3] = interface(raw, flipped, i, n)[0] * scale
            out[i, 5 * n + 4] = -interface(raw, flipped, i - 1, n)[1] * scale

    each_row(1, 11, combine)


def adjoint_coefficients(forward, raw):
    return pl.pallas_call(
        adjoint_kernel,
        in_specs=[VMEM_SPEC] * 2,
        out_specs=VMEM_SPEC,
        out_shape=struct(12, 10, LEV, 128),
        compiler_params=params(4),
        name="adjoint_coefficients",
    )(forward, raw)


def advect_kernel(*refs, steps, slot, apart, result, addend):
    refs = list(refs)
    group = 2 if steps is None else 1
    steps = refs.pop(0)[slot] if steps is None else steps
    own, r0, r1 = refs[:3]
    refs = refs[3:]
    strips = ()
    if apart:
        strips, refs = refs[:3], refs[3:]
    coef = refs.pop(0)
    if addend:
        add_main, add_strip = refs[:2]
        refs = refs[2:]
    out, *work, shift = refs
    source = lax.broadcasted_iota(I32, (256, 256), 0) % 128
    target = lax.broadcasted_iota(I32, (256, 256), 1)
    chosen = jnp.where(target < 128, target + 1, target + 127) % 128
    shift[...] = (source == chosen).astype(F32).astype(BF16)
    flip = jnp.where(lat_even(), 3, 0)
    width = r0.shape[0]

    def place(target, sources, offset, count):
        tile, intra, inter = sources

        def halo(j, carry):
            target[3 - j, offset : offset + count] = intra[j, 0:count]
            target[8 + j, offset : offset + count] = inter[width - 1 - j, 0:count]
            return carry

        def inside(j, carry):
            target[4 + j, offset : offset + count] = tile[j, 0:count]
            return carry

        lax.fori_loop(0, width, halo, 0)
        lax.fori_loop(0, 4, inside, 0)

    def start(target):
        if apart:
            place(target, (own, r0, r1), 0, VARS)
            place(target, strips, VARS, 2)
        else:
            place(target, (own, r0, r1), 0, VARS + 2)

    def when(condition, run):
        if isinstance(condition, bool):
            if condition:
                run()
        else:
            pl.when(condition)(run)

    for n in range(2):
        when(steps % 2 != n, partial(start, work[n]))
    lane = lax.broadcasted_iota(I32, (LEV, 128), 1)

    def row(now, i, last, store):
        def stencil(n, v, f, east, west):
            value = coef[i, n] * f
            value = value + coef[i, n + 1] * east
            value = value + coef[i, n + 2] * west
            value = value + coef[i, n + 3] * now[i + 1, v]
            return value + coef[i, n + 4] * now[i - 1, v]

        wanted = VARS + (0 if last and result != "both" else 2)
        halves = split(now[i, 0:wanted].reshape(wanted * LEV, 128))
        moved = dot(jnp.concatenate(halves, axis=1), shift[...], (1, 0))
        moved = moved.reshape(wanted, LEV, 256)
        for b in range(2):
            f = now[i, VARS + b]
            ends = jnp.where(lane % 32 == 25, roll(f, 18), f)
            for v in (VARS + b, *range(4 * b, 4 * b + 4)):
                if v >= wanted:
                    continue
                f = now[i, v]
                east, west = moved[v, :, :128], moved[v, :, 128:]
                if v < VARS:
                    rim = roll(ends, 103 - 32 * (v % 4))
                    east = jnp.where(lane == 127, rim, east)
                    west = jnp.where(lane == 0, rim, west)
                store(v, stencil(5 if v >= VARS else 0, v, f, east, west))

    def step(reach):
        def two(j, carry):
            for i in (4 - reach + 2 * j, 5 - reach + 2 * j):

                def store(v, value):
                    work[1 - reach % 2][i, v] = value

                row(work[reach % 2], i, False, store)
            return carry

        lax.fori_loop(0, 2 + reach, two, 0)

    for reach in (3, 2, 1):
        when(steps > reach, partial(step, reach))

    def final(j, carry):
        for q in range(group):
            r = group * j + q

            def store(v, value):
                if addend:
                    value = value + (add_main[r, v] if v < VARS else add_strip[r, v - VARS])
                if result == "native":
                    out[v, pl.ds(jnp.abs(flip - r), LEV, stride=4), :] = value
                else:
                    out[r, v] = value

            row(work[0], 4 + r, True, store)
        return carry

    lax.fori_loop(0, 4 // group, final, 0)


def advect(steps, tile, strips, coef, result, addend=None, slot=0):
    args = [*tile]
    if strips is not None:
        args += strips
    args.append(coef)
    if addend is not None:
        args += addend
    if result == "native":
        shape = (8, 256, 128)
    else:
        shape = (4, 10 if result == "both" else 8, LEV, 128)
    static = isinstance(steps, int)
    return pl.pallas_call(
        partial(
            advect_kernel,
            steps=steps if static else None,
            slot=slot,
            apart=strips is not None,
            result=result,
            addend=addend is not None,
        ),
        in_specs=([] if static else [SMEM_SPEC]) + [VMEM_SPEC] * len(args),
        out_specs=VMEM_SPEC,
        out_shape=struct(*shape),
        scratch_shapes=[pltpu.VMEM((12, 10, LEV, 128), F32)] * 2 + [pltpu.VMEM((256, 256), BF16)],
        compiler_params=params(14),
        name="advect_" + result,
    )(*([] if static else [steps]), *args)


def split(x):
    high = x.astype(BF16)
    return high, (x - high.astype(F32)).astype(BF16)


def dot(x, y, dims):
    return lax.dot_general(x, y, ((dims[:1], dims[1:]), ((), ())), preferred_element_type=F32)


def dot3(x, y, dims):
    return dot(x[0], y[0], dims) + (dot(x[0], y[1], dims) + dot(x[1], y[0], dims))


def relayout_kernel(observed, sent):
    homes = observed.shape[3]
    for k in range(2):
        for q in range(3):
            for c in range(4):
                sent[pl.ds(12 * k + 4 * q + c, homes, stride=24), :] = observed[k, 0, q, :, pl.ds(128 * c, 128)]


def relayout(observed):
    turned = jnp.transpose(observed, (0, 1, 3, 2, 4))
    homes = turned.shape[3]
    sent = pl.pallas_call(
        relayout_kernel,
        grid=(1,),
        in_specs=[whole(turned.shape)],
        out_specs=whole((homes * 24, 128)),
        out_shape=struct(homes * 24, 128),
        compiler_params=params(16),
        name="relayout",
    )(*in_hbm(turned))
    return sent.reshape(homes, 24, 128)


PADDED = 640


def column_of(row):
    square = (SND, SND)
    here = lax.broadcasted_iota(I32, square, 0) == lax.broadcasted_iota(I32, square, 1)
    return jnp.sum(jnp.where(here, jnp.broadcast_to(row, square), 0), axis=1, keepdims=True)


def load_table(table, high, low):
    count = table.shape[0]
    full = count // 16 * 16
    high[pl.ds(0, full), :], low[pl.ds(0, full), :] = split(table[pl.ds(0, full), :])
    rest = jnp.zeros((PADDED - full, table.shape[1]), F32)
    if count > full:
        zeros = jnp.zeros((PADDED - count, table.shape[1]), F32)
        rest = jnp.concatenate([table[pl.ds(full, count - full), :], zeros], axis=0)
    high[pl.ds(full, PADDED - full), :], low[pl.ds(full, PADDED - full), :] = split(rest)


def observe_kernel(cells, owners, channels, weight, field, *refs, slot):
    flip = jnp.where(lat_even(), 3, 0)
    square = (SND, SND)
    row_id = lax.broadcasted_iota(I32, square, 0)
    lane_id = lax.broadcasted_iota(I32, square, 1)
    copies = []
    if slot == 0:
        hbm, refs = refs[:3], refs[3:]
        (out, strip, first, second, *tables, late_totals, late_times), refs = refs[:10], refs[10:]
        (absorb_table, emit_table, fetched), sems = refs[:3], refs[3]
        for n, target in enumerate((absorb_table, emit_table, fetched)):
            copies.append(pltpu.make_async_copy(hbm[n], target, sems.at[n]))
            copies[n].start()
        entry = lax.broadcasted_iota(I32, (PADDED, channels.shape[1]), 0)
        listed = (entry == channels[...]).astype(F32).astype(BF16)
        times = dot(jnp.ones((8, channels.shape[1]), BF16), listed, (1, 1))
        late_times[...] = times
        times = times[0:1]
    else:
        tables, early_totals, early_times = refs[:4], refs[4], refs[5]
        before, (out, strip, first, second) = refs[6:9], refs[9:13]
        times = early_times[0:1, :]

    def observed_totals(which):
        owner_row = owners[which : which + 1, :]
        owner = column_of(owner_row)
        earlier = (owner == owner_row) & (lane_id < row_id)
        rank = jnp.sum(jnp.where(earlier, 1, 0), axis=1, keepdims=True)
        choices = [((owner == lane_id) & (rank == q)).astype(F32).astype(BF16) for q in range(3)]
        parts = []
        for c in range(4):
            part = [jnp.zeros(square, F32)] * 2
            for q in range(3):
                seen = split(fetched[pl.ds(12 * which + 4 * q + c, SND, stride=24), :])
                part = [p + dot(choices[q], x, (1, 0)) for p, x in zip(part, seen, strict=True)]
            parts.append(part)
        wanted = [jnp.concatenate([part[n] for part in parts], axis=1).astype(BF16) for n in range(2)]
        return dot(wanted[0], listed, (1, 1)) + dot(wanted[1], listed, (1, 1))

    cell = column_of(cells[slot : slot + 1, :])
    picks = [(cell == lane_id + 128 * jnp.abs(flip - r)).astype(F32).astype(BF16) for r in range(4)]
    pieces = [jnp.zeros((SND, VARS * LEV), F32)] * 2
    for r in range(4):
        x = split(field[r, 0:VARS].reshape(VARS * LEV, 128))
        pieces = [piece + dot(picks[r], part, (1, 1)) for piece, part in zip(pieces, x, strict=True)]
    column = [piece.astype(BF16) for piece in pieces]
    if slot == 0:
        for n, table in enumerate((absorb_table, emit_table)):
            copies[n].wait()
            load_table(table, tables[2 * n], tables[2 * n + 1])
    absorb = (tables[0][...], tables[1][...])
    emission = (tables[2][...], tables[3][...])
    optical = dot3(column, absorb, (1, 1))
    bright = dot3(column, emission, (1, 1))
    decay = jnp.exp(-jnp.abs(optical))
    inverse = 1.0 / (1.0 + decay)
    rest = decay * inverse
    positive = optical >= 0
    passing = jnp.where(positive, rest, inverse)
    opaque = jnp.where(positive, inverse, rest)
    if slot == 0:
        copies[2].wait()
        totals = observed_totals(0)
        late_totals[...] = observed_totals(1)
    else:
        totals = early_totals[...]
    evolved = passing * bright
    departure = weight[...] * (times * evolved - totals)
    to_bright = departure * passing
    to_optical = -(departure * evolved * opaque)
    column = dot3(split(to_optical), absorb, (1, 0)) + dot3(split(to_bright), emission, (1, 0))
    ch, cl = split(column)
    for r in range(4):
        placed = dot(ch, picks[r], (0, 0)) + dot(cl, picks[r], (0, 0))
        out[r] = placed.reshape(VARS, LEV, 128)

    even = lon_even()
    if slot == 1:
        strip[:, 2:4] = before[0][...]
        first[2:4] = before[1][...]
        second[2:4] = before[2][...]

    def strips_of(t, level):
        for b in range(2):
            strips = []
            for r in range(4):
                s = own_strip(lambda g: out[r, 4 * b + g, level, :], 4)
                strip[r, b, level, :] = s
                strips.append(s)
            first[b, level, :], second[b, level, :] = pack_strips(strips, even)

    level_tiles(LEV // STRIP_SPAN, strips_of, STRIP_SPAN)


def observe(slot, small, field, inputs, before):
    count = 2 if slot == 0 else 4
    shapes = [struct(4, 8, LEV, 128), struct(4, count, LEV, 128)] + [struct(count, LEV, 128)] * 2
    scratch = []
    specs = [VMEM_SPEC] * len(inputs)
    if slot == 0:
        shapes += [struct(PADDED, VARS * LEV, dtype=BF16)] * 4 + [struct(SND, PADDED), struct(8, PADDED)]
        scratch = [pltpu.VMEM(x.shape, F32) for x in inputs] + [pltpu.SemaphoreType.DMA((len(inputs),))]
        specs = [pl.BlockSpec(memory_space=pltpu.HBM)] * len(inputs)
        inputs = in_hbm(*inputs)
    return pl.pallas_call(
        partial(observe_kernel, slot=slot),
        in_specs=[VMEM_SPEC] * (len(small) + 1) + specs + [VMEM_SPEC] * len(before),
        out_specs=[VMEM_SPEC] * len(shapes),
        out_shape=shapes,
        scratch_shapes=scratch,
        compiler_params=params(10),
        name="observe",
    )(*small, field, *inputs, *before)


def swap(x, axis, parity, wrap):
    devices = lax.axis_size(axis)
    pairs = []
    for i in range(parity, devices, 2):
        if i + 1 < devices or wrap:
            j = (i + 1) % devices
            pairs += [(i, j), (j, i)]
    return lax.ppermute(x, axis, pairs)


def lat_swap(x, width=4):
    beyond = swap(x[4 - width :], "lat", 1, False)
    return swap(x[:width], "lat", 0, False), beyond


def lon_swap(first, second):
    beyond = swap(second, "lon", 1, True)
    return swap(first, "lon", 0, True), beyond


def per_device(
    state, winds, diffusivity, sounding_cell, sounding_owner, step_counts, channel_list, absorb_table, emit_table,
    obs_weight, observed,
):
    def by_steps(slot, run):
        branches = [partial(run, width) for width in range(1, MAXSTEP + 1)]
        return lax.switch(step_counts[slot] - 1, branches)

    main, strip, first, second = pack(state.reshape(8, 256, 128), winds.reshape(2, 256, 128), diffusivity)
    received = lon_swap(first, second)
    halo = lat_swap(main)
    sent, received = lax.optimization_barrier((relayout(observed), received))
    (strip,) = complete(strip, *received, 1)
    fetched = lax.all_to_all(sent, ("lon", "lat"), split_axis=0, concat_axis=0, tiled=True)
    tile, strips = (main, *halo), (strip, *lat_swap(strip))
    onward, raw, *halo_strips = coefficients(tile, strips)
    strips = strips[0], *halo_strips
    both0 = advect(step_counts, tile, strips, onward, "both")
    halo = lat_swap(both0)
    late = raw, both0, obs_weight, sounding_owner
    raw, both0, obs_weight, sounding_owner = lax.optimization_barrier(late)
    backward_coef = adjoint_coefficients(onward, raw)

    extra = PADDED - obs_weight.shape[0]
    padded_weight = jnp.pad(obs_weight, (0, extra))[None, :]
    small = [sounding_cell, sounding_owner[:, :, 0], channel_list[None, :], padded_weight]
    tables = [absorb_table.T, emit_table.T, fetched.reshape(-1, 128)]
    g0, *rest = observe(0, small, both0, tables, [])
    both0, backward_coef, g0 = lax.optimization_barrier((both0, backward_coef, g0))
    field1 = advect(step_counts, (both0, *halo), None, onward, "main", slot=1)
    g1, strip, first, second = observe(1, small, field1, rest[3:], rest[:3])

    def backward(width):
        received = lon_swap(first, second)
        halo = lat_swap(g1, width)
        strips1, strips0 = complete(strip, *received, 2)
        halo_strips = lat_swap(strips1, width)
        return advect(width, (g1, *halo), (strips1, *halo_strips), backward_coef, "both", (g0, strips0))

    both = by_steps(1, backward)

    def last(width):
        return advect(width, (both, *lat_swap(both, width)), None, backward_coef, "native")

    result = by_steps(0, last)
    return result.reshape(state.shape)


def solution(mesh):
    return jax.shard_map(
        per_device,
        mesh=mesh,
        in_specs=(
            P(None, None, "lat", "lon"),
            P(None, None, "lat", "lon"),
            P("lat", "lon"),
            P(None, ("lon", "lat")),
            P(None, ("lon", "lat"), None),
            P(),
            P(),
            P(),
            P(),
            P(),
            P(None, ("lon", "lat"), None, None, None),
        ),
        out_specs=P(None, None, "lat", "lon"),
        check_vma=False,
    )
```
